128 devices in a mesh: stn: 16 (over x_lo, z, core), seg: 8 (over y, x_hi).
Axes of the slice: x: 4 (x_hi: 2, x_lo: 2; x = x_hi * 2 + x_lo), y: 4, z: 4, core: 2. Of those that a mesh axis runs over, the one named last changes fastest.
Arguments:
- traces: float32 [1024, 38400], P(('stn', 'seg')), may hold values from -6 to 6
- fir_taps: float32 [31], replicated, may hold values from -0.9 to 0.9
- seg_flags: int32 [1024, 64], P(('stn', 'seg')), may hold values 0 or 1
- pair_mask: int32 [1024, 1024], P('stn', 'seg'), may hold values 0 or 1
Outputs:
- stacked: float32 [41, 1024, 1024], P(None, 'stn', 'seg')
The draws below stay inside these ranges and needn't reach their ends.
All inputs are finite; a program needn't handle non-finite values. No bound on the sum of `seg_flags` or of `pair_mask` on one device may be relied on, other than what follows from the above.
Results may differ from the reference program's by a relative error of at most 0.0095.
Values may be sent and summed in bfloat16 or wider, within the bound.
A program may use at most 192 MiB of HBM per device.

```python
import math
import jax
import jax.numpy as jnp
from jax import lax

STATIONS = 1024
SAMP = 600
LAGS = 41
TAPS = 31
RADIUS = 64
SEG_DEV = 8
SEGMENTS = 64
N_SEG = 8


def place_ends(array, key, smallest, largest):
    longest = array.shape.index(max(array.shape))
    spots = []
    for shift in (0, 1):
        where = [jax.random.randint(jax.random.fold_in(key, axis), (), 0, length) for axis, length in enumerate(array.shape)]
        where[longest] = (where[longest] + shift) % array.shape[longest]
        spots.append(tuple(where))
    return array.at[spots[0]].set(smallest).at[spots[1]].set(largest)


def shard_levels(own_key, extent, split, low, largest):
    def one(axis_at, blocks):
        heights = jax.random.uniform(jax.random.fold_in(jax.random.fold_in(own_key, 6), axis_at), (blocks,), jnp.float32, low / len(split), largest / len(split))
        return jnp.repeat(jnp.exp(heights), extent[axis_at] // blocks).reshape((-1,) + (1,) * (len(extent) - axis_at - 1))

    factor_of = one(*split[0])
    for cut in split[1:]:
        factor_of = factor_of * one(*cut)
    return factor_of


def noise(stream_key, extent, deviation, bound, cuts=(), held_as=jnp.bfloat16):
    values = deviation * jax.random.normal(stream_key, extent, jnp.float32)
    if cuts:
        values = values * shard_levels(stream_key, extent, cuts, -0.22, 0.18)
    return jnp.clip(values, -bound, bound).astype(held_as)


def setup_inputs(seed: int = 0) -> dict:
    streams_of = jax.random.split(jax.random.key(seed), 5)
    return {
        "traces": noise(streams_of[0], (STATIONS, SEGMENTS * SAMP), 1.0, 6.0, ((0, 128),), jnp.float32),
        "fir_taps": noise(streams_of[1], (TAPS,), 0.3, 0.9, (), jnp.float32),
        "seg_flags": place_ends((jax.random.randint(streams_of[2], (STATIONS, SEGMENTS), 0, 8) < 7).astype(jnp.int32), jax.random.fold_in(streams_of[2], 1), 0, 1),
        "pair_mask": place_ends((jax.random.randint(streams_of[3], (STATIONS, STATIONS), 0, 4) < 3).astype(jnp.int32), jax.random.fold_in(streams_of[3], 1), 0, 1),
    }


epsilon = 1e-06
lag_group = 8

def preprocess(traces, fir_taps, seg_flags):
    station_count = traces.shape[0]
    record_len = traces.shape[1]
    half_taps = (TAPS - 1) // 2
    padded = jnp.pad(traces, ((0, 0), (half_taps, half_taps)))
    filtered = jnp.zeros_like(traces)
    for tap_index in range(TAPS):
        filtered = filtered + fir_taps[tap_index] * padded[:, tap_index:tap_index + record_len]
    width = 2 * RADIUS + 1
    magnitude = jnp.pad(jnp.abs(filtered), ((0, 0), (RADIUS + 1, RADIUS)))
    running = jnp.cumsum(magnitude, axis=1)
    running_level = (running[:, width:] - running[:, :record_len]) / width
    whitened = filtered / (running_level + epsilon)
    flagged = whitened.reshape(station_count, -1, SAMP) * seg_flags[:, :, None].astype(jnp.float32)
    return flagged.astype(jnp.bfloat16)

def correlate(left_rows, right_rows):
    half_lag = (LAGS - 1) // 2
    row_count = left_rows.shape[0]
    right_flat = right_rows.reshape(right_rows.shape[0], -1)
    left_padded = jnp.pad(left_rows, ((0, 0), (0, 0), (half_lag, half_lag)))
    results = []
    for first_lag in range(0, LAGS, lag_group):
        lag_list = list(range(first_lag, min(first_lag + lag_group, LAGS)))
        shifted = jnp.stack([left_padded[:, :, LAGS - 1 - lag_index:LAGS - 1 - lag_index + SAMP] for lag_index in lag_list], axis=0)
        shifted = shifted.reshape(len(lag_list) * row_count, -1)
        product = lax.dot_general(shifted, right_flat, (((1,), (1,)), ((), ())), preferred_element_type=jnp.float32)
        results.append(product.reshape(len(lag_list), row_count, right_flat.shape[0]))
    return jnp.concatenate(results, axis=0)

def reference(traces, fir_taps, seg_flags, pair_mask):
    whitened = preprocess(traces, fir_taps, seg_flags)
    norm_scale = 1.0 / math.sqrt(SAMP * SEGMENTS)
    stacked = jnp.zeros((LAGS, STATIONS, STATIONS), jnp.float32)
    for group_index in range(N_SEG):
        group_rows = whitened[:, group_index * SEG_DEV:(group_index + 1) * SEG_DEV]
        group_part = (correlate(group_rows, group_rows) * norm_scale).astype(jnp.bfloat16)
        stacked = stacked + lax.optimization_barrier(group_part).astype(jnp.float32)
    return stacked * pair_mask.astype(jnp.float32)[None]
```

```python
import functools
import math

import jax
import jax.numpy as jnp
import numpy as np
from jax import lax
from jax.experimental import pallas as pl
from jax.experimental.pallas import tpu as pltpu
from jax.sharding import PartitionSpec as P

SAMP = 600
LAGS = 41
TAPS = 31
RADIUS = 64
SEGS = 64
ROWS = 8
EPS = 1e-06

LENGTH = 640
FREQS = LENGTH // 2
HALF = SEGS
FBLOCK = 64
FBLOCKS = FREQS // FBLOCK
LAGPAD = 48

RECORD = SEGS * SAMP
CHUNK = 1280
CHUNKS = RECORD // CHUNK
WINDOW = CHUNK + 256


def split_bf16(values):
    high = np.asarray(values, np.float32).astype(jnp.bfloat16)
    low = (np.asarray(values, np.float64) - high.astype(np.float64)).astype(np.float32).astype(jnp.bfloat16)
    return high, low


def forward_matrix():
    freq = (np.arange(FREQS) + 0.5) * (2 * np.pi / LENGTH)
    angle = freq[:, None] * np.arange(LENGTH)[None, :]
    keep = (np.arange(LENGTH) < SAMP)[None, :]
    parts = []
    for part in (np.cos(angle) * keep, -np.sin(angle) * keep):
        parts.append(split_bf16(part))
    (re_hi, re_lo), (im_hi, im_lo) = parts
    stacked = np.stack([re_hi, im_hi, re_lo, im_lo])
    stacked = stacked.reshape(4, FBLOCKS, FBLOCK, LENGTH).transpose(1, 0, 2, 3)
    return np.ascontiguousarray(stacked.reshape(FBLOCKS, 4 * FBLOCK, LENGTH))


def inverse_matrix():
    freq = (np.arange(FREQS) + 0.5) * (2 * np.pi / LENGTH)
    lag = np.arange(LAGS) - (LAGS - 1) // 2
    scale = 2.0 / LENGTH / math.sqrt(RECORD)
    angle = lag[:, None] * freq[None, :]
    both = np.stack([np.cos(angle), -np.sin(angle)], axis=-1).reshape(LAGS, 2 * FREQS) * scale
    padded = np.zeros((LAGPAD, 2 * FREQS))
    padded[:LAGS] = both
    return np.concatenate(split_bf16(padded), axis=0)


def spectrum_kernel(taps_ref, flags_ref, traces_ref, forward_ref, out_ref, padded, filtered, whitened, rows, block):
    edge = jnp.zeros((ROWS, 128), jnp.float32)
    padded[:, 0:128] = edge
    padded[:, 128 + RECORD : 256 + RECORD] = edge
    filtered[:, 0:128] = edge
    filtered[:, 128 + RECORD : 256 + RECORD] = edge
    whitened[:, RECORD : RECORD + 128] = edge
    padded[:, 128 : 128 + RECORD] = traces_ref[...]

    @pl.loop(0, CHUNKS)
    def _(chunk):
        start = pl.multiple_of(chunk * CHUNK, 128)
        window = padded[:, pl.ds(start, WINDOW)]
        total = jnp.zeros((ROWS, CHUNK), jnp.float32)
        for tap in range(TAPS):
            first = 128 - (TAPS - 1) // 2 + tap
            total = total + taps_ref[tap] * window[:, first : first + CHUNK]
        filtered[:, pl.ds(pl.multiple_of(start + 128, 128), CHUNK)] = total

    @pl.loop(0, CHUNKS)
    def _(chunk):
        start = pl.multiple_of(chunk * CHUNK, 128)
        window = filtered[:, pl.ds(start, WINDOW)]
        magnitude = jnp.abs(window)
        run = magnitude
        for step in (1, 2, 4, 8, 16, 32, 64):
            run = run + pltpu.roll(run, WINDOW - step, 1)
        level = run[:, 64 : 64 + CHUNK] + magnitude[:, 192 : 192 + CHUNK]
        level = level / (2 * RADIUS + 1)
        whitened[:, pl.ds(start, CHUNK)] = window[:, 128 : 128 + CHUNK] / (level + EPS)

    flags = flags_ref[...].astype(jnp.float32)
    for seg in range(SEGS):
        piece = whitened[:, seg * SAMP : seg * SAMP + LENGTH]
        piece = piece * flags[:, seg : seg + 1]
        for part in range(LENGTH // 128):
            rows[part, pl.ds(seg, ROWS, stride=SEGS), :] = piece[:, part * 128 : part * 128 + 128]
    samples = jnp.concatenate([rows[part] for part in range(LENGTH // 128)], axis=1).astype(jnp.bfloat16)

    lane = lax.broadcasted_iota(jnp.int32, (FBLOCK, 128), 1)
    low_half = lane < HALF

    @pl.loop(0, FBLOCKS)
    def _(step):
        spectrum = lax.dot_general(
            forward_ref[step],
            samples,
            (((1,), (1,)), ((), ())),
            preferred_element_type=jnp.float32,
        )
        both = spectrum[: 2 * FBLOCK] + spectrum[2 * FBLOCK :]
        for pair in range(ROWS // 2):
            real = both[:FBLOCK, pair * 128 : pair * 128 + 128]
            imag = both[FBLOCK:, pair * 128 : pair * 128 + 128]
            even = jnp.where(low_half, real, pltpu.roll(imag, HALF, 1))
            odd = jnp.where(low_half, pltpu.roll(real, HALF, 1), imag)
            block[pl.ds(2 * pair, FBLOCK, stride=ROWS), :] = even
            block[pl.ds(2 * pair + 1, FBLOCK, stride=ROWS), :] = odd
        out_ref[pl.ds(step * FBLOCK, FBLOCK)] = block[...].reshape(FBLOCK, ROWS, 128).astype(jnp.bfloat16)


def spectrum(traces, fir_taps, seg_flags):
    vmem = pl.BlockSpec(memory_space=pltpu.VMEM)
    return pl.pallas_call(
        spectrum_kernel,
        out_shape=jax.ShapeDtypeStruct((FREQS, ROWS, 128), jnp.bfloat16),
        in_specs=[pl.BlockSpec(memory_space=pltpu.SMEM), vmem, vmem, vmem],
        out_specs=vmem,
        scratch_shapes=[
            pltpu.VMEM((ROWS, RECORD + 256), jnp.float32),
            pltpu.VMEM((ROWS, RECORD + 256), jnp.float32),
            pltpu.VMEM((ROWS, RECORD + 128), jnp.float32),
            pltpu.VMEM((LENGTH // 128, ROWS * SEGS, 128), jnp.float32),
            pltpu.VMEM((FBLOCK * ROWS, 128), jnp.float32),
        ],
        compiler_params=pltpu.CompilerParams(vmem_limit_bytes=32 << 20),
    )(fir_taps, seg_flags, traces, jnp.asarray(forward_matrix()))


def correlate_kernel(left_ref, right_ref, inverse_ref, mask_ref, out_ref, cross, *, freqs, left_rows, right_rows):
    step = pl.program_id(0)
    lane = lax.broadcasted_iota(jnp.int32, (left_rows, 128), 1)
    sign = jnp.where(lane < HALF, -1.0, 1.0)

    @pl.loop(0, freqs)
    def _(index):
        left = left_ref[:, index].astype(jnp.float32).reshape(left_rows, 128)
        right = right_ref[:, index].reshape(right_rows, 128)
        turned = pltpu.roll(left, HALF, 1) * sign
        both = jnp.concatenate([left, turned], axis=0).astype(jnp.bfloat16)
        product = lax.dot_general(both, right, (((1,), (1,)), ((), ())), preferred_element_type=jnp.float32)
        at = pl.multiple_of((step * freqs + index) * (2 * left_rows), 8)
        cross[pl.ds(at, 2 * left_rows), :] = product

    @pl.when(step == pl.num_programs(0) - 1)
    def _():
        @pl.loop(0, left_rows)
        def _(row):
            values = cross[pl.ds(row, 2 * FREQS, stride=left_rows), :].astype(jnp.bfloat16)
            lagged = jnp.dot(inverse_ref[...], values, preferred_element_type=jnp.float32)
            lagged = lagged[:LAGS] + lagged[LAGPAD : LAGPAD + LAGS]
            keep = mask_ref[pl.ds(row, 1), :].astype(jnp.float32)
            out_ref[pl.ds(row, LAGS, stride=left_rows), :] = lagged * keep


def correlate(left, right, pair_mask):
    left_rows, right_rows = left.shape[0] * ROWS, right.shape[0] * ROWS
    freqs = 32
    out = pl.pallas_call(
        functools.partial(correlate_kernel, freqs=freqs, left_rows=left_rows, right_rows=right_rows),
        grid=(FREQS // freqs,),
        out_shape=jax.ShapeDtypeStruct((LAGS * left_rows, right_rows), jnp.float32),
        in_specs=[
            pl.BlockSpec((left.shape[0], freqs, ROWS, 128), lambda i: (0, i, 0, 0)),
            pl.BlockSpec((right.shape[0], freqs, ROWS, 128), lambda i: (0, i, 0, 0)),
            pl.BlockSpec((2 * LAGPAD, 2 * FREQS), lambda i: (0, 0)),
            pl.BlockSpec(pair_mask.shape, lambda i: (0, 0)),
        ],
        out_specs=pl.BlockSpec((LAGS * left_rows, right_rows), lambda i: (0, 0)),
        scratch_shapes=[pltpu.VMEM((2 * FREQS * left_rows, right_rows), jnp.float32)],
        compiler_params=pltpu.CompilerParams(vmem_limit_bytes=56 << 20),
    )(left, right, jnp.asarray(inverse_matrix()), pair_mask)
    return out.reshape(LAGS, left_rows, right_rows)


def body(traces, fir_taps, seg_flags, pair_mask):
    own = spectrum(traces, fir_taps, seg_flags)
    left = lax.all_gather(own, "seg", axis=0)
    stn, seg = lax.axis_size("stn"), lax.axis_size("seg")
    moves = [(i * seg + j, ((i % 2) * seg + j) * seg + i // 2) for i in range(stn) for j in range(seg)]
    moved = lax.ppermute(own, ("stn", "seg"), moves)
    right = lax.all_gather(moved, "stn", axis=0)
    return correlate(left, right, pair_mask)


def solution(mesh):
    return jax.shard_map(
        body,
        mesh=mesh,
        in_specs=(P(("stn", "seg"), None), P(), P(("stn", "seg"), None), P("stn", "seg")),
        out_specs=P(None, "stn", "seg"),
        check_vma=False,
    )
```

```python
import functools
import math

import jax
import jax.numpy as jnp
import numpy as np
from jax import lax
from jax.experimental import pallas as pl
from jax.experimental.pallas import tpu as pltpu
from jax.sharding import PartitionSpec as P

SAMP = 600
LAGS = 41
TAPS = 31
RADIUS = 64
SEGS = 64
ROWS = 8
EPS = 1e-06

LENGTH = 624
PADDED = 640
FREQS = LENGTH // 2
HALF = SEGS
FBLOCK = 104
FBLOCKS = FREQS // FBLOCK
LAGPAD = 48
PITCH = 136

RECORD = SEGS * SAMP
BLOCKS = RECORD // 128
PER = 30

STN, SEG = 16, 8
LEFT = ROWS * SEG
RIGHT = ROWS * STN
GROUPS = STN // 2
PARTS = 2

MESH = pl.DeviceIdType.MESH
VMEM = pl.BlockSpec(memory_space=pltpu.VMEM)
ANY = pl.BlockSpec(memory_space=pl.ANY)


def split_bf16(values):
    high = np.asarray(values, np.float32).astype(jnp.bfloat16)
    low = (np.asarray(values, np.float64) - high.astype(np.float64)).astype(np.float32).astype(jnp.bfloat16)
    return high, low


def frequencies():
    return (np.arange(FREQS) + 0.5) * (2 * np.pi / LENGTH)


def forward_matrix():
    angle = frequencies()[:, None] * np.arange(PADDED)[None, :]
    keep = (np.arange(PADDED) < SAMP)[None, :]
    (re_hi, re_lo), (im_hi, im_lo) = [split_bf16(part * keep) for part in (np.cos(angle), -np.sin(angle))]
    stacked = np.stack([re_hi, im_hi, re_lo, im_lo])
    stacked = stacked.reshape(4, FBLOCKS, FBLOCK, PADDED).transpose(1, 0, 2, 3)
    return np.ascontiguousarray(stacked.reshape(FBLOCKS, 4 * FBLOCK, PADDED))


def inverse_matrix():
    lag = np.arange(LAGS) - (LAGS - 1) // 2
    angle = lag[:, None] * frequencies()[None, :]
    padded = np.zeros((2, LAGPAD, FREQS))
    padded[0, :LAGS] = np.cos(angle)
    padded[1, :LAGS] = -np.sin(angle)
    padded *= 2.0 / LENGTH / math.sqrt(RECORD)
    return np.concatenate(split_bf16(padded.reshape(2 * LAGPAD, FREQS)), axis=0)


def spectrum_kernel(taps_ref, flags_ref, traces_ref, forward_ref, out_ref, padded, filtered, whitened, rows, block):
    edge = jnp.zeros((ROWS, 128), jnp.float32)
    padded[:, 0:128] = edge
    padded[:, 128 + RECORD : 256 + RECORD] = edge
    filtered[:, 0:128] = edge
    filtered[:, 128 + RECORD : 256 + RECORD] = edge
    whitened[:, RECORD : RECORD + 128] = edge
    padded[:, 128 : 128 + RECORD] = traces_ref[...]

    offset = lax.broadcasted_iota(jnp.int32, (384, 128), 0) - lax.broadcasted_iota(jnp.int32, (384, 128), 1)
    band = jnp.zeros((384, 128), jnp.float32)
    for tap in range(TAPS):
        band = jnp.where(offset == 128 - (TAPS - 1) // 2 + tap, taps_ref[tap], band)
    band_high = band.astype(jnp.bfloat16)
    band_low = (band - band_high.astype(jnp.float32)).astype(jnp.bfloat16)
    box = jnp.where((offset >= 128 - RADIUS) & (offset <= 128 + RADIUS), 1.0, 0.0).astype(jnp.bfloat16)

    def windows(ref, start):
        window = ref[:, pl.ds(start, (PER + 2) * 128)]
        tiles = [window[:, 128 * i : 128 * i + 128] for i in range(PER + 2)]
        stacked = [jnp.concatenate(tiles[i : i + PER], axis=0) for i in range(3)]
        return jnp.concatenate(stacked, axis=1)

    def halves(values):
        high = values.astype(jnp.bfloat16)
        return high, (values - high.astype(jnp.float32)).astype(jnp.bfloat16)

    def product(left, right):
        return jnp.dot(left, right, preferred_element_type=jnp.float32)

    def place(ref, start, values):
        for i in range(PER):
            ref[:, pl.ds(pl.multiple_of(start + 128 * i, 128), 128)] = values[ROWS * i : ROWS * (i + 1)]

    @pl.loop(0, BLOCKS // PER)
    def _(chunk):
        start = pl.multiple_of(chunk * (PER * 128), 128)
        high, low = halves(windows(padded, start))
        total = product(high, band_high) + (product(low, band_high) + product(high, band_low))
        place(filtered, start + 128, total)

    @pl.loop(0, BLOCKS // PER)
    def _(chunk):
        start = pl.multiple_of(chunk * (PER * 128), 128)
        values = windows(filtered, start)
        high, low = halves(jnp.abs(values))
        level = (product(high, box) + product(low, box)) / (2 * RADIUS + 1)
        place(whitened, start, values[:, 128:256] / (level + EPS))

    flags = flags_ref[...].astype(jnp.float32)
    for seg in range(SEGS):
        piece = whitened[:, seg * SAMP : seg * SAMP + PADDED] * flags[:, seg : seg + 1]
        for part in range(PADDED // 128):
            rows[part, pl.ds(seg, ROWS, stride=SEGS), :] = piece[:, part * 128 : part * 128 + 128]
    samples = jnp.concatenate([rows[part] for part in range(PADDED // 128)], axis=1).astype(jnp.bfloat16)

    low_half = lax.broadcasted_iota(jnp.int32, (FBLOCK, 128), 1) < HALF

    @pl.loop(0, FBLOCKS)
    def _(step):
        spectrum = lax.dot_general(
            forward_ref[step], samples, (((1,), (1,)), ((), ())), preferred_element_type=jnp.float32
        )
        both = spectrum[: 2 * FBLOCK] + spectrum[2 * FBLOCK :]
        for pair in range(ROWS // 2):
            real = both[:FBLOCK, pair * 128 : pair * 128 + 128]
            imag = both[FBLOCK:, pair * 128 : pair * 128 + 128]
            even = jnp.where(low_half, real, pltpu.roll(imag, HALF, 1))
            odd = jnp.where(low_half, pltpu.roll(real, HALF, 1), imag)
            block[pl.ds(2 * pair, FBLOCK, stride=ROWS), :] = even
            block[pl.ds(2 * pair + 1, FBLOCK, stride=ROWS), :] = odd
        out_ref[pl.ds(step * FBLOCK, FBLOCK)] = block[...].reshape(FBLOCK, ROWS, 128).astype(jnp.bfloat16)


def spectrum(traces, fir_taps, seg_flags):
    return pl.pallas_call(
        spectrum_kernel,
        out_shape=jax.ShapeDtypeStruct((FREQS, ROWS, 128), jnp.bfloat16),
        in_specs=[pl.BlockSpec(memory_space=pltpu.SMEM), VMEM, VMEM, VMEM],
        out_specs=VMEM,
        scratch_shapes=[
            pltpu.VMEM((ROWS, RECORD + 256), jnp.float32),
            pltpu.VMEM((ROWS, RECORD + 256), jnp.float32),
            pltpu.VMEM((ROWS, RECORD + 128), jnp.float32),
            pltpu.VMEM((PADDED // 128, ROWS * SEGS, 128), jnp.float32),
            pltpu.VMEM((FBLOCK * ROWS, 128), jnp.float32),
        ],
        compiler_params=pltpu.CompilerParams(vmem_limit_bytes=32 << 20),
        name="spectrum",
    )(fir_taps, seg_flags, traces, jnp.asarray(forward_matrix()))


def gather_kernel(own_ref, left_ref, right_ref, send_sem, recv_sem, local_sem):
    stn, seg = lax.axis_index("stn"), lax.axis_index("seg")
    core, z, x_lo = stn % 2, (stn // 2) % 4, stn // 8
    x_hi, y = seg % 2, seg // 2
    size = FREQS // PARTS
    half = size // 2

    def on_row(yy, hh):
        return (stn, (yy % 4) * 2 + hh)

    def on_column(zz, ll, cc):
        return ((ll * 4 + zz % 4) * 2 + cc, seg)

    neighbours = [on_row(y + 1, x_hi), on_row(y + 3, x_hi), on_row(y, 1 - x_hi)]
    neighbours += [on_column(z + 1, x_lo, core), on_column(z + 3, x_lo, core), on_column(z, 1 - x_lo, core)]
    neighbours += [on_column(z, x_lo, 1 - core)]
    barrier = pltpu.get_barrier_semaphore()
    for device in neighbours:
        pl.semaphore_signal(barrier, inc=1, device_id=device, device_id_type=MESH)
    pl.semaphore_wait(barrier, len(neighbours))

    started = []

    def send(kind, part, source, target, device):
        copy = pltpu.make_async_remote_copy(
            src_ref=source,
            dst_ref=target,
            send_sem=send_sem.at[part, kind],
            recv_sem=recv_sem.at[part, kind],
            device_id=device,
            device_id_type=MESH,
        )
        copy.start()
        started.append(copy)

    def arrive(kind, part, target):
        pltpu.make_async_remote_copy(
            src_ref=target,
            dst_ref=target,
            send_sem=send_sem.at[part, kind],
            recv_sem=recv_sem.at[part, kind],
            device_id=(stn, seg),
            device_id_type=MESH,
        ).wait_recv()

    def row_slot(yy, hh):
        return (yy % 4) * 2 + hh

    def column_slot(zz, ll, cc):
        return (ll * 4 + zz % 4) * 2 + cc

    def piece(ref, slot, part, which=None):
        first = part * size if which is None else part * size + which * half
        return ref.at[slot, pl.ds(first, size if which is None else half)]

    def own_piece(part):
        return own_ref.at[pl.ds(part * size, size)]

    class Ring:
        def __init__(self, ref, slot, device, place, first):
            self.ref, self.slot, self.device, self.place, self.first = ref, slot, device, place, first

        def start(self, part, source, group, kind):
            slot = self.slot(self.place, group)
            for side, step in ((0, 1), (1, 3)):
                send(self.first + kind + side, part, source, piece(self.ref, slot, part), self.device(self.place + step))

        def pass_on(self, part, group, kind):
            for side, step in ((0, 3), (1, 1)):
                slot = self.slot(self.place + step, group)
                arrive(self.first + kind + side, part, piece(self.ref, slot, part))
                data = piece(self.ref, slot, part, side)
                send(self.first + kind + 2 + side, part, data, data, self.device(self.place + 4 - step))

        def finish(self, part, group, kind):
            slot = self.slot(self.place + 2, group)
            for side in (0, 1):
                arrive(self.first + kind + 2 + side, part, piece(self.ref, slot, part, side))

    rows = Ring(left_ref, row_slot, lambda yy: on_row(yy, x_hi), y, 0)
    columns = Ring(right_ref, lambda zz, ll: column_slot(zz, ll, core), lambda zz: on_column(zz, x_lo, core), z, 9)
    twin = on_column(z, x_lo, 1 - core)

    def share(kind, part, zz, ll):
        data = piece(right_ref, column_slot(zz, ll, core), part)
        send(kind, part, data, data, twin)

    locals_ = []
    for part in range(PARTS):
        source = own_piece(part)
        rows.start(part, source, x_hi, 0)
        columns.start(part, source, x_lo, 0)
        send(8, part, source, piece(left_ref, row_slot(y, x_hi), part), on_row(y, 1 - x_hi))
        send(17, part, source, piece(right_ref, column_slot(z, x_lo, core), part), on_column(z, 1 - x_lo, core))
        send(18, part, source, piece(right_ref, column_slot(z, x_lo, core), part), twin)
    for index, target in enumerate((left_ref.at[row_slot(y, x_hi)], right_ref.at[column_slot(z, x_lo, core)])):
        copy = pltpu.make_async_copy(own_ref, target, local_sem.at[index])
        copy.start()
        locals_.append(copy)

    for part in range(PARTS):
        rows.pass_on(part, x_hi, 0)
        columns.pass_on(part, x_lo, 0)
        share(19, part, z + 3, x_lo)
        share(20, part, z + 1, x_lo)
        arrive(17, part, piece(right_ref, column_slot(z, 1 - x_lo, core), part))
        columns.start(part, piece(right_ref, column_slot(z, 1 - x_lo, core), part), 1 - x_lo, 4)
        share(22, part, z, 1 - x_lo)
        arrive(8, part, piece(left_ref, row_slot(y, 1 - x_hi), part))
        rows.start(part, piece(left_ref, row_slot(y, 1 - x_hi), part), 1 - x_hi, 4)
    for part in range(PARTS):
        rows.finish(part, x_hi, 0)
        columns.finish(part, x_lo, 0)
        share(21, part, z + 2, x_lo)
        columns.pass_on(part, 1 - x_lo, 4)
        share(23, part, z + 3, 1 - x_lo)
        share(24, part, z + 1, 1 - x_lo)
        rows.pass_on(part, 1 - x_hi, 4)
    for part in range(PARTS):
        columns.finish(part, 1 - x_lo, 4)
        share(25, part, z + 2, 1 - x_lo)
        rows.finish(part, 1 - x_hi, 4)
    order = ((18, 0, x_lo), (19, 3, x_lo), (20, 1, x_lo), (21, 2, x_lo))
    order += ((22, 0, 1 - x_lo), (23, 3, 1 - x_lo), (24, 1, 1 - x_lo), (25, 2, 1 - x_lo))
    for part in range(PARTS):
        for kind, step, ll in order:
            arrive(kind, part, piece(right_ref, column_slot(z + step, ll, 1 - core), part))
    for copy in started:
        copy.wait_send()
    for copy in locals_:
        copy.wait()


def gather(own):
    shapes = [jax.ShapeDtypeStruct((count,) + own.shape, own.dtype) for count in (SEG, STN)]
    return pl.pallas_call(
        gather_kernel,
        out_shape=shapes,
        in_specs=[VMEM],
        out_specs=[ANY, ANY],
        scratch_shapes=[
            pltpu.SemaphoreType.DMA((PARTS, 26)),
            pltpu.SemaphoreType.DMA((PARTS, 26)),
            pltpu.SemaphoreType.DMA((2,)),
        ],
        compiler_params=pltpu.CompilerParams(collective_id=0, has_side_effects=True),
        name="gather",
    )(own)


STEP = 24
UNROLL = 8


def correlate_kernel(left_ref, right_ref, inverse_ref, out_ref, cross):
    step = pl.program_id(0)
    sign = jnp.where(lax.broadcasted_iota(jnp.int32, (LEFT, 128), 1) < HALF, -1.0, 1.0)

    @pl.loop(0, STEP // UNROLL)
    def _(turn):
        for offset in range(UNROLL):
            index = turn * UNROLL + offset
            left = left_ref[:, index].astype(jnp.float32).reshape(LEFT, 128)
            right = right_ref[:, index].reshape(RIGHT, 128)
            turned = pltpu.roll(left, HALF, 1) * sign
            both = jnp.concatenate([left, turned], axis=0).astype(jnp.bfloat16)
            product = lax.dot_general(right, both, (((1,), (1,)), ((), ())), preferred_element_type=jnp.float32)
            at = pl.multiple_of((step * STEP + index) * PITCH, 8)
            cross[pl.ds(at, RIGHT), :] = product

    @pl.when(step == pl.num_programs(0) - 1)
    def _():
        low_half = lax.broadcasted_iota(jnp.int32, (LAGPAD, 128), 1) < HALF

        def lagged(row):
            values = cross[pl.ds(row, FREQS, stride=PITCH), :].astype(jnp.bfloat16)
            parts = jnp.dot(inverse_ref[...], values, preferred_element_type=jnp.float32)
            parts = parts[: 2 * LAGPAD] + parts[2 * LAGPAD :]
            return parts[:LAGPAD], parts[LAGPAD:]

        @pl.loop(0, GROUPS)
        def _(group):
            for row in range(ROWS):
                first_re, first_im = lagged(group * (2 * ROWS) + row)
                second_re, second_im = lagged(group * (2 * ROWS) + ROWS + row)
                straight = jnp.where(low_half, first_re, second_im)
                crossed = jnp.where(low_half, second_re, first_im)
                out_ref[group, row] = (straight + pltpu.roll(crossed, HALF, 1)).astype(jnp.bfloat16)


def correlate(left, right):
    return pl.pallas_call(
        correlate_kernel,
        grid=(FREQS // STEP,),
        out_shape=jax.ShapeDtypeStruct((GROUPS, ROWS, LAGPAD, 128), jnp.bfloat16),
        in_specs=[
            pl.BlockSpec((SEG, STEP, ROWS, 128), lambda i: (0, i, 0, 0)),
            pl.BlockSpec((STN, STEP, ROWS, 128), lambda i: (0, i, 0, 0)),
            pl.BlockSpec((4 * LAGPAD, FREQS), lambda i: (0, 0)),
        ],
        out_specs=pl.BlockSpec((GROUPS, ROWS, LAGPAD, 128), lambda i: (0, 0, 0, 0)),
        scratch_shapes=[pltpu.VMEM((FREQS * PITCH, 128), jnp.float32)],
        compiler_params=pltpu.CompilerParams(vmem_limit_bytes=50 << 20),
        name="correlate",
    )(left, right, jnp.asarray(inverse_matrix()))


def exchange_kernel(mine_ref, out_ref, send_sem, recv_sem, local_sem):
    stn, seg = lax.axis_index("stn"), lax.axis_index("seg")
    barrier = pltpu.get_barrier_semaphore()
    for shift in range(1, SEG):
        pl.semaphore_signal(barrier, inc=1, device_id=(stn, (seg + shift) % SEG), device_id_type=MESH)
    pl.semaphore_wait(barrier, SEG - 1)
    copies = []
    for shift in range(1, SEG):
        peer = (seg + shift) % SEG
        copy = pltpu.make_async_remote_copy(
            src_ref=mine_ref.at[peer],
            dst_ref=out_ref.at[seg],
            send_sem=send_sem.at[shift],
            recv_sem=recv_sem.at[shift],
            device_id=(stn, peer),
            device_id_type=MESH,
        )
        copy.start()
        copies.append(copy)
    keep = pltpu.make_async_copy(mine_ref.at[seg], out_ref.at[seg], local_sem)
    keep.start()
    for shift in range(1, SEG):
        slot = out_ref.at[(seg + SEG - shift) % SEG]
        pltpu.make_async_remote_copy(
            src_ref=slot,
            dst_ref=slot,
            send_sem=send_sem.at[shift],
            recv_sem=recv_sem.at[shift],
            device_id=(stn, seg),
            device_id_type=MESH,
        ).wait_recv()
    for copy in copies:
        copy.wait_send()
    keep.wait()


def exchange(mine):
    return pl.pallas_call(
        exchange_kernel,
        out_shape=jax.ShapeDtypeStruct(mine.shape, mine.dtype),
        in_specs=[VMEM],
        out_specs=VMEM,
        scratch_shapes=[
            pltpu.SemaphoreType.DMA((SEG,)),
            pltpu.SemaphoreType.DMA((SEG,)),
            pltpu.SemaphoreType.DMA,
        ],
        compiler_params=pltpu.CompilerParams(collective_id=1, has_side_effects=True),
        name="exchange",
    )(mine)


def finish_kernel(values_ref, mask_ref, out_ref, wide):
    pitch = LAGPAD + 8
    for source in range(SEG):
        for row in range(ROWS):
            at = (source * ROWS + row) * pitch
            wide[at : at + LAGPAD, :] = values_ref[source, row].astype(jnp.float32)
    keep = mask_ref[...].astype(jnp.float32)
    for lag in range(LAGS):
        turned = wide[pl.ds(lag, SEG * ROWS, stride=pitch), :].T
        out_ref[lag] = jnp.concatenate([turned[:LEFT], turned[LEFT:]], axis=1) * keep


def finish(values, pair_mask):
    return pl.pallas_call(
        finish_kernel,
        out_shape=jax.ShapeDtypeStruct((LAGS, LEFT, RIGHT), jnp.float32),
        in_specs=[VMEM, VMEM],
        out_specs=VMEM,
        scratch_shapes=[pltpu.VMEM((SEG * ROWS * (LAGPAD + 8), 128), jnp.float32)],
        name="finish",
    )(values, pair_mask)


def body(traces, fir_taps, seg_flags, pair_mask):
    own = spectrum(traces, fir_taps, seg_flags)
    left, right = gather(own)
    return finish(exchange(correlate(left, right)), pair_mask)


def solution(mesh):
    return jax.shard_map(
        body,
        mesh=mesh,
        in_specs=(P(("stn", "seg"), None), P(), P(("stn", "seg"), None), P("stn", "seg")),
        out_specs=P(None, "stn", "seg"),
        check_vma=False,
    )
```

```python
import functools
import math

import jax
import jax.numpy as jnp
import numpy as np
from jax import lax
from jax.experimental import pallas as pl
from jax.experimental.pallas import tpu as pltpu
from jax.sharding import PartitionSpec as P

SAMP = 600
LAGS = 41
TAPS = 31
RADIUS = 64
SEGS = 64
ROWS = 8
EPS = 1e-06

LENGTH = 624
PADDED = 640
FREQS = LENGTH // 2
HALF = SEGS
FBLOCK = 104
FBLOCKS = FREQS // FBLOCK
LAGPAD = 48
PITCH = 136

RECORD = SEGS * SAMP
BLOCKS = RECORD // 128
PER = 30

STN, SEG = 16, 8
LEFT = ROWS * SEG
RIGHT = ROWS * STN
PARTS = 3

MESH = pl.DeviceIdType.MESH
VMEM = pl.BlockSpec(memory_space=pltpu.VMEM)


def split_bf16(values):
    high = np.asarray(values, np.float32).astype(jnp.bfloat16)
    low = (np.asarray(values, np.float64) - high.astype(np.float64)).astype(np.float32).astype(jnp.bfloat16)
    return high, low


def frequencies():
    return (np.arange(FREQS) + 0.5) * (2 * np.pi / LENGTH)


def forward_matrix():
    angle = frequencies()[:, None] * np.arange(PADDED)[None, :]
    keep = (np.arange(PADDED) < SAMP)[None, :]
    (re_hi, re_lo), (im_hi, im_lo) = [split_bf16(part * keep) for part in (np.cos(angle), -np.sin(angle))]
    stacked = np.stack([re_hi, im_hi, re_lo, im_lo])
    stacked = stacked.reshape(4, FBLOCKS, FBLOCK, PADDED).transpose(1, 0, 2, 3)
    return np.ascontiguousarray(stacked.reshape(FBLOCKS, 4 * FBLOCK, PADDED))


def inverse_matrix():
    lag = np.arange(LAGS) - (LAGS - 1) // 2
    angle = lag[:, None] * frequencies()[None, :]
    padded = np.zeros((2, LAGPAD, FREQS))
    padded[0, :LAGS] = np.cos(angle)
    padded[1, :LAGS] = -np.sin(angle)
    padded *= 2.0 / LENGTH / math.sqrt(RECORD)
    return np.concatenate(split_bf16(padded.reshape(2 * LAGPAD, FREQS)), axis=0)


def spectrum_kernel(taps_ref, flags_ref, traces_ref, forward_ref, out_ref, padded, filtered, whitened, rows, block):
    edge = jnp.zeros((ROWS, 128), jnp.float32)
    padded[:, 0:128] = edge
    padded[:, 128 + RECORD : 256 + RECORD] = edge
    filtered[:, 0:128] = edge
    filtered[:, 128 + RECORD : 256 + RECORD] = edge
    whitened[:, RECORD : RECORD + 128] = edge
    padded[:, 128 : 128 + RECORD] = traces_ref[...]

    offset = lax.broadcasted_iota(jnp.int32, (384, 128), 0) - lax.broadcasted_iota(jnp.int32, (384, 128), 1)
    band = jnp.zeros((384, 128), jnp.float32)
    for tap in range(TAPS):
        band = jnp.where(offset == 128 - (TAPS - 1) // 2 + tap, taps_ref[tap], band)
    band_high = band.astype(jnp.bfloat16)
    band_low = (band - band_high.astype(jnp.float32)).astype(jnp.bfloat16)
    box = jnp.where((offset >= 128 - RADIUS) & (offset <= 128 + RADIUS), 1.0, 0.0).astype(jnp.bfloat16)

    def windows(ref, start):
        window = ref[:, pl.ds(start, (PER + 2) * 128)]
        tiles = [window[:, 128 * i : 128 * i + 128] for i in range(PER + 2)]
        stacked = [jnp.concatenate(tiles[i : i + PER], axis=0) for i in range(3)]
        return jnp.concatenate(stacked, axis=1)

    def halves(values):
        high = values.astype(jnp.bfloat16)
        return high, (values - high.astype(jnp.float32)).astype(jnp.bfloat16)

    def product(left, right):
        return jnp.dot(left, right, preferred_element_type=jnp.float32)

    def place(ref, start, values):
        for i in range(PER):
            ref[:, pl.ds(pl.multiple_of(start + 128 * i, 128), 128)] = values[ROWS * i : ROWS * (i + 1)]

    @pl.loop(0, BLOCKS // PER)
    def _(chunk):
        start = pl.multiple_of(chunk * (PER * 128), 128)
        high, low = halves(windows(padded, start))
        total = product(high, band_high) + (product(low, band_high) + product(high, band_low))
        place(filtered, start + 128, total)

    @pl.loop(0, BLOCKS // PER)
    def _(chunk):
        start = pl.multiple_of(chunk * (PER * 128), 128)
        values = windows(filtered, start)
        high, low = halves(jnp.abs(values))
        level = (product(high, box) + product(low, box)) / (2 * RADIUS + 1)
        place(whitened, start, values[:, 128:256] / (level + EPS))

    flags = flags_ref[...].astype(jnp.float32)
    for seg in range(SEGS):
        piece = whitened[:, seg * SAMP : seg * SAMP + PADDED] * flags[:, seg : seg + 1]
        for part in range(PADDED // 128):
            rows[part, pl.ds(seg, ROWS, stride=SEGS), :] = piece[:, part * 128 : part * 128 + 128]
    samples = jnp.concatenate([rows[part] for part in range(PADDED // 128)], axis=1).astype(jnp.bfloat16)

    low_half = lax.broadcasted_iota(jnp.int32, (FBLOCK, 128), 1) < HALF

    @pl.loop(0, FBLOCKS)
    def _(step):
        spectrum = lax.dot_general(
            forward_ref[step], samples, (((1,), (1,)), ((), ())), preferred_element_type=jnp.float32
        )
        both = spectrum[: 2 * FBLOCK] + spectrum[2 * FBLOCK :]
        for pair in range(ROWS // 2):
            real = both[:FBLOCK, pair * 128 : pair * 128 + 128]
            imag = both[FBLOCK:, pair * 128 : pair * 128 + 128]
            even = jnp.where(low_half, real, pltpu.roll(imag, HALF, 1))
            odd = jnp.where(low_half, pltpu.roll(real, HALF, 1), imag)
            block[pl.ds(2 * pair, FBLOCK, stride=ROWS), :] = even
            block[pl.ds(2 * pair + 1, FBLOCK, stride=ROWS), :] = odd
        out_ref[pl.ds(step * FBLOCK, FBLOCK)] = block[...].reshape(FBLOCK, ROWS, 128).astype(jnp.bfloat16)


def spectrum(traces, fir_taps, seg_flags):
    return pl.pallas_call(
        spectrum_kernel,
        out_shape=jax.ShapeDtypeStruct((FREQS, ROWS, 128), jnp.bfloat16),
        in_specs=[pl.BlockSpec(memory_space=pltpu.SMEM), VMEM, VMEM, VMEM],
        out_specs=VMEM,
        scratch_shapes=[
            pltpu.VMEM((ROWS, RECORD + 256), jnp.float32),
            pltpu.VMEM((ROWS, RECORD + 256), jnp.float32),
            pltpu.VMEM((ROWS, RECORD + 128), jnp.float32),
            pltpu.VMEM((PADDED // 128, ROWS * SEGS, 128), jnp.float32),
            pltpu.VMEM((FBLOCK * ROWS, 128), jnp.float32),
        ],
        compiler_params=pltpu.CompilerParams(vmem_limit_bytes=32 << 20),
        name="spectrum",
    )(fir_taps, seg_flags, traces, jnp.asarray(forward_matrix()))


UNROLL = 8


def pairs_kernel(own_ref, inverse_ref, out_ref, left_ref, right_ref, cross, message, stage, send_sem, recv_sem, local_sem, out_send, out_recv):
    stn, seg = lax.axis_index("stn"), lax.axis_index("seg")
    core, z, x_lo = stn % 2, (stn // 2) % 4, stn // 8
    x_hi, y = seg % 2, seg // 2
    size = FREQS // PARTS
    half = size // 2

    def on_row(yy, hh):
        return (stn, (yy % 4) * 2 + hh)

    def on_column(zz, ll, cc):
        return ((ll * 4 + zz % 4) * 2 + cc, seg)

    def row_slot(yy, hh):
        return (yy % 4) * 2 + hh

    def column_slot(zz, ll, cc):
        return (ll * 4 + zz % 4) * 2 + cc

    across = (on_column(z, 1 - x_lo, core)[0], row_slot(y, 1 - x_hi))
    twin = on_column(z, x_lo, 1 - core)
    neighbours = [on_column(z + 1, x_lo, core), on_column(z + 3, x_lo, core), on_column(z, 1 - x_lo, core), twin, across]
    neighbours += [(stn, (seg + shift) % SEG) for shift in range(1, SEG)]
    barrier = pltpu.get_barrier_semaphore()
    for device in neighbours:
        pl.semaphore_signal(barrier, inc=1, device_id=device, device_id_type=MESH)
    pl.semaphore_wait(barrier, len(neighbours))

    started = []

    def send(kind, part, source, target, device):
        copy = pltpu.make_async_remote_copy(
            src_ref=source,
            dst_ref=target,
            send_sem=send_sem.at[part, kind],
            recv_sem=recv_sem.at[part, kind],
            device_id=device,
            device_id_type=MESH,
        )
        copy.start()
        started.append(copy)

    def arrive(kind, part, target):
        pltpu.make_async_remote_copy(
            src_ref=target,
            dst_ref=target,
            send_sem=send_sem.at[part, kind],
            recv_sem=recv_sem.at[part, kind],
            device_id=(stn, seg),
            device_id_type=MESH,
        ).wait_recv()

    def piece(ref, slot, part, which=None):
        first = part * size if which is None else part * size + which * half
        return ref.at[slot, pl.ds(first, size if which is None else half)]

    class Ring:
        def __init__(self, ref, slot, device, place, first):
            self.ref, self.slot, self.device, self.place, self.first = ref, slot, device, place, first

        def start(self, part, source, group, kind):
            slot = self.slot(self.place, group)
            for side, step in ((0, 1), (1, 3)):
                send(self.first + kind + side, part, source, piece(self.ref, slot, part), self.device(self.place + step))

        def pass_on(self, part, group, kind):
            for side, step in ((0, 3), (1, 1)):
                slot = self.slot(self.place + step, group)
                arrive(self.first + kind + side, part, piece(self.ref, slot, part))
                data = piece(self.ref, slot, part, side)
                send(self.first + kind + 2 + side, part, data, data, self.device(self.place + 4 - step))

        def finish(self, part, group, kind):
            slot = self.slot(self.place + 2, group)
            for side in (0, 1):
                arrive(self.first + kind + 2 + side, part, piece(self.ref, slot, part, side))

    rows = Ring(left_ref, row_slot, lambda yy: on_row(yy, x_hi), y, 0)
    columns = Ring(right_ref, lambda zz, ll: column_slot(zz, ll, core), lambda zz: on_column(zz, x_lo, core), z, 9)

    def share(kind, part, zz, ll):
        data = piece(right_ref, column_slot(zz, ll, core), part)
        send(kind, part, data, data, twin)

    def start_own(part):
        source = own_ref.at[pl.ds(part * size, size)]
        rows.start(part, source, x_hi, 0)
        columns.start(part, source, x_lo, 0)
        own_column = piece(right_ref, column_slot(z, x_lo, core), part)
        send(17, part, source, own_column, on_column(z, 1 - x_lo, core))
        send(18, part, source, own_column, twin)

    def pass_own(part):
        rows.pass_on(part, x_hi, 0)
        columns.pass_on(part, x_lo, 0)
        share(19, part, z + 3, x_lo)
        share(20, part, z + 1, x_lo)

    def relay(part):
        data = piece(right_ref, column_slot(z, 1 - x_lo, core), part)
        arrive(17, part, data)
        send(8, part, data, piece(left_ref, row_slot(y, x_hi), part), across)
        columns.start(part, data, 1 - x_lo, 4)
        share(22, part, z, 1 - x_lo)

    def start_partner(part):
        data = piece(left_ref, row_slot(y, 1 - x_hi), part)
        arrive(8, part, data)
        rows.start(part, data, 1 - x_hi, 4)

    def pass_partner(part):
        columns.pass_on(part, 1 - x_lo, 4)
        rows.pass_on(part, 1 - x_hi, 4)
        share(23, part, z + 3, 1 - x_lo)
        share(24, part, z + 1, 1 - x_lo)

    def complete_own(part):
        columns.finish(part, x_lo, 0)
        share(21, part, z + 2, x_lo)
        rows.finish(part, x_hi, 0)

    def complete(part):
        columns.finish(part, 1 - x_lo, 4)
        share(25, part, z + 2, 1 - x_lo)
        rows.finish(part, 1 - x_hi, 4)
        order = ((18, 0, x_lo), (19, 3, x_lo), (20, 1, x_lo), (21, 2, x_lo))
        order += ((22, 0, 1 - x_lo), (23, 3, 1 - x_lo), (24, 1, 1 - x_lo), (25, 2, 1 - x_lo))
        for kind, step, ll in order:
            arrive(kind, part, piece(right_ref, column_slot(z + step, ll, 1 - core), part))

    sign = jnp.where(lax.broadcasted_iota(jnp.int32, (LEFT, 128), 1) < HALF, -1.0, 1.0)

    def multiply(part, first, last):
        @pl.loop(first, last)
        def _(turn):
            for offset in range(UNROLL):
                index = part * size + turn * UNROLL + offset
                left = left_ref[:, index].astype(jnp.float32).reshape(LEFT, 128)
                right = right_ref[:, index].reshape(RIGHT, 128)
                turned = pltpu.roll(left, HALF, 1) * sign
                both = jnp.concatenate([left, turned], axis=0).astype(jnp.bfloat16)
                product = lax.dot_general(right, both, (((1,), (1,)), ((), ())), preferred_element_type=jnp.float32)
                cross[pl.ds(pl.multiple_of(index * PITCH, 8), RIGHT), :] = product

    turns = size // UNROLL
    start_own(0)
    start_own(1)
    locals_ = []
    for index, target in enumerate((left_ref.at[row_slot(y, x_hi)], right_ref.at[column_slot(z, x_lo, core)])):
        copy = pltpu.make_async_copy(own_ref, target, local_sem.at[index])
        copy.start()
        locals_.append(copy)
    pass_own(0)
    relay(0)
    pass_own(1)
    relay(1)
    start_partner(0)
    start_own(2)
    complete_own(0)
    pass_partner(0)
    start_partner(1)
    pass_own(2)
    relay(2)
    complete_own(1)
    for copy in locals_:
        copy.wait()
    complete(0)
    multiply(0, 0, turns)
    start_partner(2)
    pass_partner(1)
    complete_own(2)
    complete(1)
    multiply(1, 0, turns // 2)
    pass_partner(2)
    multiply(1, turns // 2, turns)
    complete(2)
    multiply(2, 0, turns)

    low_half = lax.broadcasted_iota(jnp.int32, (LAGPAD, 128), 1) < HALF

    def lagged(row):
        values = cross[pl.ds(row, FREQS, stride=PITCH), :].astype(jnp.bfloat16)
        parts = jnp.dot(inverse_ref[...], values, preferred_element_type=jnp.float32)
        parts = parts[: 2 * LAGPAD] + parts[2 * LAGPAD :]
        return parts[:LAGPAD], parts[LAGPAD:]

    def transform(group):
        for row in range(ROWS):
            first_re, first_im = lagged(group * (2 * ROWS) + row)
            second_re, second_im = lagged(group * (2 * ROWS) + ROWS + row)
            straight = jnp.where(low_half, first_re, second_im)
            crossed = jnp.where(low_half, second_re, first_im)
            stage[pl.ds(row, LAGPAD, stride=ROWS), :] = straight + pltpu.roll(crossed, HALF, 1)
        return stage[: LAGS * ROWS, :].reshape(LAGS, ROWS, 128).astype(jnp.bfloat16)

    def hand_over(shift):
        peer = (seg + shift) % SEG
        return pltpu.make_async_remote_copy(
            src_ref=message.at[peer],
            dst_ref=out_ref.at[seg],
            send_sem=out_send.at[shift],
            recv_sem=out_recv.at[shift],
            device_id=(stn, peer),
            device_id_type=MESH,
        )

    @pl.loop(1, SEG)
    def _(shift):
        group = (seg + shift) % SEG
        message[group] = transform(group)

        @pl.when(shift > 1)
        def _():
            hand_over(shift - 1).start()

    out_ref[seg] = transform(seg)
    hand_over(SEG - 1).start()
    for copy in started:
        copy.wait_send()
    for shift in range(1, SEG):
        slot = out_ref.at[(seg + SEG - shift) % SEG]
        pltpu.make_async_remote_copy(
            src_ref=slot,
            dst_ref=slot,
            send_sem=out_send.at[shift],
            recv_sem=out_recv.at[shift],
            device_id=(stn, seg),
            device_id_type=MESH,
        ).wait_recv()
        hand_over(shift).wait_send()


def pairs(own):
    result = (SEG, LAGS, ROWS, 128)
    return pl.pallas_call(
        pairs_kernel,
        out_shape=jax.ShapeDtypeStruct(result, jnp.bfloat16),
        in_specs=[VMEM, VMEM],
        out_specs=VMEM,
        scratch_shapes=[
            pltpu.VMEM((SEG,) + own.shape, jnp.bfloat16),
            pltpu.VMEM((STN,) + own.shape, jnp.bfloat16),
            pltpu.VMEM((FREQS * PITCH, 128), jnp.float32),
            pltpu.VMEM(result, jnp.bfloat16),
            pltpu.VMEM((LAGPAD * ROWS, 128), jnp.float32),
            pltpu.SemaphoreType.DMA((PARTS, 26)),
            pltpu.SemaphoreType.DMA((PARTS, 26)),
            pltpu.SemaphoreType.DMA((2,)),
            pltpu.SemaphoreType.DMA((SEG,)),
            pltpu.SemaphoreType.DMA((SEG,)),
        ],
        compiler_params=pltpu.CompilerParams(collective_id=0, has_side_effects=True, vmem_limit_bytes=56 << 20),
        name="pairs",
    )(own, jnp.asarray(inverse_matrix()))


def finish_kernel(values_ref, mask_ref, out_ref):
    keep = mask_ref[...].astype(jnp.float32)
    for lag in range(LAGS):
        turned = values_ref[:, lag].astype(jnp.float32).reshape(LEFT, 128).T
        out_ref[lag] = jnp.concatenate([turned[:LEFT], turned[LEFT:]], axis=1) * keep


def finish(values, pair_mask):
    return pl.pallas_call(
        finish_kernel,
        out_shape=jax.ShapeDtypeStruct((LAGS, LEFT, RIGHT), jnp.float32),
        in_specs=[VMEM, VMEM],
        out_specs=VMEM,
        name="finish",
    )(values, pair_mask)


def body(traces, fir_taps, seg_flags, pair_mask):
    own = spectrum(traces, fir_taps, seg_flags)
    return finish(pairs(own), pair_mask)


def solution(mesh):
    return jax.shard_map(
        body,
        mesh=mesh,
        in_specs=(P(("stn", "seg"), None), P(), P(("stn", "seg"), None), P("stn", "seg")),
        out_specs=P(None, "stn", "seg"),
        check_vma=False,
    )
```

```python
import functools
import math

import jax
import jax.numpy as jnp
import numpy as np
from jax import lax
from jax.experimental import pallas as pl
from jax.experimental.pallas import tpu as pltpu
from jax.sharding import PartitionSpec as P

SAMP = 600
LAGS = 41
TAPS = 31
RADIUS = 64
SEGS = 64
ROWS = 8
EPS = 1e-06

LENGTH = 624
PADDED = 640
FREQS = LENGTH // 2
HALF = SEGS
FBLOCK = 104
FBLOCKS = FREQS // FBLOCK
LAGPAD = 48
PITCH = 136

RECORD = SEGS * SAMP
BLOCKS = RECORD // 128
PER = 30

STN, SEG = 16, 8
LEFT = ROWS * SEG
RIGHT = ROWS * STN
PARTS = 6

MESH = pl.DeviceIdType.MESH
VMEM = pl.BlockSpec(memory_space=pltpu.VMEM)


def split_bf16(values):
    high = np.asarray(values, np.float32).astype(jnp.bfloat16)
    low = (np.asarray(values, np.float64) - high.astype(np.float64)).astype(np.float32).astype(jnp.bfloat16)
    return high, low


def frequencies():
    return (np.arange(FREQS) + 0.5) * (2 * np.pi / LENGTH)


def forward_matrix():
    angle = frequencies()[:, None] * np.arange(PADDED)[None, :]
    keep = (np.arange(PADDED) < SAMP)[None, :]
    (re_hi, re_lo), (im_hi, im_lo) = [split_bf16(part * keep) for part in (np.cos(angle), -np.sin(angle))]
    stacked = np.stack([re_hi, im_hi, re_lo, im_lo])
    stacked = stacked.reshape(4, FBLOCKS, FBLOCK, PADDED).transpose(1, 0, 2, 3)
    return np.ascontiguousarray(stacked.reshape(FBLOCKS, 4 * FBLOCK, PADDED))


def inverse_matrix():
    lag = np.arange(LAGS) - (LAGS - 1) // 2
    angle = lag[:, None] * frequencies()[None, :]
    padded = np.zeros((2, LAGPAD, FREQS))
    padded[0, :LAGS] = np.cos(angle)
    padded[1, :LAGS] = -np.sin(angle)
    padded *= 2.0 / LENGTH / math.sqrt(RECORD)
    return np.concatenate(split_bf16(padded.reshape(2 * LAGPAD, FREQS)), axis=0)


def spectrum_kernel(taps_ref, flags_ref, traces_ref, forward_ref, out_ref, padded, filtered, whitened, rows, block):
    edge = jnp.zeros((ROWS, 128), jnp.float32)
    padded[:, 0:128] = edge
    padded[:, 128 + RECORD : 256 + RECORD] = edge
    filtered[:, 0:128] = edge
    filtered[:, 128 + RECORD : 256 + RECORD] = edge
    whitened[:, RECORD : RECORD + 128] = edge
    padded[:, 128 : 128 + RECORD] = traces_ref[...]

    offset = lax.broadcasted_iota(jnp.int32, (384, 128), 0) - lax.broadcasted_iota(jnp.int32, (384, 128), 1)
    band = jnp.zeros((384, 128), jnp.float32)
    for tap in range(TAPS):
        band = jnp.where(offset == 128 - (TAPS - 1) // 2 + tap, taps_ref[tap], band)
    band_high = band.astype(jnp.bfloat16)
    band_low = (band - band_high.astype(jnp.float32)).astype(jnp.bfloat16)
    box = jnp.where((offset >= 128 - RADIUS) & (offset <= 128 + RADIUS), 1.0, 0.0).astype(jnp.bfloat16)

    def windows(ref, start):
        window = ref[:, pl.ds(start, (PER + 2) * 128)]
        tiles = [window[:, 128 * i : 128 * i + 128] for i in range(PER + 2)]
        stacked = [jnp.concatenate(tiles[i : i + PER], axis=0) for i in range(3)]
        return jnp.concatenate(stacked, axis=1)

    def halves(values):
        high = values.astype(jnp.bfloat16)
        return high, (values - high.astype(jnp.float32)).astype(jnp.bfloat16)

    def product(left, right):
        return jnp.dot(left, right, preferred_element_type=jnp.float32)

    def place(ref, start, values):
        for i in range(PER):
            ref[:, pl.ds(pl.multiple_of(start + 128 * i, 128), 128)] = values[ROWS * i : ROWS * (i + 1)]

    @pl.loop(0, BLOCKS // PER)
    def _(chunk):
        start = pl.multiple_of(chunk * (PER * 128), 128)
        high, low = halves(windows(padded, start))
        total = product(high, band_high) + (product(low, band_high) + product(high, band_low))
        place(filtered, start + 128, total)

    @pl.loop(0, BLOCKS // PER)
    def _(chunk):
        start = pl.multiple_of(chunk * (PER * 128), 128)
        values = windows(filtered, start)
        high, low = halves(jnp.abs(values))
        level = (product(high, box) + product(low, box)) / (2 * RADIUS + 1)
        place(whitened, start, values[:, 128:256] / (level + EPS))

    flags = flags_ref[...].astype(jnp.float32)
    for seg in range(SEGS):
        piece = whitened[:, seg * SAMP : seg * SAMP + PADDED] * flags[:, seg : seg + 1]
        for part in range(PADDED // 128):
            rows[part, pl.ds(seg, ROWS, stride=SEGS), :] = piece[:, part * 128 : part * 128 + 128]
    samples = jnp.concatenate([rows[part] for part in range(PADDED // 128)], axis=1).astype(jnp.bfloat16)

    low_half = lax.broadcasted_iota(jnp.int32, (FBLOCK, 128), 1) < HALF

    @pl.loop(0, FBLOCKS)
    def _(step):
        spectrum = lax.dot_general(
            forward_ref[step], samples, (((1,), (1,)), ((), ())), preferred_element_type=jnp.float32
        )
        both = spectrum[: 2 * FBLOCK] + spectrum[2 * FBLOCK :]
        for pair in range(ROWS // 2):
            real = both[:FBLOCK, pair * 128 : pair * 128 + 128]
            imag = both[FBLOCK:, pair * 128 : pair * 128 + 128]
            even = jnp.where(low_half, real, pltpu.roll(imag, HALF, 1))
            odd = jnp.where(low_half, pltpu.roll(real, HALF, 1), imag)
            block[pl.ds(2 * pair, FBLOCK, stride=ROWS), :] = even
            block[pl.ds(2 * pair + 1, FBLOCK, stride=ROWS), :] = odd
        out_ref[pl.ds(step * FBLOCK, FBLOCK)] = block[...].reshape(FBLOCK, ROWS, 128).astype(jnp.bfloat16)


def spectrum(traces, fir_taps, seg_flags):
    return pl.pallas_call(
        spectrum_kernel,
        out_shape=jax.ShapeDtypeStruct((FREQS, ROWS, 128), jnp.bfloat16),
        in_specs=[pl.BlockSpec(memory_space=pltpu.SMEM), VMEM, VMEM, VMEM],
        out_specs=VMEM,
        scratch_shapes=[
            pltpu.VMEM((ROWS, RECORD + 256), jnp.float32),
            pltpu.VMEM((ROWS, RECORD + 256), jnp.float32),
            pltpu.VMEM((ROWS, RECORD + 128), jnp.float32),
            pltpu.VMEM((PADDED // 128, ROWS * SEGS, 128), jnp.float32),
            pltpu.VMEM((FBLOCK * ROWS, 128), jnp.float32),
        ],
        compiler_params=pltpu.CompilerParams(vmem_limit_bytes=32 << 20),
        name="spectrum",
    )(fir_taps, seg_flags, traces, jnp.asarray(forward_matrix()))


UNROLL = 13

ROWS_ALONG_X = (2,)
COLUMNS_ALONG_X = (1, 4)
AHEAD = 3


def transfer_order():
    unit, latency, twin, product = 15.2 / PARTS, 1.6, 3.0 / PARTS, 12.7 * UNROLL / FREQS
    rank = ("own", "rel", "stp", "pro", "pco", "prp", "pcp", "cro", "cco", "ccp", "done")
    acts = {}
    for part in range(PARTS):
        in_rows, in_columns = part in ROWS_ALONG_X, part in COLUMNS_ALONG_X

        def both(axis, stage, share):
            return [(link, stage + link, share * unit) for link in (axis + "+", axis + "-")]

        table = {
            "own": ("", both("y", "o", 1) + both("z", "o", 1) + [("l", "l", unit), ("t", "t0", twin)]),
            "pro": ("oy+ oy-", both("y", "f", 0.5) + [("l c", "r1", 2 * unit)] * in_rows),
            "pco": ("oz+ oz-", both("z", "f", 0.5) + [("l", "c1", 2 * unit)] * in_columns + [("t", "t1", 2 * twin)]),
            "rel": ("l", [("c", "c", unit), ("t", "t2", twin)] + ([] if in_columns else both("z", "p", 1))),
            "stp": ("c", [] if in_rows else both("y", "p", 1)),
            "cco": ("fz+ fz-", [("l", "c2", unit)] * in_columns + [("t", "t4", twin)]),
        }
        if in_rows:
            table["cro"] = ("fy+ fy-", [("l c", "r2", unit)])
        else:
            table["prp"] = ("py+ py-", both("y", "q", 0.5))
        if in_columns:
            table["ccp"] = ("c1 c2", [("t", "t3", 3 * twin)])
        else:
            table["pcp"] = ("pz+ pz-", both("z", "q", 0.5) + [("t", "t3", 2 * twin)])
            table["ccp"] = ("qz+ qz-", [("t", "t5", twin)])
        ends = "fy+ fy- t0 t1 t2 t3 t4 " + ("r1 r2" if in_rows else "qy+ qy-") + ("" if in_columns else " t5")
        table["done"] = (ends, [])
        for name, (waits, issues) in table.items():
            acts[name, part] = ([(key, part) for key in waits.split()], issues)
    now, free, arrival, order, ready_products = 0.0, {}, {}, [], []

    def issue(act):
        for links, key, length in acts.pop(act)[1]:
            end = 0.0
            for link in links.split():
                free[link] = max(now, free.get(link, 0.0)) + length
                end = max(end, free[link])
            arrival[key, act[1]] = end + latency

    for part in range(AHEAD):
        issue(("own", part))
    while acts or ready_products:
        for part in range(AHEAD, PARTS):
            if ("own", part) in acts and ("stp", part - AHEAD) not in acts:
                issue(("own", part))
                order.append(("own", part))
        known = []
        for act, (waits, _) in acts.items():
            if act[0] != "own" and all(key in arrival for key in waits):
                known.append((max(arrival[key] for key in waits), act))
        ready = [(act[1], rank.index(act[0]), act) for when, act in known if when <= now]
        if ready:
            act = min(ready)[2]
            issue(act)
            order.append(act)
            if act[0] == "done":
                ready_products += [(act[1], turn) for turn in range(FREQS // PARTS // UNROLL)]
        elif ready_products:
            part, turn = ready_products.pop(0)
            if order[-1][:2] == ("mul", part):
                order[-1] = ("mul", part, order[-1][2], turn + 1)
            else:
                order.append(("mul", part, turn, turn + 1))
            now += product
        else:
            now = min(when for when, _ in known)
    return order


def pairs_kernel(own_ref, inverse_ref, out_ref, left_ref, right_ref, cross, message, stage, send_sem, recv_sem, local_sem, out_send, out_recv):
    stn, seg = lax.axis_index("stn"), lax.axis_index("seg")
    core, z, x_lo = stn % 2, (stn // 2) % 4, stn // 8
    x_hi, y = seg % 2, seg // 2
    size = FREQS // PARTS
    half = size // 2

    def on_row(yy, hh):
        return (stn, (yy % 4) * 2 + hh)

    def on_column(zz, ll, cc):
        return ((ll * 4 + zz % 4) * 2 + cc, seg)

    def row_slot(yy, hh):
        return (yy % 4) * 2 + hh

    def column_slot(zz, ll, cc):
        return (ll * 4 + zz % 4) * 2 + cc

    across = (on_column(z, 1 - x_lo, core)[0], row_slot(y, 1 - x_hi))
    twin = on_column(z, x_lo, 1 - core)
    neighbours = [on_column(z + 1, x_lo, core), on_column(z + 3, x_lo, core), on_column(z, 1 - x_lo, core), twin, across]
    neighbours += [(stn, (seg + shift) % SEG) for shift in range(1, SEG)]
    barrier = pltpu.get_barrier_semaphore()
    for device in neighbours:
        pl.semaphore_signal(barrier, inc=1, device_id=device, device_id_type=MESH)
    pl.semaphore_wait(barrier, len(neighbours))

    started = []

    def send(kind, part, source, target, device):
        copy = pltpu.make_async_remote_copy(
            src_ref=source,
            dst_ref=target,
            send_sem=send_sem.at[part, kind],
            recv_sem=recv_sem.at[part, kind],
            device_id=device,
            device_id_type=MESH,
        )
        copy.start()
        started.append(copy)

    def arrive(kind, part, target):
        pltpu.make_async_remote_copy(
            src_ref=target,
            dst_ref=target,
            send_sem=send_sem.at[part, kind],
            recv_sem=recv_sem.at[part, kind],
            device_id=(stn, seg),
            device_id_type=MESH,
        ).wait_recv()

    def piece(ref, slot, part, which=None):
        first = part * size if which is None else part * size + which * half
        return ref.at[slot, pl.ds(first, size if which is None else half)]

    class Ring:
        def __init__(self, ref, slot, device, place, first):
            self.ref, self.slot, self.device, self.place, self.first = ref, slot, device, place, first

        def start(self, part, source, group, kind):
            slot = self.slot(self.place, group)
            for side, step in ((0, 1), (1, 3)):
                send(self.first + kind + side, part, source, piece(self.ref, slot, part), self.device(self.place + step))

        def pass_on(self, part, group, kind):
            for side, step in ((0, 3), (1, 1)):
                slot = self.slot(self.place + step, group)
                arrive(self.first + kind + side, part, piece(self.ref, slot, part))
                data = piece(self.ref, slot, part, side)
                send(self.first + kind + 2 + side, part, data, data, self.device(self.place + 4 - step))

        def finish(self, part, group, kind):
            slot = self.slot(self.place + 2, group)
            for side in (0, 1):
                arrive(self.first + kind + 2 + side, part, piece(self.ref, slot, part, side))

    rows = Ring(left_ref, row_slot, lambda yy: on_row(yy, x_hi), y, 0)
    columns = Ring(right_ref, lambda zz, ll: column_slot(zz, ll, core), lambda zz: on_column(zz, x_lo, core), z, 9)

    def share(kind, part, zz, ll):
        data = piece(right_ref, column_slot(zz, ll, core), part)
        send(kind, part, data, data, twin)

    beside = on_column(z, 1 - x_lo, core)

    def start_own(part):
        source = own_ref.at[pl.ds(part * size, size)]
        rows.start(part, source, x_hi, 0)
        columns.start(part, source, x_lo, 0)
        own_column = piece(right_ref, column_slot(z, x_lo, core), part)
        send(17, part, source, own_column, beside)
        send(18, part, source, own_column, twin)

    def forward(kind, part, ref, slot, device):
        data = piece(ref, slot, part)
        send(kind, part, data, data, device)

    def pass_rows(part):
        rows.pass_on(part, x_hi, 0)
        if part in ROWS_ALONG_X:
            for kind, step in ((4, 3), (5, 1)):
                forward(kind, part, left_ref, row_slot(y + step, x_hi), on_row(y, 1 - x_hi))

    def pass_columns(part):
        columns.pass_on(part, x_lo, 0)
        if part in COLUMNS_ALONG_X:
            for kind, step in ((13, 3), (14, 1)):
                forward(kind, part, right_ref, column_slot(z + step, x_lo, core), beside)
        share(19, part, z + 3, x_lo)
        share(20, part, z + 1, x_lo)

    def relay(part):
        data = piece(right_ref, column_slot(z, 1 - x_lo, core), part)
        arrive(17, part, data)
        send(8, part, data, piece(left_ref, row_slot(y, x_hi), part), across)
        if part not in COLUMNS_ALONG_X:
            columns.start(part, data, 1 - x_lo, 4)
        share(22, part, z, 1 - x_lo)

    def start_partner(part):
        data = piece(left_ref, row_slot(y, 1 - x_hi), part)
        arrive(8, part, data)
        if part not in ROWS_ALONG_X:
            rows.start(part, data, 1 - x_hi, 4)

    def pass_partner_rows(part):
        rows.pass_on(part, 1 - x_hi, 4)

    def pass_partner_columns(part):
        columns.pass_on(part, 1 - x_lo, 4)
        share(23, part, z + 3, 1 - x_lo)
        share(24, part, z + 1, 1 - x_lo)

    def end_rows(part):
        rows.finish(part, x_hi, 0)
        forward(6, part, left_ref, row_slot(y + 2, x_hi), on_row(y, 1 - x_hi))

    def end_columns(part):
        columns.finish(part, x_lo, 0)
        if part in COLUMNS_ALONG_X:
            forward(15, part, right_ref, column_slot(z + 2, x_lo, core), beside)
        share(21, part, z + 2, x_lo)

    def end_partner_columns(part):
        if part in COLUMNS_ALONG_X:
            for kind, share_kind, step in ((13, 23, 3), (14, 24, 1), (15, 25, 2)):
                arrive(kind, part, piece(right_ref, column_slot(z + step, 1 - x_lo, core), part))
                share(share_kind, part, z + step, 1 - x_lo)
        else:
            columns.finish(part, 1 - x_lo, 4)
            share(25, part, z + 2, 1 - x_lo)

    def complete(part):
        if part in ROWS_ALONG_X:
            for kind, step in ((4, 3), (5, 1), (6, 2)):
                arrive(kind, part, piece(left_ref, row_slot(y + step, 1 - x_hi), part))
        else:
            rows.finish(part, x_hi, 0)
            rows.finish(part, 1 - x_hi, 4)
        order = ((18, 0, x_lo), (19, 3, x_lo), (20, 1, x_lo), (21, 2, x_lo))
        order += ((22, 0, 1 - x_lo), (23, 3, 1 - x_lo), (24, 1, 1 - x_lo), (25, 2, 1 - x_lo))
        for kind, step, ll in order:
            arrive(kind, part, piece(right_ref, column_slot(z + step, ll, 1 - core), part))

    sign = jnp.where(lax.broadcasted_iota(jnp.int32, (LEFT, 128), 1) < HALF, -1.0, 1.0)

    def multiply(part, first, last):
        @pl.loop(first, last)
        def _(turn):
            for offset in range(UNROLL):
                index = part * size + turn * UNROLL + offset
                left = left_ref[:, index].astype(jnp.float32).reshape(LEFT, 128)
                right = right_ref[:, index].reshape(RIGHT, 128)
                turned = pltpu.roll(left, HALF, 1) * sign
                both = jnp.concatenate([left, turned], axis=0).astype(jnp.bfloat16)
                product = lax.dot_general(right, both, (((1,), (1,)), ((), ())), preferred_element_type=jnp.float32)
                cross[pl.ds(pl.multiple_of(index * PITCH, 8), RIGHT), :] = product

    actions = {
        "own": start_own,
        "pro": pass_rows,
        "pco": pass_columns,
        "rel": relay,
        "stp": start_partner,
        "prp": pass_partner_rows,
        "pcp": pass_partner_columns,
        "cro": end_rows,
        "cco": end_columns,
        "ccp": end_partner_columns,
        "done": complete,
    }
    for part in range(AHEAD):
        start_own(part)
    locals_ = []
    for index, target in enumerate((left_ref.at[row_slot(y, x_hi)], right_ref.at[column_slot(z, x_lo, core)])):
        copy = pltpu.make_async_copy(own_ref, target, local_sem.at[index])
        copy.start()
        locals_.append(copy)
    for name, part, *turns in transfer_order():
        if name == "mul":
            if locals_:
                locals_.pop().wait()
                locals_.pop().wait()
            multiply(part, *turns)
        else:
            actions[name](part)

    low_half = lax.broadcasted_iota(jnp.int32, (LAGPAD, 128), 1) < HALF

    def lagged(row):
        values = cross[pl.ds(row, FREQS, stride=PITCH), :].astype(jnp.bfloat16)
        parts = jnp.dot(inverse_ref[...], values, preferred_element_type=jnp.float32)
        parts = parts[: 2 * LAGPAD] + parts[2 * LAGPAD :]
        return parts[:LAGPAD], parts[LAGPAD:]

    def transform(group):
        for row in range(ROWS):
            first_re, first_im = lagged(group * (2 * ROWS) + row)
            second_re, second_im = lagged(group * (2 * ROWS) + ROWS + row)
            straight = jnp.where(low_half, first_re, second_im)
            crossed = jnp.where(low_half, second_re, first_im)
            stage[pl.ds(row, LAGPAD, stride=ROWS), :] = straight + pltpu.roll(crossed, HALF, 1)
        return stage[: LAGS * ROWS, :].reshape(LAGS, ROWS, 128).astype(jnp.bfloat16)

    def hand_over(shift):
        peer = (seg + shift) % SEG
        return pltpu.make_async_remote_copy(
            src_ref=message.at[peer],
            dst_ref=out_ref.at[seg],
            send_sem=out_send.at[shift],
            recv_sem=out_recv.at[shift],
            device_id=(stn, peer),
            device_id_type=MESH,
        )

    @pl.loop(1, SEG)
    def _(shift):
        group = (seg + shift) % SEG
        message[group] = transform(group)

        @pl.when(shift > 1)
        def _():
            hand_over(shift - 1).start()

    out_ref[seg] = transform(seg)
    hand_over(SEG - 1).start()
    for copy in started:
        copy.wait_send()
    for shift in range(1, SEG):
        slot = out_ref.at[(seg + SEG - shift) % SEG]
        pltpu.make_async_remote_copy(
            src_ref=slot,
            dst_ref=slot,
            send_sem=out_send.at[shift],
            recv_sem=out_recv.at[shift],
            device_id=(stn, seg),
            device_id_type=MESH,
        ).wait_recv()
        hand_over(shift).wait_send()


def pairs(own):
    result = (SEG, LAGS, ROWS, 128)
    return pl.pallas_call(
        pairs_kernel,
        out_shape=jax.ShapeDtypeStruct(result, jnp.bfloat16),
        in_specs=[VMEM, VMEM],
        out_specs=VMEM,
        scratch_shapes=[
            pltpu.VMEM((SEG,) + own.shape, jnp.bfloat16),
            pltpu.VMEM((STN,) + own.shape, jnp.bfloat16),
            pltpu.VMEM((FREQS * PITCH, 128), jnp.float32),
            pltpu.VMEM(result, jnp.bfloat16),
            pltpu.VMEM((LAGPAD * ROWS, 128), jnp.float32),
            pltpu.SemaphoreType.DMA((PARTS, 26)),
            pltpu.SemaphoreType.DMA((PARTS, 26)),
            pltpu.SemaphoreType.DMA((2,)),
            pltpu.SemaphoreType.DMA((SEG,)),
            pltpu.SemaphoreType.DMA((SEG,)),
        ],
        compiler_params=pltpu.CompilerParams(collective_id=0, has_side_effects=True, vmem_limit_bytes=56 << 20),
        name="pairs",
    )(own, jnp.asarray(inverse_matrix()))


def finish_kernel(values_ref, mask_ref, out_ref):
    keep = mask_ref[...].astype(jnp.float32)
    for lag in range(LAGS):
        turned = values_ref[:, lag].astype(jnp.float32).reshape(LEFT, 128).T
        out_ref[lag] = jnp.concatenate([turned[:LEFT], turned[LEFT:]], axis=1) * keep


def finish(values, pair_mask):
    return pl.pallas_call(
        finish_kernel,
        out_shape=jax.ShapeDtypeStruct((LAGS, LEFT, RIGHT), jnp.float32),
        in_specs=[VMEM, VMEM],
        out_specs=VMEM,
        name="finish",
    )(values, pair_mask)


def body(traces, fir_taps, seg_flags, pair_mask):
    own = spectrum(traces, fir_taps, seg_flags)
    return finish(pairs(own), pair_mask)


def solution(mesh):
    return jax.shard_map(
        body,
        mesh=mesh,
        in_specs=(P(("stn", "seg"), None), P(), P(("stn", "seg"), None), P("stn", "seg")),
        out_specs=P(None, "stn", "seg"),
        check_vma=False,
    )
```

```python
import functools
import math

import jax
import jax.numpy as jnp
import numpy as np
from jax import lax
from jax.experimental import pallas as pl
from jax.experimental.pallas import tpu as pltpu
from jax.sharding import PartitionSpec as P

SAMP = 600
LAGS = 41
TAPS = 31
RADIUS = 64
SEGS = 64
ROWS = 8
EPS = 1e-06

LENGTH = 624
PADDED = 640
FREQS = LENGTH // 2
HALF = SEGS
FBLOCK = 104
FBLOCKS = FREQS // FBLOCK
LAGPAD = 48
PITCH = 136

RECORD = SEGS * SAMP
BLOCKS = RECORD // 128
PER = 60
SEGPITCH = SEGS + 8

STN, SEG = 16, 8
LEFT = ROWS * SEG
RIGHT = ROWS * STN
PARTS = 6

EARLY_PARTS = 2
EARLY = EARLY_PARTS * FREQS // PARTS

MESH = pl.DeviceIdType.MESH
VMEM = pl.BlockSpec(memory_space=pltpu.VMEM)
HBM = pl.BlockSpec(memory_space=pltpu.HBM)


def split_bf16(values):
    high = np.asarray(values, np.float32).astype(jnp.bfloat16)
    low = (np.asarray(values, np.float64) - high.astype(np.float64)).astype(np.float32).astype(jnp.bfloat16)
    return high, low


def frequencies():
    return (np.arange(FREQS) + 0.5) * (2 * np.pi / LENGTH)


def forward_matrix():
    angle = frequencies()[:, None] * np.arange(PADDED)[None, :]
    keep = (np.arange(PADDED) < SAMP)[None, :]
    (re_hi, re_lo), (im_hi, im_lo) = [split_bf16(part * keep) for part in (np.cos(angle), -np.sin(angle))]
    stacked = np.stack([re_hi, im_hi, re_lo, im_lo])
    stacked = stacked.reshape(4, FBLOCKS, FBLOCK, PADDED).transpose(1, 0, 2, 3)
    return np.ascontiguousarray(stacked.reshape(FBLOCKS, 4 * FBLOCK, PADDED))


def inverse_matrix():
    lag = np.arange(LAGS) - (LAGS - 1) // 2
    angle = lag[:, None] * frequencies()[None, :]
    padded = np.zeros((2, LAGPAD, FREQS))
    padded[0, :LAGS] = np.cos(angle)
    padded[1, :LAGS] = -np.sin(angle)
    padded *= 2.0 / LENGTH / math.sqrt(RECORD)
    whole = np.concatenate(split_bf16(padded.reshape(2 * LAGPAD, FREQS)), axis=0)
    return [np.ascontiguousarray(piece) for piece in np.split(whole, [EARLY], axis=1)]


def whiten(taps_ref, flags_ref, padded, filtered, whitened, rows, ready):
    edge = jnp.zeros((ROWS, 128), jnp.float32)
    padded[:, 0:128] = edge
    padded[:, 128 + RECORD : 256 + RECORD] = edge
    filtered[:, 0:128] = edge
    filtered[:, 128 + RECORD : 256 + RECORD] = edge
    whitened[:, RECORD : RECORD + 128] = edge

    offset = lax.broadcasted_iota(jnp.int32, (384, 128), 0) - lax.broadcasted_iota(jnp.int32, (384, 128), 1)
    band = jnp.zeros((384, 128), jnp.float32)
    for tap in range(TAPS):
        band = jnp.where(offset == 128 - (TAPS - 1) // 2 + tap, taps_ref[tap], band)
    band_high = band.astype(jnp.bfloat16)
    band_low = (band - band_high.astype(jnp.float32)).astype(jnp.bfloat16)
    box = jnp.where((offset >= 128 - RADIUS) & (offset <= 128 + RADIUS), 1.0, 0.0).astype(jnp.bfloat16)

    def windows(ref, start):
        window = ref[:, pl.ds(start, (PER + 2) * 128)]
        tiles = [window[:, 128 * i : 128 * i + 128] for i in range(PER + 2)]
        stacked = [jnp.concatenate(tiles[i : i + PER], axis=0) for i in range(3)]
        return jnp.concatenate(stacked, axis=1)

    def halves(values):
        high = values.astype(jnp.bfloat16)
        return high, (values - high.astype(jnp.float32)).astype(jnp.bfloat16)

    def product(left, right):
        return jnp.dot(left, right, preferred_element_type=jnp.float32)

    def place(ref, start, values):
        for i in range(PER):
            ref[:, pl.ds(pl.multiple_of(start + 128 * i, 128), 128)] = values[ROWS * i : ROWS * (i + 1)]

    ready()

    @pl.loop(0, BLOCKS // PER)
    def _(chunk):
        start = pl.multiple_of(chunk * (PER * 128), 128)
        high, low = halves(windows(padded, start))
        total = product(high, band_high) + (product(low, band_high) + product(high, band_low))
        place(filtered, start + 128, total)

    @pl.loop(0, BLOCKS // PER)
    def _(chunk):
        start = pl.multiple_of(chunk * (PER * 128), 128)
        values = windows(filtered, start)
        high, low = halves(jnp.abs(values))
        level = (product(high, box) + product(low, box)) / (2 * RADIUS + 1)
        place(whitened, start, values[:, 128:256] / (level + EPS))

    flags = flags_ref[...].astype(jnp.float32)
    for seg in range(SEGS):
        piece = whitened[:, seg * SAMP : seg * SAMP + PADDED] * flags[:, seg : seg + 1]
        for part in range(PADDED // 128):
            rows[part, pl.ds(seg, ROWS, stride=SEGPITCH), :] = piece[:, part * 128 : part * 128 + 128]


def gathered_samples(rows):
    columns = []
    for part in range(PADDED // 128):
        pieces = [rows[part, SEGPITCH * row : SEGPITCH * row + SEGS, :] for row in range(ROWS)]
        columns.append(jnp.concatenate(pieces, axis=0))
    return jnp.concatenate(columns, axis=1).astype(jnp.bfloat16)


def spectrum(step, forward, samples, block, own):
    low_half = lax.broadcasted_iota(jnp.int32, (FBLOCK, 128), 1) < HALF
    both = lax.dot_general(forward[step], samples, (((1,), (1,)), ((), ())), preferred_element_type=jnp.float32)
    both = both[: 2 * FBLOCK] + both[2 * FBLOCK :]
    for pair in range(ROWS // 2):
        real = both[:FBLOCK, pair * 128 : pair * 128 + 128]
        imag = both[FBLOCK:, pair * 128 : pair * 128 + 128]
        even = jnp.where(low_half, real, pltpu.roll(imag, HALF, 1))
        odd = jnp.where(low_half, pltpu.roll(real, HALF, 1), imag)
        block[pl.ds(2 * pair, FBLOCK, stride=ROWS), :] = even
        block[pl.ds(2 * pair + 1, FBLOCK, stride=ROWS), :] = odd
    own[pl.ds(step * FBLOCK, FBLOCK)] = block[...].reshape(FBLOCK, ROWS, 128).astype(jnp.bfloat16)


UNROLL = 13

ROWS_ALONG_X = (2,)
COLUMNS_ALONG_X = (1, 4)
AHEAD = 3


def transfer_order():
    unit, latency, twin = 15.2 / PARTS, 1.6, 3.0 / PARTS
    product, transform, turns = 12.7 * UNROLL / FREQS, 0.6, FREQS // PARTS // UNROLL
    rank = ("own", "rel", "stp", "pro", "pco", "prp", "pcp", "cro", "cco", "ccp", "done")
    acts = {}
    for part in range(PARTS):
        in_rows, in_columns = part in ROWS_ALONG_X, part in COLUMNS_ALONG_X

        def both(axis, stage, share):
            return [(link, stage + link, share * unit) for link in (axis + "+", axis + "-")]

        table = {
            "own": ("", both("y", "o", 1) + both("z", "o", 1) + [("l", "l", unit), ("t", "t0", twin)]),
            "pro": ("oy+ oy-", both("y", "f", 0.5) + [("l c", "r1", 2 * unit)] * in_rows),
            "pco": ("oz+ oz-", both("z", "f", 0.5) + [("l", "c1", 2 * unit)] * in_columns + [("t", "t1", 2 * twin)]),
            "rel": ("l", [("c", "c", unit), ("t", "t2", twin)] + ([] if in_columns else both("z", "p", 1))),
            "stp": ("c", [] if in_rows else both("y", "p", 1)),
            "cco": ("fz+ fz-", [("l", "c2", unit)] * in_columns + [("t", "t4", twin)]),
        }
        if in_rows:
            table["cro"] = ("fy+ fy-", [("l c", "r2", unit)])
        else:
            table["prp"] = ("py+ py-", both("y", "q", 0.5))
        if in_columns:
            table["ccp"] = ("c1 c2", [("t", "t3", 3 * twin)])
        else:
            table["pcp"] = ("pz+ pz-", both("z", "q", 0.5) + [("t", "t3", 2 * twin)])
            table["ccp"] = ("qz+ qz-", [("t", "t5", twin)])
        ends = "fy+ fy- t0 t1 t2 t3 t4 " + ("r1 r2" if in_rows else "qy+ qy-") + ("" if in_columns else " t5")
        table["done"] = (ends, [])
        for name, (waits, issues) in table.items():
            acts[name, part] = ([(key, part) for key in waits.split()], issues)
    now, free, arrival, order, ready_products, early = 0.0, {}, {}, [], [], []

    def issue(act):
        for links, key, length in acts.pop(act)[1]:
            end = 0.0
            for link in links.split():
                free[link] = max(now, free.get(link, 0.0)) + length
                end = max(end, free[link])
            arrival[key, act[1]] = end + latency

    for part in range(AHEAD):
        issue(("own", part))
    while acts or ready_products or early:
        for part in range(AHEAD, PARTS):
            if ("own", part) in acts and ("stp", part - AHEAD) not in acts:
                issue(("own", part))
                order.append(("own", part))
        known = []
        for act, (waits, _) in acts.items():
            if act[0] != "own" and all(key in arrival for key in waits):
                known.append((max(arrival[key] for key in waits), act))
        ready = [(act[1], rank.index(act[0]), act) for when, act in known if when <= now]
        if ready:
            act = min(ready)[2]
            issue(act)
            order.append(act)
            if act[0] == "done":
                ready_products += [(act[1], turn) for turn in range(turns)]
        elif ready_products:
            part, turn = ready_products.pop(0)
            if order[-1][:2] == ("mul", part):
                order[-1] = ("mul", part, order[-1][2], turn + 1)
            else:
                order.append(("mul", part, turn, turn + 1))
            now += product
            if (part, turn) == (EARLY_PARTS - 1, turns - 1):
                early = list(range(SEG))
        elif early:
            group = early.pop(0)
            if order[-1][0] == "inv":
                order[-1] = ("inv", 0, order[-1][2], group + 1)
            else:
                order.append(("inv", 0, group, group + 1))
            now += transform
        else:
            now = min(when for when, _ in known)
    return order


def pairs_kernel(
    taps_ref, flags_hbm, traces_hbm, forward_hbm, early_hbm, late_hbm, out_ref, flags_ref, forward, early_ref, late_ref,
    padded, filtered, whitened, rows_ref, block, own_ref, left_ref, right_ref, cross, message, stage, early_sum,
    send_sem, recv_sem, local_sem, out_send, out_recv,
):
    loads = ((traces_hbm, padded.at[:, pl.ds(128, RECORD)]), (flags_hbm, flags_ref), (forward_hbm, forward))
    loads += ((early_hbm, early_ref), (late_hbm, late_ref))
    loads = [pltpu.make_async_copy(*pair, local_sem.at[2 + index]) for index, pair in enumerate(loads)]
    for copy in loads:
        copy.start()
    stn, seg = lax.axis_index("stn"), lax.axis_index("seg")
    core, z, x_lo = stn % 2, (stn // 2) % 4, stn // 8
    x_hi, y = seg % 2, seg // 2
    size = FREQS // PARTS
    half = size // 2

    def on_row(yy, hh):
        return (stn, (yy % 4) * 2 + hh)

    def on_column(zz, ll, cc):
        return ((ll * 4 + zz % 4) * 2 + cc, seg)

    def row_slot(yy, hh):
        return (yy % 4) * 2 + hh

    def column_slot(zz, ll, cc):
        return (ll * 4 + zz % 4) * 2 + cc

    across = (on_column(z, 1 - x_lo, core)[0], row_slot(y, 1 - x_hi))
    twin = on_column(z, x_lo, 1 - core)
    neighbours = [on_column(z + 1, x_lo, core), on_column(z + 3, x_lo, core), on_column(z, 1 - x_lo, core), twin, across]
    neighbours += [(stn, (seg + shift) % SEG) for shift in range(1, SEG)]
    barrier = pltpu.get_barrier_semaphore()
    for device in neighbours:
        pl.semaphore_signal(barrier, inc=1, device_id=device, device_id_type=MESH)

    def ready():
        loads[0].wait()
        loads[1].wait()

    whiten(taps_ref, flags_ref, padded, filtered, whitened, rows_ref, ready)
    samples = gathered_samples(rows_ref)
    loads[2].wait()
    spectrum(0, forward, samples, block, own_ref)
    pl.semaphore_wait(barrier, len(neighbours))

    started = []

    def send(kind, part, source, target, device):
        copy = pltpu.make_async_remote_copy(
            src_ref=source,
            dst_ref=target,
            send_sem=send_sem.at[part, kind],
            recv_sem=recv_sem.at[part, kind],
            device_id=device,
            device_id_type=MESH,
        )
        copy.start()
        started.append(copy)

    def arrive(kind, part, target):
        pltpu.make_async_remote_copy(
            src_ref=target,
            dst_ref=target,
            send_sem=send_sem.at[part, kind],
            recv_sem=recv_sem.at[part, kind],
            device_id=(stn, seg),
            device_id_type=MESH,
        ).wait_recv()

    def piece(ref, slot, part, which=None):
        first = part * size if which is None else part * size + which * half
        return ref.at[slot, pl.ds(first, size if which is None else half)]

    class Ring:
        def __init__(self, ref, slot, device, place, first):
            self.ref, self.slot, self.device, self.place, self.first = ref, slot, device, place, first

        def start(self, part, source, group, kind):
            slot = self.slot(self.place, group)
            for side, step in ((0, 1), (1, 3)):
                send(self.first + kind + side, part, source, piece(self.ref, slot, part), self.device(self.place + step))

        def pass_on(self, part, group, kind):
            for side, step in ((0, 3), (1, 1)):
                slot = self.slot(self.place + step, group)
                arrive(self.first + kind + side, part, piece(self.ref, slot, part))
                data = piece(self.ref, slot, part, side)
                send(self.first + kind + 2 + side, part, data, data, self.device(self.place + 4 - step))

        def finish(self, part, group, kind):
            slot = self.slot(self.place + 2, group)
            for side in (0, 1):
                arrive(self.first + kind + 2 + side, part, piece(self.ref, slot, part, side))

    rows = Ring(left_ref, row_slot, lambda yy: on_row(yy, x_hi), y, 0)
    columns = Ring(right_ref, lambda zz, ll: column_slot(zz, ll, core), lambda zz: on_column(zz, x_lo, core), z, 9)

    def share(kind, part, zz, ll):
        data = piece(right_ref, column_slot(zz, ll, core), part)
        send(kind, part, data, data, twin)

    beside = on_column(z, 1 - x_lo, core)

    def start_own(part):
        source = own_ref.at[pl.ds(part * size, size)]
        rows.start(part, source, x_hi, 0)
        columns.start(part, source, x_lo, 0)
        own_column = piece(right_ref, column_slot(z, x_lo, core), part)
        send(17, part, source, own_column, beside)
        send(18, part, source, own_column, twin)

    def pass_along(kind, part, ref, slot, device):
        data = piece(ref, slot, part)
        send(kind, part, data, data, device)

    def pass_rows(part):
        rows.pass_on(part, x_hi, 0)
        if part in ROWS_ALONG_X:
            for kind, step in ((4, 3), (5, 1)):
                pass_along(kind, part, left_ref, row_slot(y + step, x_hi), on_row(y, 1 - x_hi))

    def pass_columns(part):
        columns.pass_on(part, x_lo, 0)
        if part in COLUMNS_ALONG_X:
            for kind, step in ((13, 3), (14, 1)):
                pass_along(kind, part, right_ref, column_slot(z + step, x_lo, core), beside)
        share(19, part, z + 3, x_lo)
        share(20, part, z + 1, x_lo)

    def relay(part):
        data = piece(right_ref, column_slot(z, 1 - x_lo, core), part)
        arrive(17, part, data)
        send(8, part, data, piece(left_ref, row_slot(y, x_hi), part), across)
        if part not in COLUMNS_ALONG_X:
            columns.start(part, data, 1 - x_lo, 4)
        share(22, part, z, 1 - x_lo)

    def start_partner(part):
        data = piece(left_ref, row_slot(y, 1 - x_hi), part)
        arrive(8, part, data)
        if part not in ROWS_ALONG_X:
            rows.start(part, data, 1 - x_hi, 4)

    def pass_partner_rows(part):
        rows.pass_on(part, 1 - x_hi, 4)

    def pass_partner_columns(part):
        columns.pass_on(part, 1 - x_lo, 4)
        share(23, part, z + 3, 1 - x_lo)
        share(24, part, z + 1, 1 - x_lo)

    def end_rows(part):
        rows.finish(part, x_hi, 0)
        pass_along(6, part, left_ref, row_slot(y + 2, x_hi), on_row(y, 1 - x_hi))

    def end_columns(part):
        columns.finish(part, x_lo, 0)
        if part in COLUMNS_ALONG_X:
            pass_along(15, part, right_ref, column_slot(z + 2, x_lo, core), beside)
        share(21, part, z + 2, x_lo)

    def end_partner_columns(part):
        if part in COLUMNS_ALONG_X:
            for kind, share_kind, step in ((13, 23, 3), (14, 24, 1), (15, 25, 2)):
                arrive(kind, part, piece(right_ref, column_slot(z + step, 1 - x_lo, core), part))
                share(share_kind, part, z + step, 1 - x_lo)
        else:
            columns.finish(part, 1 - x_lo, 4)
            share(25, part, z + 2, 1 - x_lo)

    def complete(part):
        if part in ROWS_ALONG_X:
            for kind, step in ((4, 3), (5, 1), (6, 2)):
                arrive(kind, part, piece(left_ref, row_slot(y + step, 1 - x_hi), part))
        else:
            rows.finish(part, x_hi, 0)
            rows.finish(part, 1 - x_hi, 4)
        order = ((18, 0, x_lo), (19, 3, x_lo), (20, 1, x_lo), (21, 2, x_lo))
        order += ((22, 0, 1 - x_lo), (23, 3, 1 - x_lo), (24, 1, 1 - x_lo), (25, 2, 1 - x_lo))
        for kind, step, ll in order:
            arrive(kind, part, piece(right_ref, column_slot(z + step, ll, 1 - core), part))

    sign = jnp.where(lax.broadcasted_iota(jnp.int32, (LEFT, 128), 1) < HALF, -1.0, 1.0)

    def multiply(part, first, last):
        @pl.loop(first, last)
        def _(turn):
            for offset in range(UNROLL):
                index = part * size + turn * UNROLL + offset
                left = left_ref[:, index].astype(jnp.float32).reshape(LEFT, 128)
                right = right_ref[:, index].reshape(RIGHT, 128)
                turned = pltpu.roll(left, HALF, 1) * sign
                both = jnp.concatenate([left, turned], axis=0).astype(jnp.bfloat16)
                product = lax.dot_general(right, both, (((1,), (1,)), ((), ())), preferred_element_type=jnp.float32)
                cross[pl.ds(pl.multiple_of(index * PITCH, 8), RIGHT), :] = product

    low_half = lax.broadcasted_iota(jnp.int32, (LAGPAD, 128), 1) < HALF

    def inverse(group, matrix_ref, first, last, into):
        def lagged(row):
            values = cross[pl.ds(first * PITCH + row, last - first, stride=PITCH), :].astype(jnp.bfloat16)
            parts = jnp.dot(matrix_ref[...], values, preferred_element_type=jnp.float32)
            parts = parts[: 2 * LAGPAD] + parts[2 * LAGPAD :]
            return parts[:LAGPAD], parts[LAGPAD:]

        for row in range(ROWS):
            first_re, first_im = lagged(group * (2 * ROWS) + row)
            second_re, second_im = lagged(group * (2 * ROWS) + ROWS + row)
            straight = jnp.where(low_half, first_re, second_im)
            crossed = jnp.where(low_half, second_re, first_im)
            into[pl.ds(row, LAGPAD, stride=ROWS), :] = straight + pltpu.roll(crossed, HALF, 1)

    def transform_early(first, last):
        @pl.loop(first, last)
        def _(group):
            inverse(group, early_ref, 0, EARLY, early_sum.at[group])

    actions = {
        "own": start_own,
        "pro": pass_rows,
        "pco": pass_columns,
        "rel": relay,
        "stp": start_partner,
        "prp": pass_partner_rows,
        "pcp": pass_partner_columns,
        "cro": end_rows,
        "cco": end_columns,
        "ccp": end_partner_columns,
        "done": complete,
    }
    per = PARTS // FBLOCKS
    for step in range(FBLOCKS):
        for part in range(step * per, min(step * per + per, AHEAD)):
            start_own(part)
        if step + 1 < FBLOCKS:
            spectrum(step + 1, forward, samples, block, own_ref)
    loads[3].wait()
    loads[4].wait()
    locals_ = []
    for index, target in enumerate((left_ref.at[row_slot(y, x_hi)], right_ref.at[column_slot(z, x_lo, core)])):
        copy = pltpu.make_async_copy(own_ref, target, local_sem.at[index])
        copy.start()
        locals_.append(copy)
    for name, part, *turns in transfer_order():
        if name == "mul":
            if locals_:
                locals_.pop().wait()
                locals_.pop().wait()
            multiply(part, *turns)
        elif name == "inv":
            transform_early(*turns)
        else:
            actions[name](part)

    def hand_over(shift):
        peer = (seg + shift) % SEG
        return pltpu.make_async_remote_copy(
            src_ref=message.at[peer],
            dst_ref=out_ref.at[seg],
            send_sem=out_send.at[shift],
            recv_sem=out_recv.at[shift],
            device_id=(stn, peer),
            device_id_type=MESH,
        )

    def transform(group):
        inverse(group, late_ref, EARLY, FREQS, stage)
        both = stage[: LAGS * ROWS, :] + early_sum[group, : LAGS * ROWS, :]
        return both.reshape(LAGS, ROWS, 128).astype(jnp.bfloat16)

    @pl.loop(1, SEG)
    def _(shift):
        group = (seg + shift) % SEG
        message[group] = transform(group)

        @pl.when(shift > 1)
        def _():
            hand_over(shift - 1).start()

    out_ref[seg] = transform(seg)
    hand_over(SEG - 1).start()
    for copy in started:
        copy.wait_send()
    for shift in range(1, SEG):
        slot = out_ref.at[(seg + SEG - shift) % SEG]
        pltpu.make_async_remote_copy(
            src_ref=slot,
            dst_ref=slot,
            send_sem=out_send.at[shift],
            recv_sem=out_recv.at[shift],
            device_id=(stn, seg),
            device_id_type=MESH,
        ).wait_recv()
        hand_over(shift).wait_send()


def pairs(traces, fir_taps, seg_flags):
    result = (SEG, LAGS, ROWS, 128)
    spectra = (FREQS, ROWS, 128)
    forward = forward_matrix()
    early, late = inverse_matrix()
    return pl.pallas_call(
        pairs_kernel,
        out_shape=jax.ShapeDtypeStruct(result, jnp.bfloat16),
        in_specs=[pl.BlockSpec(memory_space=pltpu.SMEM), HBM, HBM, HBM, HBM, HBM],
        out_specs=VMEM,
        scratch_shapes=[
            pltpu.VMEM((ROWS, SEGS), jnp.int32),
            pltpu.VMEM(forward.shape, jnp.bfloat16),
            pltpu.VMEM(early.shape, jnp.bfloat16),
            pltpu.VMEM(late.shape, jnp.bfloat16),
            pltpu.VMEM((ROWS, RECORD + 256), jnp.float32),
            pltpu.VMEM((ROWS, RECORD + 256), jnp.float32),
            pltpu.VMEM((ROWS, RECORD + 128), jnp.float32),
            pltpu.VMEM((PADDED // 128, ROWS * SEGPITCH, 128), jnp.float32),
            pltpu.VMEM((FBLOCK * ROWS, 128), jnp.float32),
            pltpu.VMEM(spectra, jnp.bfloat16),
            pltpu.VMEM((SEG,) + spectra, jnp.bfloat16),
            pltpu.VMEM((STN,) + spectra, jnp.bfloat16),
            pltpu.VMEM((FREQS * PITCH, 128), jnp.float32),
            pltpu.VMEM(result, jnp.bfloat16),
            pltpu.VMEM((LAGPAD * ROWS, 128), jnp.float32),
            pltpu.VMEM((SEG, LAGPAD * ROWS, 128), jnp.float32),
            pltpu.SemaphoreType.DMA((PARTS, 26)),
            pltpu.SemaphoreType.DMA((PARTS, 26)),
            pltpu.SemaphoreType.DMA((7,)),
            pltpu.SemaphoreType.DMA((SEG,)),
            pltpu.SemaphoreType.DMA((SEG,)),
        ],
        compiler_params=pltpu.CompilerParams(collective_id=0, has_side_effects=True, vmem_limit_bytes=60 << 20),
        name="pairs",
    )(fir_taps, seg_flags, traces, jnp.asarray(forward), jnp.asarray(early), jnp.asarray(late))


def finish_kernel(values_ref, mask_ref, out_ref):
    keep = mask_ref[...].astype(jnp.float32)
    for lag in range(LAGS):
        turned = values_ref[:, lag].astype(jnp.float32).reshape(LEFT, 128).T
        out_ref[lag] = jnp.concatenate([turned[:LEFT], turned[LEFT:]], axis=1) * keep


def finish(values, pair_mask):
    return pl.pallas_call(
        finish_kernel,
        out_shape=jax.ShapeDtypeStruct((LAGS, LEFT, RIGHT), jnp.float32),
        in_specs=[VMEM, VMEM],
        out_specs=VMEM,
        name="finish",
    )(values, pair_mask)


def body(traces, fir_taps, seg_flags, pair_mask):
    return finish(pairs(traces, fir_taps, seg_flags), pair_mask)


def solution(mesh):
    return jax.shard_map(
        body,
        mesh=mesh,
        in_specs=(P(("stn", "seg"), None), P(), P(("stn", "seg"), None), P("stn", "seg")),
        out_specs=P(None, "stn", "seg"),
        check_vma=False,
    )
```

```python
import functools
import math

import jax
import jax.numpy as jnp
import numpy as np
from jax import lax
from jax.experimental import pallas as pl
from jax.experimental.pallas import tpu as pltpu
from jax.sharding import PartitionSpec as P

SAMP = 600
LAGS = 41
TAPS = 31
RADIUS = 64
SEGS = 64
ROWS = 8
EPS = 1e-06

LENGTH = 624
PADDED = 640
FREQS = LENGTH // 2
HALF = SEGS
FBLOCK = 104
FBLOCKS = FREQS // FBLOCK
LAGPAD = 48
PITCH = 136

RECORD = SEGS * SAMP
BLOCKS = RECORD // 128
PER = 100
SEGPITCH = SEGS + 8

STN, SEG = 16, 8
LEFT = ROWS * SEG
RIGHT = ROWS * STN
PARTS = 6

EARLY_PARTS = 2
EARLY = EARLY_PARTS * FREQS // PARTS

MESH = pl.DeviceIdType.MESH
VMEM = pl.BlockSpec(memory_space=pltpu.VMEM)
HBM = pl.BlockSpec(memory_space=pltpu.HBM)


def split_bf16(values):
    high = np.asarray(values, np.float32).astype(jnp.bfloat16)
    low = (np.asarray(values, np.float64) - high.astype(np.float64)).astype(np.float32).astype(jnp.bfloat16)
    return high, low


def frequencies():
    return (np.arange(FREQS) + 0.5) * (2 * np.pi / LENGTH)


def forward_matrix():
    angle = frequencies()[:, None] * np.arange(PADDED)[None, :]
    keep = (np.arange(PADDED) < SAMP)[None, :]
    (re_hi, re_lo), (im_hi, im_lo) = [split_bf16(part * keep) for part in (np.cos(angle), -np.sin(angle))]
    stacked = np.stack([re_hi, im_hi, re_lo, im_lo])
    stacked = stacked.reshape(4, FBLOCKS, FBLOCK, PADDED).transpose(1, 0, 2, 3)
    return np.ascontiguousarray(stacked.reshape(FBLOCKS, 4 * FBLOCK, PADDED))


def inverse_matrix():
    lag = np.arange(LAGS) - (LAGS - 1) // 2
    angle = lag[:, None] * frequencies()[None, :]
    padded = np.zeros((2, LAGPAD, FREQS))
    padded[0, :LAGS] = np.cos(angle)
    padded[1, :LAGS] = -np.sin(angle)
    padded *= 2.0 / LENGTH / math.sqrt(RECORD)
    whole = np.concatenate(split_bf16(padded.reshape(2 * LAGPAD, FREQS)), axis=0)
    return [np.ascontiguousarray(piece) for piece in np.split(whole, [EARLY], axis=1)]


def whiten(taps_ref, flags_ref, padded, filtered, whitened, rows, ready):
    edge = jnp.zeros((ROWS, 128), jnp.float32)
    padded[:, 0:128] = edge
    padded[:, 128 + RECORD : 256 + RECORD] = edge
    filtered[:, 0:128] = edge
    filtered[:, 128 + RECORD : 256 + RECORD] = edge
    whitened[:, RECORD : RECORD + 128] = edge

    offset = lax.broadcasted_iota(jnp.int32, (384, 128), 0) - lax.broadcasted_iota(jnp.int32, (384, 128), 1)
    band = jnp.zeros((384, 128), jnp.float32)
    for tap in range(TAPS):
        band = jnp.where(offset == 128 - (TAPS - 1) // 2 + tap, taps_ref[tap], band)
    band_high = band.astype(jnp.bfloat16)
    band_low = (band - band_high.astype(jnp.float32)).astype(jnp.bfloat16)
    box = jnp.where((offset >= 128 - RADIUS) & (offset <= 128 + RADIUS), 1.0, 0.0).astype(jnp.bfloat16)

    def windows(ref, start):
        window = ref[:, pl.ds(start, (PER + 2) * 128)]
        tiles = [window[:, 128 * i : 128 * i + 128] for i in range(PER + 2)]
        stacked = [jnp.concatenate(tiles[i : i + PER], axis=0) for i in range(3)]
        return jnp.concatenate(stacked, axis=1)

    def halves(values):
        high = values.astype(jnp.bfloat16)
        return high, (values - high.astype(jnp.float32)).astype(jnp.bfloat16)

    def product(left, right):
        return jnp.dot(left, right, preferred_element_type=jnp.float32)

    def place(ref, start, values):
        for i in range(PER):
            ref[:, pl.ds(pl.multiple_of(start + 128 * i, 128), 128)] = values[ROWS * i : ROWS * (i + 1)]

    ready()

    @pl.loop(0, BLOCKS // PER)
    def _(chunk):
        start = pl.multiple_of(chunk * (PER * 128), 128)
        high, low = halves(windows(padded, start))
        total = product(high, band_high) + (product(low, band_high) + product(high, band_low))
        place(filtered, start + 128, total)

    @pl.loop(0, BLOCKS // PER)
    def _(chunk):
        start = pl.multiple_of(chunk * (PER * 128), 128)
        values = windows(filtered, start)
        high, low = halves(jnp.abs(values))
        level = (product(high, box) + product(low, box)) / (2 * RADIUS + 1)
        place(whitened, start, values[:, 128:256] / (level + EPS))

    flags = flags_ref[...].astype(jnp.float32)
    for seg in range(SEGS):
        piece = whitened[:, seg * SAMP : seg * SAMP + PADDED] * flags[:, seg : seg + 1]
        for part in range(PADDED // 128):
            rows[part, pl.ds(seg, ROWS, stride=SEGPITCH), :] = piece[:, part * 128 : part * 128 + 128]


def gathered_samples(rows):
    columns = []
    for part in range(PADDED // 128):
        pieces = [rows[part, SEGPITCH * row : SEGPITCH * row + SEGS, :] for row in range(ROWS)]
        columns.append(jnp.concatenate(pieces, axis=0))
    return jnp.concatenate(columns, axis=1).astype(jnp.bfloat16)


def spectrum(step, forward, samples, block, own):
    low_half = lax.broadcasted_iota(jnp.int32, (FBLOCK, 128), 1) < HALF
    both = lax.dot_general(forward[step], samples, (((1,), (1,)), ((), ())), preferred_element_type=jnp.float32)
    both = both[: 2 * FBLOCK] + both[2 * FBLOCK :]
    for pair in range(ROWS // 2):
        real = both[:FBLOCK, pair * 128 : pair * 128 + 128]
        imag = both[FBLOCK:, pair * 128 : pair * 128 + 128]
        even = jnp.where(low_half, real, pltpu.roll(imag, HALF, 1))
        odd = jnp.where(low_half, pltpu.roll(real, HALF, 1), imag)
        block[pl.ds(2 * pair, FBLOCK, stride=ROWS), :] = even
        block[pl.ds(2 * pair + 1, FBLOCK, stride=ROWS), :] = odd
    own[pl.ds(step * FBLOCK, FBLOCK)] = block[...].reshape(FBLOCK, ROWS, 128).astype(jnp.bfloat16)


UNROLL = 13

ROWS_ALONG_X = (2,)
COLUMNS_ALONG_X = (1, 4)
SLACK = 2.5
LATER = 2


def transfer_order():
    unit, latency, twin = 15.7 / PARTS, 2.5, 4.0 / PARTS
    product, transform, turns = 12.7 * UNROLL / FREQS, 0.25 + 0.55 * EARLY_PARTS / PARTS, FREQS // PARTS // UNROLL
    rank = ("rel", "stp", "pro", "pco", "prp", "pcp", "cro", "cco", "ccp", "done")
    links_of = {"owx": "l", "owy": "y+", "owz": "z+"}
    acts = {}
    for part in range(PARTS):
        in_rows, in_columns = part in ROWS_ALONG_X, part in COLUMNS_ALONG_X

        def both(axis, stage, share):
            return [(link, stage + link, share * unit) for link in (axis + "+", axis + "-")]

        table = {
            "owx": ("", [("l", "l", unit), ("t", "t0", twin)]),
            "owy": ("", both("y", "o", 1)),
            "owz": ("", both("z", "o", 1)),
            "pro": ("oy+ oy-", both("y", "f", 0.5) + [("l c", "r1", 2 * unit)] * in_rows),
            "pco": ("oz+ oz-", both("z", "f", 0.5) + [("l", "c1", 2 * unit)] * in_columns + [("t", "t1", 2 * twin)]),
            "rel": ("l", [("c", "c", unit), ("t", "t2", twin)] + ([] if in_columns else both("z", "p", 1))),
            "stp": ("c", [] if in_rows else both("y", "p", 1)),
            "cco": ("fz+ fz-", [("l", "c2", unit)] * in_columns + [("t", "t4", twin)]),
        }
        if in_rows:
            table["cro"] = ("fy+ fy-", [("l c", "r2", unit)])
        else:
            table["prp"] = ("py+ py-", both("y", "q", 0.5))
        if in_columns:
            table["ccp"] = ("c1 c2", [("t", "t3", 3 * twin)])
        else:
            table["pcp"] = ("pz+ pz-", both("z", "q", 0.5) + [("t", "t3", 2 * twin)])
            table["ccp"] = ("qz+ qz-", [("t", "t5", twin)])
        ends = "fy+ fy- t0 t1 t2 t3 t4 " + ("r1 r2" if in_rows else "qy+ qy-") + ("" if in_columns else " t5")
        table["done"] = (ends, [])
        for name, (waits, issues) in table.items():
            acts[name, part] = ([(key, part) for key in waits.split()], issues)
    now, free, arrival, order, products, early, count = 0.0, {}, {}, [], [], [], 0

    def issue(act):
        for links, key, length in acts.pop(act)[1]:
            end = 0.0
            for link in links.split():
                free[link] = max(now, free.get(link, 0.0)) + length
                end = max(end, free[link])
            arrival[key, act[1]] = end + latency
        order.append(act)

    def extend(name, part, turn):
        if order[-1][:2] == (name, part):
            order[-1] = (name, part, order[-1][2], turn + 1)
        else:
            order.append((name, part, turn, turn + 1))

    while acts or products or early:
        known = []
        for act, (waits, _) in acts.items():
            name, part = act
            if name in links_of:
                if not any((name, other) in acts for other in range(part)):
                    place = part - 1 if name == "owx" else part + LATER
                    known.append((free.get(links_of[name], 0.0) - SLACK, (place, -1, act)))
            elif all(key in arrival for key in waits):
                known.append((max(arrival[key] for key in waits), (part, rank.index(name), act)))
        ready = [choice for when, choice in known if when <= now]
        if ready:
            act = min(ready)[2]
            issue(act)
            if act[0] == "done":
                products += [(act[1], turn) for turn in range(turns)]
        elif products:
            part, turn = products.pop(0)
            extend("mul", part, turn)
            now += product
            count += part < EARLY_PARTS
            if part < EARLY_PARTS and count == EARLY_PARTS * turns:
                early = list(range(SEG))
        elif early:
            extend("inv", 0, early.pop(0))
            now += transform
        else:
            now = min(when for when, _ in known)
    return order


def pairs_kernel(
    taps_ref, flags_hbm, traces_hbm, forward_hbm, early_hbm, late_hbm, out_ref, flags_ref, forward, early_ref, late_ref,
    padded, filtered, whitened, rows_ref, block, own_ref, left_ref, right_ref, cross, message, stage, early_sum,
    send_sem, recv_sem, local_sem, out_send, out_recv,
):
    loads = ((traces_hbm, padded.at[:, pl.ds(128, RECORD)]), (flags_hbm, flags_ref), (forward_hbm, forward))
    loads += ((early_hbm, early_ref), (late_hbm, late_ref))
    loads = [pltpu.make_async_copy(*pair, local_sem.at[2 + index]) for index, pair in enumerate(loads)]
    for copy in loads:
        copy.start()
    stn, seg = lax.axis_index("stn"), lax.axis_index("seg")
    core, z, x_lo = stn % 2, (stn // 2) % 4, stn // 8
    x_hi, y = seg % 2, seg // 2
    size = FREQS // PARTS
    half = size // 2

    def on_row(yy, hh):
        return (stn, (yy % 4) * 2 + hh)

    def on_column(zz, ll, cc):
        return ((ll * 4 + zz % 4) * 2 + cc, seg)

    def row_slot(yy, hh):
        return (yy % 4) * 2 + hh

    def column_slot(zz, ll, cc):
        return (ll * 4 + zz % 4) * 2 + cc

    across = (on_column(z, 1 - x_lo, core)[0], row_slot(y, 1 - x_hi))
    twin = on_column(z, x_lo, 1 - core)
    neighbours = [on_column(z + 1, x_lo, core), on_column(z + 3, x_lo, core), on_column(z, 1 - x_lo, core), twin, across]
    neighbours += [(stn, (seg + shift) % SEG) for shift in range(1, SEG)]
    barrier = pltpu.get_barrier_semaphore()
    for device in neighbours:
        pl.semaphore_signal(barrier, inc=1, device_id=device, device_id_type=MESH)

    def ready():
        loads[0].wait()
        loads[1].wait()

    whiten(taps_ref, flags_ref, padded, filtered, whitened, rows_ref, ready)
    samples = gathered_samples(rows_ref)
    loads[2].wait()
    spectrum(0, forward, samples, block, own_ref)
    pl.semaphore_wait(barrier, len(neighbours))

    started = []

    def send(kind, part, source, target, device):
        copy = pltpu.make_async_remote_copy(
            src_ref=source,
            dst_ref=target,
            send_sem=send_sem.at[part, kind],
            recv_sem=recv_sem.at[part, kind],
            device_id=device,
            device_id_type=MESH,
        )
        copy.start()
        started.append(copy)

    def arrive(kind, part, target):
        pltpu.make_async_remote_copy(
            src_ref=target,
            dst_ref=target,
            send_sem=send_sem.at[part, kind],
            recv_sem=recv_sem.at[part, kind],
            device_id=(stn, seg),
            device_id_type=MESH,
        ).wait_recv()

    def piece(ref, slot, part, which=None):
        first = part * size if which is None else part * size + which * half
        return ref.at[slot, pl.ds(first, size if which is None else half)]

    class Ring:
        def __init__(self, ref, slot, device, place, first):
            self.ref, self.slot, self.device, self.place, self.first = ref, slot, device, place, first

        def start(self, part, source, group, kind):
            slot = self.slot(self.place, group)
            for side, step in ((0, 1), (1, 3)):
                send(self.first + kind + side, part, source, piece(self.ref, slot, part), self.device(self.place + step))

        def pass_on(self, part, group, kind):
            for side, step in ((0, 3), (1, 1)):
                slot = self.slot(self.place + step, group)
                arrive(self.first + kind + side, part, piece(self.ref, slot, part))
                data = piece(self.ref, slot, part, side)
                send(self.first + kind + 2 + side, part, data, data, self.device(self.place + 4 - step))

        def finish(self, part, group, kind):
            slot = self.slot(self.place + 2, group)
            for side in (0, 1):
                arrive(self.first + kind + 2 + side, part, piece(self.ref, slot, part, side))

    rows = Ring(left_ref, row_slot, lambda yy: on_row(yy, x_hi), y, 0)
    columns = Ring(right_ref, lambda zz, ll: column_slot(zz, ll, core), lambda zz: on_column(zz, x_lo, core), z, 9)

    def share(kind, part, zz, ll):
        data = piece(right_ref, column_slot(zz, ll, core), part)
        send(kind, part, data, data, twin)

    beside = on_column(z, 1 - x_lo, core)

    def own_piece(part):
        return own_ref.at[pl.ds(part * size, size)]

    def start_rows(part):
        rows.start(part, own_piece(part), x_hi, 0)

    def start_columns(part):
        columns.start(part, own_piece(part), x_lo, 0)

    def start_beside(part):
        source = own_piece(part)
        own_column = piece(right_ref, column_slot(z, x_lo, core), part)
        send(17, part, source, own_column, beside)
        send(18, part, source, own_column, twin)

    def pass_along(kind, part, ref, slot, device):
        data = piece(ref, slot, part)
        send(kind, part, data, data, device)

    def pass_rows(part):
        rows.pass_on(part, x_hi, 0)
        if part in ROWS_ALONG_X:
            for kind, step in ((4, 3), (5, 1)):
                pass_along(kind, part, left_ref, row_slot(y + step, x_hi), on_row(y, 1 - x_hi))

    def pass_columns(part):
        columns.pass_on(part, x_lo, 0)
        if part in COLUMNS_ALONG_X:
            for kind, step in ((13, 3), (14, 1)):
                pass_along(kind, part, right_ref, column_slot(z + step, x_lo, core), beside)
        share(19, part, z + 3, x_lo)
        share(20, part, z + 1, x_lo)

    def relay(part):
        data = piece(right_ref, column_slot(z, 1 - x_lo, core), part)
        arrive(17, part, data)
        send(8, part, data, piece(left_ref, row_slot(y, x_hi), part), across)
        if part not in COLUMNS_ALONG_X:
            columns.start(part, data, 1 - x_lo, 4)
        share(22, part, z, 1 - x_lo)

    def start_partner(part):
        data = piece(left_ref, row_slot(y, 1 - x_hi), part)
        arrive(8, part, data)
        if part not in ROWS_ALONG_X:
            rows.start(part, data, 1 - x_hi, 4)

    def pass_partner_rows(part):
        rows.pass_on(part, 1 - x_hi, 4)

    def pass_partner_columns(part):
        columns.pass_on(part, 1 - x_lo, 4)
        share(23, part, z + 3, 1 - x_lo)
        share(24, part, z + 1, 1 - x_lo)

    def end_rows(part):
        rows.finish(part, x_hi, 0)
        pass_along(6, part, left_ref, row_slot(y + 2, x_hi), on_row(y, 1 - x_hi))

    def end_columns(part):
        columns.finish(part, x_lo, 0)
        if part in COLUMNS_ALONG_X:
            pass_along(15, part, right_ref, column_slot(z + 2, x_lo, core), beside)
        share(21, part, z + 2, x_lo)

    def end_partner_columns(part):
        if part in COLUMNS_ALONG_X:
            for kind, share_kind, step in ((13, 23, 3), (14, 24, 1), (15, 25, 2)):
                arrive(kind, part, piece(right_ref, column_slot(z + step, 1 - x_lo, core), part))
                share(share_kind, part, z + step, 1 - x_lo)
        else:
            columns.finish(part, 1 - x_lo, 4)
            share(25, part, z + 2, 1 - x_lo)

    def complete(part):
        if part in ROWS_ALONG_X:
            for kind, step in ((4, 3), (5, 1), (6, 2)):
                arrive(kind, part, piece(left_ref, row_slot(y + step, 1 - x_hi), part))
        else:
            rows.finish(part, x_hi, 0)
            rows.finish(part, 1 - x_hi, 4)
        order = ((18, 0, x_lo), (19, 3, x_lo), (20, 1, x_lo), (21, 2, x_lo))
        order += ((22, 0, 1 - x_lo), (23, 3, 1 - x_lo), (24, 1, 1 - x_lo), (25, 2, 1 - x_lo))
        for kind, step, ll in order:
            arrive(kind, part, piece(right_ref, column_slot(z + step, ll, 1 - core), part))

    def multiply(part, first, last):
        @pl.loop(first, last)
        def _(turn):
            for offset in range(UNROLL):
                index = part * size + turn * UNROLL + offset
                left = left_ref[:, index].reshape(LEFT, 128)
                right = right_ref[:, index].reshape(RIGHT, 128)
                turned = jnp.concatenate([-left[:, HALF:], left[:, :HALF]], axis=1)
                both = jnp.concatenate([left, turned], axis=0)
                product = lax.dot_general(right, both, (((1,), (1,)), ((), ())), preferred_element_type=jnp.float32)
                cross[pl.ds(pl.multiple_of(index * PITCH, 8), RIGHT), :] = product

    low_half = lax.broadcasted_iota(jnp.int32, (LAGPAD, 128), 1) < HALF

    def inverse(group, matrix_ref, first, last, into):
        def lagged(row):
            values = cross[pl.ds(first * PITCH + row, last - first, stride=PITCH), :].astype(jnp.bfloat16)
            parts = jnp.dot(matrix_ref[...], values, preferred_element_type=jnp.float32)
            parts = parts[: 2 * LAGPAD] + parts[2 * LAGPAD :]
            return parts[:LAGPAD], parts[LAGPAD:]

        for row in range(ROWS):
            first_re, first_im = lagged(group * (2 * ROWS) + row)
            second_re, second_im = lagged(group * (2 * ROWS) + ROWS + row)
            straight = jnp.where(low_half, first_re, second_im)
            crossed = jnp.where(low_half, second_re, first_im)
            into[pl.ds(row, LAGPAD, stride=ROWS), :] = straight + pltpu.roll(crossed, HALF, 1)

    def transform_early(first, last):
        @pl.loop(first, last)
        def _(group):
            inverse(group, early_ref, 0, EARLY, early_sum.at[group])

    actions = {
        "owx": start_beside,
        "owy": start_rows,
        "owz": start_columns,
        "pro": pass_rows,
        "pco": pass_columns,
        "rel": relay,
        "stp": start_partner,
        "prp": pass_partner_rows,
        "pcp": pass_partner_columns,
        "cro": end_rows,
        "cco": end_columns,
        "ccp": end_partner_columns,
        "done": complete,
    }
    per = PARTS // FBLOCKS
    blocks_done = 1
    locals_ = []
    for name, part, *turns in transfer_order():
        needed = part // per + 1 if name in ("owx", "owy", "owz") else FBLOCKS
        while blocks_done < needed:
            spectrum(blocks_done, forward, samples, block, own_ref)
            blocks_done += 1
            if blocks_done == FBLOCKS:
                loads[3].wait()
                loads[4].wait()
                for index, target in enumerate(
                    (left_ref.at[row_slot(y, x_hi)], right_ref.at[column_slot(z, x_lo, core)])
                ):
                    copy = pltpu.make_async_copy(own_ref, target, local_sem.at[index])
                    copy.start()
                    locals_.append(copy)
        if name == "mul":
            if locals_:
                locals_.pop().wait()
                locals_.pop().wait()
            multiply(part, *turns)
        elif name == "inv":
            transform_early(*turns)
        else:
            actions[name](part)

    def peer_of(turn, sign):
        if isinstance(turn, int):
            along_y, along_x = ((2, 1), (2, 0), (1, 1), (3, 1), (0, 1), (1, 0), (3, 0))[turn]
        else:
            odd = jnp.where((turn == 2) | (turn == 5), 1, jnp.where(turn == 4, 0, 3))
            along_y = jnp.where(turn < 2, 2, odd)
            along_x = jnp.where((turn == 0) | ((turn >= 2) & (turn <= 4)), 1, 0)
        return ((y + 4 + sign * along_y) % 4) * 2 + (x_hi + along_x) % 2

    def hand_over(turn):
        peer = peer_of(turn, 1)
        return pltpu.make_async_remote_copy(
            src_ref=message.at[peer],
            dst_ref=out_ref.at[seg],
            send_sem=out_send.at[turn],
            recv_sem=out_recv.at[turn],
            device_id=(stn, peer),
            device_id_type=MESH,
        )

    def transform(group):
        inverse(group, late_ref, EARLY, FREQS, stage)
        both = stage[: LAGS * ROWS, :] + early_sum[group, : LAGS * ROWS, :]
        return both.reshape(LAGS, ROWS, 128).astype(jnp.bfloat16)

    @pl.loop(0, SEG - 1)
    def _(turn):
        group = peer_of(turn, 1)
        message[group] = transform(group)

        @pl.when(turn > 0)
        def _():
            hand_over(turn - 1).start()

    out_ref[seg] = transform(seg)
    hand_over(SEG - 2).start()
    for copy in started:
        copy.wait_send()
    for turn in range(SEG - 1):
        slot = out_ref.at[peer_of(turn, -1)]
        pltpu.make_async_remote_copy(
            src_ref=slot,
            dst_ref=slot,
            send_sem=out_send.at[turn],
            recv_sem=out_recv.at[turn],
            device_id=(stn, seg),
            device_id_type=MESH,
        ).wait_recv()
        hand_over(turn).wait_send()


def pairs(traces, fir_taps, seg_flags):
    result = (SEG, LAGS, ROWS, 128)
    spectra = (FREQS, ROWS, 128)
    forward = forward_matrix()
    early, late = inverse_matrix()
    return pl.pallas_call(
        pairs_kernel,
        out_shape=jax.ShapeDtypeStruct(result, jnp.bfloat16),
        in_specs=[pl.BlockSpec(memory_space=pltpu.SMEM), HBM, HBM, HBM, HBM, HBM],
        out_specs=VMEM,
        scratch_shapes=[
            pltpu.VMEM((ROWS, SEGS), jnp.int32),
            pltpu.VMEM(forward.shape, jnp.bfloat16),
            pltpu.VMEM(early.shape, jnp.bfloat16),
            pltpu.VMEM(late.shape, jnp.bfloat16),
            pltpu.VMEM((ROWS, RECORD + 256), jnp.float32),
            pltpu.VMEM((ROWS, RECORD + 256), jnp.float32),
            pltpu.VMEM((ROWS, RECORD + 128), jnp.float32),
            pltpu.VMEM((PADDED // 128, ROWS * SEGPITCH, 128), jnp.float32),
            pltpu.VMEM((FBLOCK * ROWS, 128), jnp.float32),
            pltpu.VMEM(spectra, jnp.bfloat16),
            pltpu.VMEM((SEG,) + spectra, jnp.bfloat16),
            pltpu.VMEM((STN,) + spectra, jnp.bfloat16),
            pltpu.VMEM((FREQS * PITCH, 128), jnp.float32),
            pltpu.VMEM(result, jnp.bfloat16),
            pltpu.VMEM((LAGPAD * ROWS, 128), jnp.float32),
            pltpu.VMEM((SEG, LAGPAD * ROWS, 128), jnp.float32),
            pltpu.SemaphoreType.DMA((PARTS, 26)),
            pltpu.SemaphoreType.DMA((PARTS, 26)),
            pltpu.SemaphoreType.DMA((7,)),
            pltpu.SemaphoreType.DMA((SEG,)),
            pltpu.SemaphoreType.DMA((SEG,)),
        ],
        compiler_params=pltpu.CompilerParams(collective_id=0, has_side_effects=True, vmem_limit_bytes=60 << 20),
        name="pairs",
    )(fir_taps, seg_flags, traces, jnp.asarray(forward), jnp.asarray(early), jnp.asarray(late))


def finish_kernel(values_ref, mask_ref, out_ref, buffer, sem):
    keep = mask_ref[...].astype(jnp.float32)
    place = lax.broadcasted_iota(jnp.int32, (LEFT, 128), 1) % LEFT
    pick = jnp.where(place == lax.broadcasted_iota(jnp.int32, (LEFT, 128), 0), 1.0, 0.0).astype(jnp.bfloat16)
    first = lax.broadcasted_iota(jnp.int32, (LEFT, 128), 1) < LEFT
    copies = []
    for start in range(0, LAGS, 8):
        stop = min(start + 8, LAGS)
        for lag in range(start, stop):
            values = values_ref[:, lag].astype(jnp.float32).reshape(LEFT, 128)
            spread = jnp.concatenate([jnp.where(first, values, 0.0), jnp.where(first, 0.0, values)], axis=0)
            turned = lax.dot_general(
                pick, spread.astype(jnp.bfloat16), (((1,), (1,)), ((), ())), preferred_element_type=jnp.float32
            )
            buffer[lag] = turned * keep
        copy = pltpu.make_async_copy(
            buffer.at[pl.ds(start, stop - start)], out_ref.at[pl.ds(start, stop - start)], sem.at[start // 8]
        )
        copy.start()
        copies.append(copy)
    for copy in copies:
        copy.wait()


def finish(values, pair_mask):
    shape = (LAGS, LEFT, RIGHT)
    return pl.pallas_call(
        finish_kernel,
        out_shape=jax.ShapeDtypeStruct(shape, jnp.float32),
        in_specs=[VMEM, VMEM],
        out_specs=HBM,
        scratch_shapes=[pltpu.VMEM(shape, jnp.float32), pltpu.SemaphoreType.DMA((6,))],
        name="finish",
    )(values, pair_mask)


def body(traces, fir_taps, seg_flags, pair_mask):
    return finish(pairs(traces, fir_taps, seg_flags), pair_mask)


def solution(mesh):
    return jax.shard_map(
        body,
        mesh=mesh,
        in_specs=(P(("stn", "seg"), None), P(), P(("stn", "seg"), None), P("stn", "seg")),
        out_specs=P(None, "stn", "seg"),
        check_vma=False,
    )
```

```python
import functools
import math

import jax
import jax.numpy as jnp
import numpy as np
from jax import lax
from jax.experimental import pallas as pl
from jax.experimental.pallas import tpu as pltpu
from jax.sharding import PartitionSpec as P

SAMP = 600
LAGS = 41
TAPS = 31
RADIUS = 64
SEGS = 64
ROWS = 8
EPS = 1e-06

LENGTH = 624
PADDED = 640
FREQS = LENGTH // 2
HALF = SEGS
FBLOCK = 104
FBLOCKS = FREQS // FBLOCK
LAGPAD = 48
PITCH = 136

RECORD = SEGS * SAMP
BLOCKS = RECORD // 128
PER = 100
SEGPITCH = SEGS + 8

STN, SEG = 16, 8
LEFT = ROWS * SEG
RIGHT = ROWS * STN
PARTS = 6

EARLY_PARTS = 2
EARLY = EARLY_PARTS * FREQS // PARTS

MESH = pl.DeviceIdType.MESH
VMEM = pl.BlockSpec(memory_space=pltpu.VMEM)
HBM = pl.BlockSpec(memory_space=pltpu.HBM)


def split_bf16(values):
    high = np.asarray(values, np.float32).astype(jnp.bfloat16)
    low = (np.asarray(values, np.float64) - high.astype(np.float64)).astype(np.float32).astype(jnp.bfloat16)
    return high, low


def frequencies():
    return (np.arange(FREQS) + 0.5) * (2 * np.pi / LENGTH)


def forward_matrix():
    angle = frequencies()[:, None] * np.arange(PADDED)[None, :]
    keep = (np.arange(PADDED) < SAMP)[None, :]
    stacked = np.stack([split_bf16(part * keep)[0] for part in (np.cos(angle), -np.sin(angle))])
    stacked = stacked.reshape(2, FBLOCKS, FBLOCK, PADDED).transpose(1, 0, 2, 3)
    return np.ascontiguousarray(stacked.reshape(FBLOCKS, 2 * FBLOCK, PADDED))


def inverse_matrix():
    lag = np.arange(LAGS) - (LAGS - 1) // 2
    angle = lag[:, None] * frequencies()[None, :]
    padded = np.zeros((2, LAGPAD, FREQS))
    padded[0, :LAGS] = np.cos(angle)
    padded[1, :LAGS] = -np.sin(angle)
    padded *= 2.0 / LENGTH / math.sqrt(RECORD)
    whole = split_bf16(padded.reshape(2 * LAGPAD, FREQS))[0]
    return [np.ascontiguousarray(piece) for piece in np.split(whole, [EARLY], axis=1)]


def whiten(taps_ref, flags_ref, padded, filtered, whitened, rows, ready):
    edge = jnp.zeros((ROWS, 128), jnp.float32)
    padded[:, 0:128] = edge
    padded[:, 128 + RECORD : 256 + RECORD] = edge
    filtered[:, 0:128] = edge
    filtered[:, 128 + RECORD : 256 + RECORD] = edge
    whitened[:, RECORD : RECORD + 128] = edge

    offset = lax.broadcasted_iota(jnp.int32, (384, 128), 0) - lax.broadcasted_iota(jnp.int32, (384, 128), 1)
    band = jnp.zeros((384, 128), jnp.float32)
    for tap in range(TAPS):
        band = jnp.where(offset == 128 - (TAPS - 1) // 2 + tap, taps_ref[tap], band)
    band_high = band.astype(jnp.bfloat16)
    band_low = (band - band_high.astype(jnp.float32)).astype(jnp.bfloat16)
    box = jnp.where((offset >= 128 - RADIUS) & (offset <= 128 + RADIUS), 1.0, 0.0).astype(jnp.bfloat16)

    def side_by_side(matrix):
        return jnp.concatenate([matrix[:128], matrix[128:256], matrix[256:]], axis=1)

    band_high, band_low, box = side_by_side(band_high), side_by_side(band_low), side_by_side(box)
    band_twice = jnp.concatenate([band_high, band_high], axis=0)
    box_twice = jnp.concatenate([box, box], axis=0)

    def blocks(ref, start):
        window = ref[:, pl.ds(start, (PER + 2) * 128)]
        return jnp.concatenate([window[:, 128 * i : 128 * i + 128] for i in range(PER + 2)], axis=0)

    def halves(values):
        high = values.astype(jnp.bfloat16)
        return jnp.concatenate([high, (values - high.astype(jnp.float32)).astype(jnp.bfloat16)], axis=1)

    def over_neighbours(parts):
        size = ROWS * PER
        shifted = [parts[ROWS * i : ROWS * i + size, 128 * i : 128 * i + 128] for i in range(3)]
        return shifted[0] + shifted[1] + shifted[2]

    def product(left, right):
        return jnp.dot(left, right, preferred_element_type=jnp.float32)

    def place(ref, start, values):
        for i in range(PER):
            ref[:, pl.ds(pl.multiple_of(start + 128 * i, 128), 128)] = values[ROWS * i : ROWS * (i + 1)]

    ready()

    @pl.loop(0, BLOCKS // PER)
    def _(chunk):
        start = pl.multiple_of(chunk * (PER * 128), 128)
        both = halves(blocks(padded, start))
        total = over_neighbours(product(both, band_twice) + product(both[:, :128], band_low))
        place(filtered, start + 128, total)

    @pl.loop(0, BLOCKS // PER)
    def _(chunk):
        start = pl.multiple_of(chunk * (PER * 128), 128)
        values = blocks(filtered, start)
        level = over_neighbours(product(halves(jnp.abs(values)), box_twice)) / (2 * RADIUS + 1)
        place(whitened, start, values[ROWS : ROWS * (PER + 1)] / (level + EPS))

    flags = flags_ref[...].astype(jnp.float32)
    for seg in range(SEGS):
        piece = whitened[:, seg * SAMP : seg * SAMP + PADDED] * flags[:, seg : seg + 1]
        for part in range(PADDED // 128):
            rows[part, pl.ds(seg, ROWS, stride=SEGPITCH), :] = piece[:, part * 128 : part * 128 + 128]


def gathered_samples(rows):
    columns = []
    for part in range(PADDED // 128):
        pieces = [rows[part, SEGPITCH * row : SEGPITCH * row + SEGS, :] for row in range(ROWS)]
        columns.append(jnp.concatenate(pieces, axis=0))
    return jnp.concatenate(columns, axis=1).astype(jnp.bfloat16)


def spectrum(step, forward, samples, block, own):
    low_half = lax.broadcasted_iota(jnp.int32, (FBLOCK, 128), 1) < HALF
    both = lax.dot_general(forward[step], samples, (((1,), (1,)), ((), ())), preferred_element_type=jnp.float32)
    for pair in range(ROWS // 2):
        real = both[:FBLOCK, pair * 128 : pair * 128 + 128]
        imag = both[FBLOCK:, pair * 128 : pair * 128 + 128]
        even = jnp.where(low_half, real, pltpu.roll(imag, HALF, 1))
        odd = jnp.where(low_half, pltpu.roll(real, HALF, 1), imag)
        block[pl.ds(2 * pair, FBLOCK, stride=ROWS), :] = even
        block[pl.ds(2 * pair + 1, FBLOCK, stride=ROWS), :] = odd
    own[pl.ds(step * FBLOCK, FBLOCK)] = block[...].reshape(FBLOCK, ROWS, 128).astype(jnp.bfloat16)


UNROLL = 13

ROWS_ALONG_X = (2,)
COLUMNS_ALONG_X = (1, 4)
SLACK = 2.5
LATER = 2


def transfer_order():
    unit, latency, twin = 15.7 / PARTS, 2.5, 4.0 / PARTS
    product, transform, turns = 12.7 * UNROLL / FREQS, 0.25 + 0.55 * EARLY_PARTS / PARTS, FREQS // PARTS // UNROLL
    rank = ("rel", "stp", "pro", "pco", "prp", "pcp", "cro", "cco", "ccp", "done")
    links_of = {"owx": "l", "owy": "y+", "owz": "z+"}
    acts = {}
    for part in range(PARTS):
        in_rows, in_columns = part in ROWS_ALONG_X, part in COLUMNS_ALONG_X

        def both(axis, stage, share):
            return [(link, stage + link, share * unit) for link in (axis + "+", axis + "-")]

        table = {
            "owx": ("", [("l", "l", unit), ("t", "t0", twin)]),
            "owy": ("", both("y", "o", 1)),
            "owz": ("", both("z", "o", 1)),
            "pro": ("oy+ oy-", both("y", "f", 0.5) + [("l c", "r1", 2 * unit)] * in_rows),
            "pco": ("oz+ oz-", both("z", "f", 0.5) + [("l", "c1", 2 * unit)] * in_columns + [("t", "t1", 2 * twin)]),
            "rel": ("l", [("c", "c", unit), ("t", "t2", twin)] + ([] if in_columns else both("z", "p", 1))),
            "stp": ("c", [] if in_rows else both("y", "p", 1)),
            "cco": ("fz+ fz-", [("l", "c2", unit)] * in_columns + [("t", "t4", twin)]),
        }
        if in_rows:
            table["cro"] = ("fy+ fy-", [("l c", "r2", unit)])
        else:
            table["prp"] = ("py+ py-", both("y", "q", 0.5))
        if in_columns:
            table["ccp"] = ("c1 c2", [("t", "t3", 3 * twin)])
        else:
            table["pcp"] = ("pz+ pz-", both("z", "q", 0.5) + [("t", "t3", 2 * twin)])
            table["ccp"] = ("qz+ qz-", [("t", "t5", twin)])
        ends = "fy+ fy- t0 t1 t2 t3 t4 " + ("r1 r2" if in_rows else "qy+ qy-") + ("" if in_columns else " t5")
        table["done"] = (ends, [])
        for name, (waits, issues) in table.items():
            acts[name, part] = ([(key, part) for key in waits.split()], issues)
    now, free, arrival, order, products, early, count = 0.0, {}, {}, [], [], [], 0

    def issue(act):
        for links, key, length in acts.pop(act)[1]:
            end = 0.0
            for link in links.split():
                free[link] = max(now, free.get(link, 0.0)) + length
                end = max(end, free[link])
            arrival[key, act[1]] = end + latency
        order.append(act)

    def extend(name, part, turn):
        if order[-1][:2] == (name, part):
            order[-1] = (name, part, order[-1][2], turn + 1)
        else:
            order.append((name, part, turn, turn + 1))

    while acts or products or early:
        known = []
        for act, (waits, _) in acts.items():
            name, part = act
            if name in links_of:
                if not any((name, other) in acts for other in range(part)):
                    place = part - 1 if name == "owx" else part + LATER
                    known.append((free.get(links_of[name], 0.0) - SLACK, (place, -1, act)))
            elif all(key in arrival for key in waits):
                known.append((max(arrival[key] for key in waits), (part, rank.index(name), act)))
        ready = [choice for when, choice in known if when <= now]
        if ready:
            act = min(ready)[2]
            issue(act)
            if act[0] == "done":
                products += [(act[1], turn) for turn in range(turns)]
        elif products:
            part, turn = products.pop(0)
            extend("mul", part, turn)
            now += product
            count += part < EARLY_PARTS
            if part < EARLY_PARTS and count == EARLY_PARTS * turns:
                early = list(range(SEG))
        elif early:
            extend("inv", 0, early.pop(0))
            now += transform
        else:
            now = min(when for when, _ in known)
    return order


def pairs_kernel(
    taps_ref, flags_hbm, traces_hbm, forward_hbm, early_hbm, late_hbm, out_ref, flags_ref, forward, early_ref, late_ref,
    padded, filtered, whitened, rows_ref, block, own_ref, left_ref, right_ref, cross, message, stage, early_sum,
    send_sem, recv_sem, local_sem, out_send, out_recv,
):
    loads = ((traces_hbm, padded.at[:, pl.ds(128, RECORD)]), (flags_hbm, flags_ref), (forward_hbm, forward))
    loads += ((early_hbm, early_ref), (late_hbm, late_ref))
    loads = [pltpu.make_async_copy(*pair, local_sem.at[2 + index]) for index, pair in enumerate(loads)]
    for copy in loads:
        copy.start()
    stn, seg = lax.axis_index("stn"), lax.axis_index("seg")
    core, z, x_lo = stn % 2, (stn // 2) % 4, stn // 8
    x_hi, y = seg % 2, seg // 2
    size = FREQS // PARTS
    half = size // 2

    def on_row(yy, hh):
        return (stn, (yy % 4) * 2 + hh)

    def on_column(zz, ll, cc):
        return ((ll * 4 + zz % 4) * 2 + cc, seg)

    def row_slot(yy, hh):
        return (yy % 4) * 2 + hh

    def column_slot(zz, ll, cc):
        return (ll * 4 + zz % 4) * 2 + cc

    across = (on_column(z, 1 - x_lo, core)[0], row_slot(y, 1 - x_hi))
    twin = on_column(z, x_lo, 1 - core)
    neighbours = [on_column(z + 1, x_lo, core), on_column(z + 3, x_lo, core), on_column(z, 1 - x_lo, core), twin, across]
    neighbours += [(stn, (seg + shift) % SEG) for shift in range(1, SEG)]
    barrier = pltpu.get_barrier_semaphore()
    for device in neighbours:
        pl.semaphore_signal(barrier, inc=1, device_id=device, device_id_type=MESH)

    def ready():
        loads[0].wait()
        loads[1].wait()

    whiten(taps_ref, flags_ref, padded, filtered, whitened, rows_ref, ready)
    samples = gathered_samples(rows_ref)
    loads[2].wait()
    spectrum(0, forward, samples, block, own_ref)
    pl.semaphore_wait(barrier, len(neighbours))

    started = []

    def send(kind, part, source, target, device):
        copy = pltpu.make_async_remote_copy(
            src_ref=source,
            dst_ref=target,
            send_sem=send_sem.at[part, kind],
            recv_sem=recv_sem.at[part, kind],
            device_id=device,
            device_id_type=MESH,
        )
        copy.start()
        started.append(copy)

    def arrive(kind, part, target):
        pltpu.make_async_remote_copy(
            src_ref=target,
            dst_ref=target,
            send_sem=send_sem.at[part, kind],
            recv_sem=recv_sem.at[part, kind],
            device_id=(stn, seg),
            device_id_type=MESH,
        ).wait_recv()

    def piece(ref, slot, part, which=None):
        first = part * size if which is None else part * size + which * half
        return ref.at[slot, pl.ds(first, size if which is None else half)]

    class Ring:
        def __init__(self, ref, slot, device, place, first):
            self.ref, self.slot, self.device, self.place, self.first = ref, slot, device, place, first

        def start(self, part, source, group, kind):
            slot = self.slot(self.place, group)
            for side, step in ((0, 1), (1, 3)):
                send(self.first + kind + side, part, source, piece(self.ref, slot, part), self.device(self.place + step))

        def pass_on(self, part, group, kind):
            for side, step in ((0, 3), (1, 1)):
                slot = self.slot(self.place + step, group)
                arrive(self.first + kind + side, part, piece(self.ref, slot, part))
                data = piece(self.ref, slot, part, side)
                send(self.first + kind + 2 + side, part, data, data, self.device(self.place + 4 - step))

        def finish(self, part, group, kind):
            slot = self.slot(self.place + 2, group)
            for side in (0, 1):
                arrive(self.first + kind + 2 + side, part, piece(self.ref, slot, part, side))

    rows = Ring(left_ref, row_slot, lambda yy: on_row(yy, x_hi), y, 0)
    columns = Ring(right_ref, lambda zz, ll: column_slot(zz, ll, core), lambda zz: on_column(zz, x_lo, core), z, 9)

    def share(kind, part, zz, ll):
        data = piece(right_ref, column_slot(zz, ll, core), part)
        send(kind, part, data, data, twin)

    beside = on_column(z, 1 - x_lo, core)

    def own_piece(part):
        return own_ref.at[pl.ds(part * size, size)]

    def start_rows(part):
        rows.start(part, own_piece(part), x_hi, 0)

    def start_columns(part):
        columns.start(part, own_piece(part), x_lo, 0)

    def start_beside(part):
        source = own_piece(part)
        own_column = piece(right_ref, column_slot(z, x_lo, core), part)
        send(17, part, source, own_column, beside)
        send(18, part, source, own_column, twin)

    def pass_along(kind, part, ref, slot, device):
        data = piece(ref, slot, part)
        send(kind, part, data, data, device)

    def pass_rows(part):
        rows.pass_on(part, x_hi, 0)
        if part in ROWS_ALONG_X:
            for kind, step in ((4, 3), (5, 1)):
                pass_along(kind, part, left_ref, row_slot(y + step, x_hi), on_row(y, 1 - x_hi))

    def pass_columns(part):
        columns.pass_on(part, x_lo, 0)
        if part in COLUMNS_ALONG_X:
            for kind, step in ((13, 3), (14, 1)):
                pass_along(kind, part, right_ref, column_slot(z + step, x_lo, core), beside)
        share(19, part, z + 3, x_lo)
        share(20, part, z + 1, x_lo)

    def relay(part):
        data = piece(right_ref, column_slot(z, 1 - x_lo, core), part)
        arrive(17, part, data)
        send(8, part, data, piece(left_ref, row_slot(y, x_hi), part), across)
        if part not in COLUMNS_ALONG_X:
            columns.start(part, data, 1 - x_lo, 4)
        share(22, part, z, 1 - x_lo)

    def start_partner(part):
        data = piece(left_ref, row_slot(y, 1 - x_hi), part)
        arrive(8, part, data)
        if part not in ROWS_ALONG_X:
            rows.start(part, data, 1 - x_hi, 4)

    def pass_partner_rows(part):
        rows.pass_on(part, 1 - x_hi, 4)

    def pass_partner_columns(part):
        columns.pass_on(part, 1 - x_lo, 4)
        share(23, part, z + 3, 1 - x_lo)
        share(24, part, z + 1, 1 - x_lo)

    def end_rows(part):
        rows.finish(part, x_hi, 0)
        pass_along(6, part, left_ref, row_slot(y + 2, x_hi), on_row(y, 1 - x_hi))

    def end_columns(part):
        columns.finish(part, x_lo, 0)
        if part in COLUMNS_ALONG_X:
            pass_along(15, part, right_ref, column_slot(z + 2, x_lo, core), beside)
        share(21, part, z + 2, x_lo)

    def end_partner_columns(part):
        if part in COLUMNS_ALONG_X:
            for kind, share_kind, step in ((13, 23, 3), (14, 24, 1), (15, 25, 2)):
                arrive(kind, part, piece(right_ref, column_slot(z + step, 1 - x_lo, core), part))
                share(share_kind, part, z + step, 1 - x_lo)
        else:
            columns.finish(part, 1 - x_lo, 4)
            share(25, part, z + 2, 1 - x_lo)

    def complete(part):
        if part in ROWS_ALONG_X:
            for kind, step in ((4, 3), (5, 1), (6, 2)):
                arrive(kind, part, piece(left_ref, row_slot(y + step, 1 - x_hi), part))
        else:
            rows.finish(part, x_hi, 0)
            rows.finish(part, 1 - x_hi, 4)
        order = ((18, 0, x_lo), (19, 3, x_lo), (20, 1, x_lo), (21, 2, x_lo))
        order += ((22, 0, 1 - x_lo), (23, 3, 1 - x_lo), (24, 1, 1 - x_lo), (25, 2, 1 - x_lo))
        for kind, step, ll in order:
            arrive(kind, part, piece(right_ref, column_slot(z + step, ll, 1 - core), part))

    def multiply(part, first, last):
        @pl.loop(first, last)
        def _(turn):
            for offset in range(UNROLL):
                index = part * size + turn * UNROLL + offset
                left = left_ref[:, index].reshape(LEFT, 128)
                right = right_ref[:, index].reshape(RIGHT, 128)
                turned = jnp.concatenate([-left[:, HALF:], left[:, :HALF]], axis=1)
                both = jnp.concatenate([left, turned], axis=0)
                product = lax.dot_general(right, both, (((1,), (1,)), ((), ())), preferred_element_type=jnp.float32)
                cross[pl.ds(pl.multiple_of(index * PITCH, 8), RIGHT), :] = product

    low_half = lax.broadcasted_iota(jnp.int32, (LAGPAD, 128), 1) < HALF

    def inverse(group, matrix_ref, first, last, into):
        def lagged(row):
            values = cross[pl.ds(first * PITCH + row, last - first, stride=PITCH), :].astype(jnp.bfloat16)
            parts = jnp.dot(matrix_ref[...], values, preferred_element_type=jnp.float32)
            return parts[:LAGPAD], parts[LAGPAD:]

        for row in range(ROWS):
            first_re, first_im = lagged(group * (2 * ROWS) + row)
            second_re, second_im = lagged(group * (2 * ROWS) + ROWS + row)
            straight = jnp.where(low_half, first_re, second_im)
            crossed = jnp.where(low_half, second_re, first_im)
            into[pl.ds(row, LAGPAD, stride=ROWS), :] = straight + pltpu.roll(crossed, HALF, 1)

    def transform_early(first, last):
        @pl.loop(first, last)
        def _(group):
            inverse(group, early_ref, 0, EARLY, early_sum.at[group])

    actions = {
        "owx": start_beside,
        "owy": start_rows,
        "owz": start_columns,
        "pro": pass_rows,
        "pco": pass_columns,
        "rel": relay,
        "stp": start_partner,
        "prp": pass_partner_rows,
        "pcp": pass_partner_columns,
        "cro": end_rows,
        "cco": end_columns,
        "ccp": end_partner_columns,
        "done": complete,
    }
    per = PARTS // FBLOCKS
    blocks_done = 1
    locals_ = []
    for name, part, *turns in transfer_order():
        needed = part // per + 1 if name in ("owx", "owy", "owz") else FBLOCKS
        while blocks_done < needed:
            spectrum(blocks_done, forward, samples, block, own_ref)
            blocks_done += 1
            if blocks_done == FBLOCKS:
                loads[3].wait()
                loads[4].wait()
                for index, target in enumerate(
                    (left_ref.at[row_slot(y, x_hi)], right_ref.at[column_slot(z, x_lo, core)])
                ):
                    copy = pltpu.make_async_copy(own_ref, target, local_sem.at[index])
                    copy.start()
                    locals_.append(copy)
        if name == "mul":
            if locals_:
                locals_.pop().wait()
                locals_.pop().wait()
            multiply(part, *turns)
        elif name == "inv":
            transform_early(*turns)
        else:
            actions[name](part)

    def peer_of(turn, sign):
        if isinstance(turn, int):
            along_y, along_x = ((2, 1), (2, 0), (1, 1), (3, 1), (0, 1), (1, 0), (3, 0))[turn]
        else:
            odd = jnp.where((turn == 2) | (turn == 5), 1, jnp.where(turn == 4, 0, 3))
            along_y = jnp.where(turn < 2, 2, odd)
            along_x = jnp.where((turn == 0) | ((turn >= 2) & (turn <= 4)), 1, 0)
        return ((y + 4 + sign * along_y) % 4) * 2 + (x_hi + along_x) % 2

    def hand_over(turn):
        peer = peer_of(turn, 1)
        return pltpu.make_async_remote_copy(
            src_ref=message.at[peer],
            dst_ref=out_ref.at[seg],
            send_sem=out_send.at[turn],
            recv_sem=out_recv.at[turn],
            device_id=(stn, peer),
            device_id_type=MESH,
        )

    def transform(group):
        inverse(group, late_ref, EARLY, FREQS, stage)
        both = stage[: LAGS * ROWS, :] + early_sum[group, : LAGS * ROWS, :]
        return both.reshape(LAGS, ROWS, 128).astype(jnp.bfloat16)

    @pl.loop(0, SEG - 1)
    def _(turn):
        group = peer_of(turn, 1)
        message[group] = transform(group)

        @pl.when(turn > 0)
        def _():
            hand_over(turn - 1).start()

    out_ref[seg] = transform(seg)
    hand_over(SEG - 2).start()
    for copy in started:
        copy.wait_send()
    for turn in range(SEG - 1):
        slot = out_ref.at[peer_of(turn, -1)]
        pltpu.make_async_remote_copy(
            src_ref=slot,
            dst_ref=slot,
            send_sem=out_send.at[turn],
            recv_sem=out_recv.at[turn],
            device_id=(stn, seg),
            device_id_type=MESH,
        ).wait_recv()
        hand_over(turn).wait_send()


def pairs(traces, fir_taps, seg_flags):
    result = (SEG, LAGS, ROWS, 128)
    spectra = (FREQS, ROWS, 128)
    forward = forward_matrix()
    early, late = inverse_matrix()
    return pl.pallas_call(
        pairs_kernel,
        out_shape=jax.ShapeDtypeStruct(result, jnp.bfloat16),
        in_specs=[pl.BlockSpec(memory_space=pltpu.SMEM), HBM, HBM, HBM, HBM, HBM],
        out_specs=VMEM,
        scratch_shapes=[
            pltpu.VMEM((ROWS, SEGS), jnp.int32),
            pltpu.VMEM(forward.shape, jnp.bfloat16),
            pltpu.VMEM(early.shape, jnp.bfloat16),
            pltpu.VMEM(late.shape, jnp.bfloat16),
            pltpu.VMEM((ROWS, RECORD + 256), jnp.float32),
            pltpu.VMEM((ROWS, RECORD + 256), jnp.float32),
            pltpu.VMEM((ROWS, RECORD + 128), jnp.float32),
            pltpu.VMEM((PADDED // 128, ROWS * SEGPITCH, 128), jnp.float32),
            pltpu.VMEM((FBLOCK * ROWS, 128), jnp.float32),
            pltpu.VMEM(spectra, jnp.bfloat16),
            pltpu.VMEM((SEG,) + spectra, jnp.bfloat16),
            pltpu.VMEM((STN,) + spectra, jnp.bfloat16),
            pltpu.VMEM((FREQS * PITCH, 128), jnp.float32),
            pltpu.VMEM(result, jnp.bfloat16),
            pltpu.VMEM((LAGPAD * ROWS, 128), jnp.float32),
            pltpu.VMEM((SEG, LAGPAD * ROWS, 128), jnp.float32),
            pltpu.SemaphoreType.DMA((PARTS, 26)),
            pltpu.SemaphoreType.DMA((PARTS, 26)),
            pltpu.SemaphoreType.DMA((7,)),
            pltpu.SemaphoreType.DMA((SEG,)),
            pltpu.SemaphoreType.DMA((SEG,)),
        ],
        compiler_params=pltpu.CompilerParams(collective_id=0, has_side_effects=True, vmem_limit_bytes=60 << 20),
        name="pairs",
    )(fir_taps, seg_flags, traces, jnp.asarray(forward), jnp.asarray(early), jnp.asarray(late))


def finish_kernel(values_ref, mask_ref, out_ref, buffer, sem):
    keep = mask_ref[...].astype(jnp.float32)
    place = lax.broadcasted_iota(jnp.int32, (LEFT, 128), 1) % LEFT
    pick = jnp.where(place == lax.broadcasted_iota(jnp.int32, (LEFT, 128), 0), 1.0, 0.0).astype(jnp.bfloat16)
    first = lax.broadcasted_iota(jnp.int32, (LEFT, 128), 1) < LEFT
    copies = []
    for start in range(0, LAGS, 8):
        stop = min(start + 8, LAGS)
        for lag in range(start, stop):
            values = values_ref[:, lag].astype(jnp.float32).reshape(LEFT, 128)
            spread = jnp.concatenate([jnp.where(first, values, 0.0), jnp.where(first, 0.0, values)], axis=0)
            turned = lax.dot_general(
                pick, spread.astype(jnp.bfloat16), (((1,), (1,)), ((), ())), preferred_element_type=jnp.float32
            )
            buffer[lag] = turned * keep
        copy = pltpu.make_async_copy(
            buffer.at[pl.ds(start, stop - start)], out_ref.at[pl.ds(start, stop - start)], sem.at[start // 8]
        )
        copy.start()
        copies.append(copy)
    for copy in copies:
        copy.wait()


def finish(values, pair_mask):
    shape = (LAGS, LEFT, RIGHT)
    return pl.pallas_call(
        finish_kernel,
        out_shape=jax.ShapeDtypeStruct(shape, jnp.float32),
        in_specs=[VMEM, VMEM],
        out_specs=HBM,
        scratch_shapes=[pltpu.VMEM(shape, jnp.float32), pltpu.SemaphoreType.DMA((6,))],
        name="finish",
    )(values, pair_mask)


def body(traces, fir_taps, seg_flags, pair_mask):
    return finish(pairs(traces, fir_taps, seg_flags), pair_mask)


def solution(mesh):
    return jax.shard_map(
        body,
        mesh=mesh,
        in_specs=(P(("stn", "seg"), None), P(), P(("stn", "seg"), None), P("stn", "seg")),
        out_specs=P(None, "stn", "seg"),
        check_vma=False,
    )
```

```python
import functools
import math

import jax
import jax.numpy as jnp
import numpy as np
from jax import lax
from jax.experimental import pallas as pl
from jax.experimental.pallas import tpu as pltpu
from jax.sharding import PartitionSpec as P

SAMP = 600
LAGS = 41
TAPS = 31
RADIUS = 64
SEGS = 64
ROWS = 8
EPS = 1e-06

LENGTH = 624
PADDED = 640
FREQS = LENGTH // 2
HALF = SEGS
FBLOCK = 104
FBLOCKS = FREQS // FBLOCK
LAGPAD = 48
PITCH = 136

RECORD = SEGS * SAMP
BLOCKS = RECORD // 128
PER = 100
SEGPITCH = SEGS + 8

STN, SEG = 16, 8
LEFT = ROWS * SEG
RIGHT = ROWS * STN
PARTS = 6

EARLY_PARTS = 2
EARLY = EARLY_PARTS * FREQS // PARTS

MESH = pl.DeviceIdType.MESH
VMEM = pl.BlockSpec(memory_space=pltpu.VMEM)
HBM = pl.BlockSpec(memory_space=pltpu.HBM)


def split_bf16(values):
    high = np.asarray(values, np.float32).astype(jnp.bfloat16)
    low = (np.asarray(values, np.float64) - high.astype(np.float64)).astype(np.float32).astype(jnp.bfloat16)
    return high, low


def frequencies():
    return (np.arange(FREQS) + 0.5) * (2 * np.pi / LENGTH)


def forward_matrix():
    angle = frequencies()[:, None] * np.arange(PADDED)[None, :]
    keep = (np.arange(PADDED) < SAMP)[None, :]
    stacked = np.stack([split_bf16(part * keep)[0] for part in (np.cos(angle), -np.sin(angle))])
    stacked = stacked.reshape(2, FBLOCKS, FBLOCK, PADDED).transpose(1, 0, 2, 3)
    return np.ascontiguousarray(stacked.reshape(FBLOCKS, 2 * FBLOCK, PADDED))


def inverse_matrix():
    lag = np.arange(LAGS) - (LAGS - 1) // 2
    angle = lag[:, None] * frequencies()[None, :]
    padded = np.zeros((2, LAGPAD, FREQS))
    padded[0, :LAGS] = np.cos(angle)
    padded[1, :LAGS] = -np.sin(angle)
    padded *= 2.0 / LENGTH / math.sqrt(RECORD)
    whole = split_bf16(padded.reshape(2 * LAGPAD, FREQS))[0]
    return [np.ascontiguousarray(piece) for piece in np.split(whole, [EARLY], axis=1)]


def whiten(taps_ref, flags_ref, padded, filtered, whitened, rows, ready):
    edge = jnp.zeros((ROWS, 128), jnp.float32)
    padded[:, 0:128] = edge
    padded[:, 128 + RECORD : 256 + RECORD] = edge
    filtered[:, 0:128] = edge
    filtered[:, 128 + RECORD : 256 + RECORD] = edge
    whitened[:, RECORD : RECORD + 128] = edge

    offset = lax.broadcasted_iota(jnp.int32, (384, 128), 0) - lax.broadcasted_iota(jnp.int32, (384, 128), 1)
    band = jnp.zeros((384, 128), jnp.float32)
    for tap in range(TAPS):
        band = jnp.where(offset == 128 - (TAPS - 1) // 2 + tap, taps_ref[tap], band)
    band_high = band.astype(jnp.bfloat16)
    band_low = (band - band_high.astype(jnp.float32)).astype(jnp.bfloat16)
    box = jnp.where((offset >= 128 - RADIUS) & (offset <= 128 + RADIUS), 1.0, 0.0).astype(jnp.bfloat16)

    def side_by_side(matrix):
        return jnp.concatenate([matrix[:128], matrix[128:256], matrix[256:]], axis=1)

    band_high, band_low, box = side_by_side(band_high), side_by_side(band_low), side_by_side(box)
    band_twice = jnp.concatenate([band_high, band_high], axis=0)
    box_twice = jnp.concatenate([box, box], axis=0)

    def blocks(ref, start):
        window = ref[:, pl.ds(start, (PER + 2) * 128)]
        return jnp.concatenate([window[:, 128 * i : 128 * i + 128] for i in range(PER + 2)], axis=0)

    def halves(values):
        high = values.astype(jnp.bfloat16)
        return jnp.concatenate([high, (values - high.astype(jnp.float32)).astype(jnp.bfloat16)], axis=1)

    def over_neighbours(parts):
        size = ROWS * PER
        shifted = [parts[ROWS * i : ROWS * i + size, 128 * i : 128 * i + 128] for i in range(3)]
        return shifted[0] + shifted[1] + shifted[2]

    def product(left, right):
        return jnp.dot(left, right, preferred_element_type=jnp.float32)

    def place(ref, start, values):
        for i in range(PER):
            ref[:, pl.ds(pl.multiple_of(start + 128 * i, 128), 128)] = values[ROWS * i : ROWS * (i + 1)]

    ready()

    @pl.loop(0, BLOCKS // PER)
    def _(chunk):
        start = pl.multiple_of(chunk * (PER * 128), 128)
        both = halves(blocks(padded, start))
        total = over_neighbours(product(both, band_twice) + product(both[:, :128], band_low))
        place(filtered, start + 128, total)

    @pl.loop(0, BLOCKS // PER)
    def _(chunk):
        start = pl.multiple_of(chunk * (PER * 128), 128)
        values = blocks(filtered, start)
        level = over_neighbours(product(halves(jnp.abs(values)), box_twice)) / (2 * RADIUS + 1)
        place(whitened, start, values[ROWS : ROWS * (PER + 1)] / (level + EPS))

    flags = flags_ref[...].astype(jnp.float32)
    for seg in range(SEGS):
        piece = whitened[:, seg * SAMP : seg * SAMP + PADDED] * flags[:, seg : seg + 1]
        for part in range(PADDED // 128):
            rows[part, pl.ds(seg, ROWS, stride=SEGPITCH), :] = piece[:, part * 128 : part * 128 + 128]


def gathered_samples(rows):
    columns = []
    for part in range(PADDED // 128):
        pieces = [rows[part, SEGPITCH * row : SEGPITCH * row + SEGS, :] for row in range(ROWS)]
        columns.append(jnp.concatenate(pieces, axis=0))
    return jnp.concatenate(columns, axis=1).astype(jnp.bfloat16)


def spectrum(step, forward, samples, block, own):
    low_half = lax.broadcasted_iota(jnp.int32, (FBLOCK, 128), 1) < HALF
    both = lax.dot_general(forward[step], samples, (((1,), (1,)), ((), ())), preferred_element_type=jnp.float32)
    for pair in range(ROWS // 2):
        real = both[:FBLOCK, pair * 128 : pair * 128 + 128]
        imag = both[FBLOCK:, pair * 128 : pair * 128 + 128]
        even = jnp.where(low_half, real, pltpu.roll(imag, HALF, 1))
        odd = jnp.where(low_half, pltpu.roll(real, HALF, 1), imag)
        block[pl.ds(2 * pair, FBLOCK, stride=ROWS), :] = even
        block[pl.ds(2 * pair + 1, FBLOCK, stride=ROWS), :] = odd
    own[pl.ds(step * FBLOCK, FBLOCK)] = block[...].reshape(FBLOCK, ROWS, 128).astype(jnp.bfloat16)


UNROLL = 13

ROWS_ALONG_X = (2,)
COLUMNS_ALONG_X = (1, 4)
SLACK = 2.5
LATER = 2


def transfer_order():
    unit, latency, twin = 15.7 / PARTS, 2.5, 4.0 / PARTS
    product, transform, turns = 12.7 * UNROLL / FREQS, 0.25 + 0.55 * EARLY_PARTS / PARTS, FREQS // PARTS // UNROLL
    rank = ("rel", "stp", "pro", "pco", "prp", "pcp", "cro", "cco", "ccp", "done")
    links_of = {"owx": "l", "owy": "y+", "owz": "z+"}
    acts = {}
    for part in range(PARTS):
        in_rows, in_columns = part in ROWS_ALONG_X, part in COLUMNS_ALONG_X

        def both(axis, stage, share):
            return [(link, stage + link, share * unit) for link in (axis + "+", axis + "-")]

        table = {
            "owx": ("", [("l", "l", unit), ("t", "t0", twin)]),
            "owy": ("", both("y", "o", 1)),
            "owz": ("", both("z", "o", 1)),
            "pro": ("oy+ oy-", both("y", "f", 0.5) + [("l c", "r1", 2 * unit)] * in_rows),
            "pco": ("oz+ oz-", both("z", "f", 0.5) + [("l", "c1", 2 * unit)] * in_columns + [("t", "t1", 2 * twin)]),
            "rel": ("l", [("c", "c", unit), ("t", "t2", twin)] + ([] if in_columns else both("z", "p", 1))),
            "stp": ("c", [] if in_rows else both("y", "p", 1)),
            "cco": ("fz+ fz-", [("l", "c2", unit)] * in_columns + [("t", "t4", twin)]),
        }
        if in_rows:
            table["cro"] = ("fy+ fy-", [("l c", "r2", unit)])
        else:
            table["prp"] = ("py+ py-", both("y", "q", 0.5))
        if in_columns:
            table["ccp"] = ("c1 c2", [("t", "t3", 3 * twin)])
        else:
            table["pcp"] = ("pz+ pz-", both("z", "q", 0.5) + [("t", "t3", 2 * twin)])
            table["ccp"] = ("qz+ qz-", [("t", "t5", twin)])
        ends = "fy+ fy- t0 t1 t2 t3 t4 " + ("r1 r2" if in_rows else "qy+ qy-") + ("" if in_columns else " t5")
        table["done"] = (ends, [])
        for name, (waits, issues) in table.items():
            acts[name, part] = ([(key, part) for key in waits.split()], issues)
    now, free, arrival, order, products, early, count = 0.0, {}, {}, [], [], [], 0

    def issue(act):
        for links, key, length in acts.pop(act)[1]:
            end = 0.0
            for link in links.split():
                free[link] = max(now, free.get(link, 0.0)) + length
                end = max(end, free[link])
            arrival[key, act[1]] = end + latency
        order.append(act)

    def extend(name, part, turn):
        if order[-1][:2] == (name, part):
            order[-1] = (name, part, order[-1][2], turn + 1)
        else:
            order.append((name, part, turn, turn + 1))

    while acts or products or early:
        known = []
        for act, (waits, _) in acts.items():
            name, part = act
            if name in links_of:
                if not any((name, other) in acts for other in range(part)):
                    place = part - 1 if name == "owx" else part + LATER
                    known.append((free.get(links_of[name], 0.0) - SLACK, (place, -1, act)))
            elif all(key in arrival for key in waits):
                known.append((max(arrival[key] for key in waits), (part, rank.index(name), act)))
        ready = [choice for when, choice in known if when <= now]
        if ready:
            act = min(ready)[2]
            issue(act)
            if act[0] == "done":
                products += [(act[1], turn) for turn in range(turns)]
        elif products:
            part, turn = products.pop(0)
            extend("mul", part, turn)
            now += product
            count += part < EARLY_PARTS
            if part < EARLY_PARTS and count == EARLY_PARTS * turns:
                early = list(range(SEG))
        elif early:
            extend("inv", 0, early.pop(0))
            now += transform
        else:
            now = min(when for when, _ in known)
    return order


def pairs_kernel(
    taps_ref, flags_hbm, traces_hbm, forward_hbm, early_hbm, late_hbm, out_ref, flags_ref, forward, early_ref, late_ref,
    padded, filtered, whitened, rows_ref, block, own_ref, left_ref, right_ref, cross, message, stage, early_sum,
    send_sem, recv_sem, local_sem, out_send, out_recv,
):
    loads = ((traces_hbm, padded.at[:, pl.ds(128, RECORD)]), (flags_hbm, flags_ref), (forward_hbm, forward))
    loads += ((early_hbm, early_ref), (late_hbm, late_ref))
    loads = [pltpu.make_async_copy(*pair, local_sem.at[2 + index]) for index, pair in enumerate(loads)]
    for copy in loads:
        copy.start()
    stn, seg = lax.axis_index("stn"), lax.axis_index("seg")
    core, z, x_lo = stn % 2, (stn // 2) % 4, stn // 8
    x_hi, y = seg % 2, seg // 2
    size = FREQS // PARTS
    half = size // 2

    def on_row(yy, hh):
        return (stn, (yy % 4) * 2 + hh)

    def on_column(zz, ll, cc):
        return ((ll * 4 + zz % 4) * 2 + cc, seg)

    def row_slot(yy, hh):
        return (yy % 4) * 2 + hh

    def column_slot(zz, ll, cc):
        return (ll * 4 + zz % 4) * 2 + cc

    across = (on_column(z, 1 - x_lo, core)[0], row_slot(y, 1 - x_hi))
    twin = on_column(z, x_lo, 1 - core)
    neighbours = [on_column(z + 1, x_lo, core), on_column(z + 3, x_lo, core), on_column(z, 1 - x_lo, core), twin, across]
    neighbours += [(stn, (seg + shift) % SEG) for shift in range(1, SEG)]
    barrier = pltpu.get_barrier_semaphore()
    for device in neighbours:
        pl.semaphore_signal(barrier, inc=1, device_id=device, device_id_type=MESH)

    def ready():
        loads[0].wait()
        loads[1].wait()

    whiten(taps_ref, flags_ref, padded, filtered, whitened, rows_ref, ready)
    samples = gathered_samples(rows_ref)
    loads[2].wait()
    spectrum(0, forward, samples, block, own_ref)
    pl.semaphore_wait(barrier, len(neighbours))

    started = []

    def send(kind, part, source, target, device):
        copy = pltpu.make_async_remote_copy(
            src_ref=source,
            dst_ref=target,
            send_sem=send_sem.at[part, kind],
            recv_sem=recv_sem.at[part, kind],
            device_id=device,
            device_id_type=MESH,
        )
        copy.start()
        started.append(copy)

    def arrive(kind, part, target):
        pltpu.make_async_remote_copy(
            src_ref=target,
            dst_ref=target,
            send_sem=send_sem.at[part, kind],
            recv_sem=recv_sem.at[part, kind],
            device_id=(stn, seg),
            device_id_type=MESH,
        ).wait_recv()

    def piece(ref, slot, part, which=None):
        first = part * size if which is None else part * size + which * half
        return ref.at[slot, pl.ds(first, size if which is None else half)]

    class Ring:
        def __init__(self, ref, slot, device, place, first):
            self.ref, self.slot, self.device, self.place, self.first = ref, slot, device, place, first

        def start(self, part, source, group, kind):
            slot = self.slot(self.place, group)
            for side, step in ((0, 1), (1, 3)):
                send(self.first + kind + side, part, source, piece(self.ref, slot, part), self.device(self.place + step))

        def pass_on(self, part, group, kind):
            for side, step in ((0, 3), (1, 1)):
                slot = self.slot(self.place + step, group)
                arrive(self.first + kind + side, part, piece(self.ref, slot, part))
                data = piece(self.ref, slot, part, side)
                send(self.first + kind + 2 + side, part, data, data, self.device(self.place + 4 - step))

        def finish(self, part, group, kind):
            slot = self.slot(self.place + 2, group)
            for side in (0, 1):
                arrive(self.first + kind + 2 + side, part, piece(self.ref, slot, part, side))

    rows = Ring(left_ref, row_slot, lambda yy: on_row(yy, x_hi), y, 0)
    columns = Ring(right_ref, lambda zz, ll: column_slot(zz, ll, core), lambda zz: on_column(zz, x_lo, core), z, 9)

    def share(kind, part, zz, ll):
        data = piece(right_ref, column_slot(zz, ll, core), part)
        send(kind, part, data, data, twin)

    beside = on_column(z, 1 - x_lo, core)

    def own_piece(part):
        return own_ref.at[pl.ds(part * size, size)]

    def start_rows(part):
        rows.start(part, own_piece(part), x_hi, 0)

    def start_columns(part):
        columns.start(part, own_piece(part), x_lo, 0)

    def start_beside(part):
        source = own_piece(part)
        own_column = piece(right_ref, column_slot(z, x_lo, core), part)
        send(17, part, source, own_column, beside)
        send(18, part, source, own_column, twin)

    def pass_along(kind, part, ref, slot, device):
        data = piece(ref, slot, part)
        send(kind, part, data, data, device)

    def pass_rows(part):
        rows.pass_on(part, x_hi, 0)
        if part in ROWS_ALONG_X:
            for kind, step in ((4, 3), (5, 1)):
                pass_along(kind, part, left_ref, row_slot(y + step, x_hi), on_row(y, 1 - x_hi))

    def pass_columns(part):
        columns.pass_on(part, x_lo, 0)
        if part in COLUMNS_ALONG_X:
            for kind, step in ((13, 3), (14, 1)):
                pass_along(kind, part, right_ref, column_slot(z + step, x_lo, core), beside)
        share(19, part, z + 3, x_lo)
        share(20, part, z + 1, x_lo)

    def relay(part):
        data = piece(right_ref, column_slot(z, 1 - x_lo, core), part)
        arrive(17, part, data)
        send(8, part, data, piece(left_ref, row_slot(y, x_hi), part), across)
        if part not in COLUMNS_ALONG_X:
            columns.start(part, data, 1 - x_lo, 4)
        share(22, part, z, 1 - x_lo)

    def start_partner(part):
        data = piece(left_ref, row_slot(y, 1 - x_hi), part)
        arrive(8, part, data)
        if part not in ROWS_ALONG_X:
            rows.start(part, data, 1 - x_hi, 4)

    def pass_partner_rows(part):
        rows.pass_on(part, 1 - x_hi, 4)

    def pass_partner_columns(part):
        columns.pass_on(part, 1 - x_lo, 4)
        share(23, part, z + 3, 1 - x_lo)
        share(24, part, z + 1, 1 - x_lo)

    def end_rows(part):
        rows.finish(part, x_hi, 0)
        pass_along(6, part, left_ref, row_slot(y + 2, x_hi), on_row(y, 1 - x_hi))

    def end_columns(part):
        columns.finish(part, x_lo, 0)
        if part in COLUMNS_ALONG_X:
            pass_along(15, part, right_ref, column_slot(z + 2, x_lo, core), beside)
        share(21, part, z + 2, x_lo)

    def end_partner_columns(part):
        if part in COLUMNS_ALONG_X:
            for kind, share_kind, step in ((13, 23, 3), (14, 24, 1), (15, 25, 2)):
                arrive(kind, part, piece(right_ref, column_slot(z + step, 1 - x_lo, core), part))
                share(share_kind, part, z + step, 1 - x_lo)
        else:
            columns.finish(part, 1 - x_lo, 4)
            share(25, part, z + 2, 1 - x_lo)

    def complete(part):
        if part in ROWS_ALONG_X:
            for kind, step in ((4, 3), (5, 1), (6, 2)):
                arrive(kind, part, piece(left_ref, row_slot(y + step, 1 - x_hi), part))
        else:
            rows.finish(part, x_hi, 0)
            rows.finish(part, 1 - x_hi, 4)
        order = ((18, 0, x_lo), (19, 3, x_lo), (20, 1, x_lo), (21, 2, x_lo))
        order += ((22, 0, 1 - x_lo), (23, 3, 1 - x_lo), (24, 1, 1 - x_lo), (25, 2, 1 - x_lo))
        for kind, step, ll in order:
            arrive(kind, part, piece(right_ref, column_slot(z + step, ll, 1 - core), part))

    def multiply(part, first, last):
        @pl.loop(first, last)
        def _(turn):
            for offset in range(UNROLL):
                index = part * size + turn * UNROLL + offset
                left = left_ref[:, index].reshape(LEFT, 128)
                right = right_ref[:, index].reshape(RIGHT, 128)
                turned = jnp.concatenate([-left[:, HALF:], left[:, :HALF]], axis=1)
                both = jnp.concatenate([left, turned], axis=0)
                product = lax.dot_general(right, both, (((1,), (1,)), ((), ())), preferred_element_type=jnp.float32)
                cross[pl.ds(pl.multiple_of(index * PITCH, 8), RIGHT), :] = product

    low_half = lax.broadcasted_iota(jnp.int32, (LAGPAD, 128), 1) < HALF

    def inverse(group, matrix_ref, first, last, into):
        def lagged(row):
            values = cross[pl.ds(first * PITCH + row, last - first, stride=PITCH), :].astype(jnp.bfloat16)
            parts = jnp.dot(matrix_ref[...], values, preferred_element_type=jnp.float32)
            return parts[:LAGPAD], parts[LAGPAD:]

        for row in range(ROWS):
            first_re, first_im = lagged(group * (2 * ROWS) + row)
            second_re, second_im = lagged(group * (2 * ROWS) + ROWS + row)
            straight = jnp.where(low_half, first_re, second_im)
            crossed = jnp.where(low_half, second_re, first_im)
            into[pl.ds(row, LAGPAD, stride=ROWS), :] = straight + pltpu.roll(crossed, HALF, 1)

    def transform_early(first, last):
        @pl.loop(first, last)
        def _(group):
            inverse(group, early_ref, 0, EARLY, early_sum.at[group])

    actions = {
        "owx": start_beside,
        "owy": start_rows,
        "owz": start_columns,
        "pro": pass_rows,
        "pco": pass_columns,
        "rel": relay,
        "stp": start_partner,
        "prp": pass_partner_rows,
        "pcp": pass_partner_columns,
        "cro": end_rows,
        "cco": end_columns,
        "ccp": end_partner_columns,
        "done": complete,
    }
    per = PARTS // FBLOCKS
    blocks_done = 1
    locals_ = []
    for name, part, *turns in transfer_order():
        needed = part // per + 1 if name in ("owx", "owy", "owz") else FBLOCKS
        while blocks_done < needed:
            spectrum(blocks_done, forward, samples, block, own_ref)
            blocks_done += 1
            if blocks_done == FBLOCKS:
                loads[3].wait()
                loads[4].wait()
                for index, target in enumerate(
                    (left_ref.at[row_slot(y, x_hi)], right_ref.at[column_slot(z, x_lo, core)])
                ):
                    copy = pltpu.make_async_copy(own_ref, target, local_sem.at[index])
                    copy.start()
                    locals_.append(copy)
        if name == "mul":
            if locals_:
                locals_.pop().wait()
                locals_.pop().wait()
            multiply(part, *turns)
        elif name == "inv":
            transform_early(*turns)
        else:
            actions[name](part)

    def peer_of(turn, sign):
        if isinstance(turn, int):
            along_y, along_x = ((2, 1), (2, 0), (1, 1), (3, 1), (0, 1), (1, 0), (3, 0))[turn]
        else:
            odd = jnp.where((turn == 2) | (turn == 5), 1, jnp.where(turn == 4, 0, 3))
            along_y = jnp.where(turn < 2, 2, odd)
            along_x = jnp.where((turn == 0) | ((turn >= 2) & (turn <= 4)), 1, 0)
        return ((y + 4 + sign * along_y) % 4) * 2 + (x_hi + along_x) % 2

    def hand_over(turn):
        peer = peer_of(turn, 1)
        return pltpu.make_async_remote_copy(
            src_ref=message.at[peer],
            dst_ref=out_ref.at[seg],
            send_sem=out_send.at[turn],
            recv_sem=out_recv.at[turn],
            device_id=(stn, peer),
            device_id_type=MESH,
        )

    def transform(group):
        inverse(group, late_ref, EARLY, FREQS, stage)
        both = stage[: LAGS * ROWS, :] + early_sum[group, : LAGS * ROWS, :]
        return both.reshape(LAGS, ROWS, 128).astype(jnp.bfloat16)

    @pl.loop(0, SEG - 1)
    def _(turn):
        group = peer_of(turn, 1)
        message[group] = transform(group)

        @pl.when(turn > 0)
        def _():
            hand_over(turn - 1).start()

    message[seg] = transform(seg)
    hand_over(SEG - 2).start()
    keep = pltpu.make_async_copy(message.at[seg], out_ref.at[seg], local_sem.at[7])
    keep.start()
    for copy in started:
        copy.wait_send()
    for turn in range(SEG - 1):
        slot = out_ref.at[peer_of(turn, -1)]
        pltpu.make_async_remote_copy(
            src_ref=slot,
            dst_ref=slot,
            send_sem=out_send.at[turn],
            recv_sem=out_recv.at[turn],
            device_id=(stn, seg),
            device_id_type=MESH,
        ).wait_recv()
        hand_over(turn).wait_send()
    keep.wait()


def pairs(traces, fir_taps, seg_flags):
    result = (SEG, LAGS, ROWS, 128)
    spectra = (FREQS, ROWS, 128)
    forward = forward_matrix()
    early, late = inverse_matrix()
    return pl.pallas_call(
        pairs_kernel,
        out_shape=jax.ShapeDtypeStruct(result, jnp.bfloat16),
        in_specs=[pl.BlockSpec(memory_space=pltpu.SMEM), HBM, HBM, HBM, HBM, HBM],
        out_specs=HBM,
        scratch_shapes=[
            pltpu.VMEM((ROWS, SEGS), jnp.int32),
            pltpu.VMEM(forward.shape, jnp.bfloat16),
            pltpu.VMEM(early.shape, jnp.bfloat16),
            pltpu.VMEM(late.shape, jnp.bfloat16),
            pltpu.VMEM((ROWS, RECORD + 256), jnp.float32),
            pltpu.VMEM((ROWS, RECORD + 256), jnp.float32),
            pltpu.VMEM((ROWS, RECORD + 128), jnp.float32),
            pltpu.VMEM((PADDED // 128, ROWS * SEGPITCH, 128), jnp.float32),
            pltpu.VMEM((FBLOCK * ROWS, 128), jnp.float32),
            pltpu.VMEM(spectra, jnp.bfloat16),
            pltpu.VMEM((SEG,) + spectra, jnp.bfloat16),
            pltpu.VMEM((STN,) + spectra, jnp.bfloat16),
            pltpu.VMEM((FREQS * PITCH, 128), jnp.float32),
            pltpu.VMEM(result, jnp.bfloat16),
            pltpu.VMEM((LAGPAD * ROWS, 128), jnp.float32),
            pltpu.VMEM((SEG, LAGPAD * ROWS, 128), jnp.float32),
            pltpu.SemaphoreType.DMA((PARTS, 26)),
            pltpu.SemaphoreType.DMA((PARTS, 26)),
            pltpu.SemaphoreType.DMA((8,)),
            pltpu.SemaphoreType.DMA((SEG,)),
            pltpu.SemaphoreType.DMA((SEG,)),
        ],
        compiler_params=pltpu.CompilerParams(collective_id=0, has_side_effects=True, vmem_limit_bytes=60 << 20),
        name="pairs",
    )(fir_taps, seg_flags, traces, jnp.asarray(forward), jnp.asarray(early), jnp.asarray(late))


def finish_kernel(values_ref, mask_ref, out_ref, buffer, sem):
    keep = mask_ref[...].astype(jnp.float32)
    place = lax.broadcasted_iota(jnp.int32, (LEFT, 128), 1) % LEFT
    pick = jnp.where(place == lax.broadcasted_iota(jnp.int32, (LEFT, 128), 0), 1.0, 0.0).astype(jnp.bfloat16)
    first = lax.broadcasted_iota(jnp.int32, (LEFT, 128), 1) < LEFT
    copies = []
    for start in range(0, LAGS, 8):
        stop = min(start + 8, LAGS)
        for lag in range(start, stop):
            values = values_ref[:, lag].astype(jnp.float32).reshape(LEFT, 128)
            spread = jnp.concatenate([jnp.where(first, values, 0.0), jnp.where(first, 0.0, values)], axis=0)
            turned = lax.dot_general(
                pick, spread.astype(jnp.bfloat16), (((1,), (1,)), ((), ())), preferred_element_type=jnp.float32
            )
            buffer[lag] = turned * keep
        copy = pltpu.make_async_copy(
            buffer.at[pl.ds(start, stop - start)], out_ref.at[pl.ds(start, stop - start)], sem.at[start // 8]
        )
        copy.start()
        copies.append(copy)
    for copy in copies:
        copy.wait()


def finish(values, pair_mask):
    shape = (LAGS, LEFT, RIGHT)
    return pl.pallas_call(
        finish_kernel,
        out_shape=jax.ShapeDtypeStruct(shape, jnp.float32),
        in_specs=[VMEM, VMEM],
        out_specs=HBM,
        scratch_shapes=[pltpu.VMEM(shape, jnp.float32), pltpu.SemaphoreType.DMA((6,))],
        name="finish",
    )(values, pair_mask)


def body(traces, fir_taps, seg_flags, pair_mask):
    return finish(pairs(traces, fir_taps, seg_flags), pair_mask)


def solution(mesh):
    return jax.shard_map(
        body,
        mesh=mesh,
        in_specs=(P(("stn", "seg"), None), P(), P(("stn", "seg"), None), P("stn", "seg")),
        out_specs=P(None, "stn", "seg"),
        check_vma=False,
    )
```

```python
import functools
import math

import jax
import jax.numpy as jnp
import numpy as np
from jax import lax
from jax.experimental import pallas as pl
from jax.experimental.pallas import tpu as pltpu
from jax.sharding import PartitionSpec as P

SAMP = 600
LAGS = 41
TAPS = 31
RADIUS = 64
SEGS = 64
ROWS = 8
EPS = 1e-06

LENGTH = 624
PADDED = 640
FREQS = LENGTH // 2
HALF = SEGS
FBLOCK = 104
FBLOCKS = FREQS // FBLOCK
LAGPAD = 48
PITCH = 136

RECORD = SEGS * SAMP
BLOCKS = RECORD // 128
PER = 100
SEGPITCH = SEGS + 8

STN, SEG = 16, 8
LEFT = ROWS * SEG
RIGHT = ROWS * STN
PARTS = 6

EARLY_PARTS = 2
EARLY = EARLY_PARTS * FREQS // PARTS

MESH = pl.DeviceIdType.MESH
VMEM = pl.BlockSpec(memory_space=pltpu.VMEM)
HBM = pl.BlockSpec(memory_space=pltpu.HBM)


def split_bf16(values):
    high = np.asarray(values, np.float32).astype(jnp.bfloat16)
    low = (np.asarray(values, np.float64) - high.astype(np.float64)).astype(np.float32).astype(jnp.bfloat16)
    return high, low


def frequencies():
    return (np.arange(FREQS) + 0.5) * (2 * np.pi / LENGTH)


def forward_matrix():
    angle = frequencies()[:, None] * np.arange(PADDED)[None, :]
    keep = (np.arange(PADDED) < SAMP)[None, :]
    stacked = np.stack([split_bf16(part * keep)[0] for part in (np.cos(angle), -np.sin(angle))])
    stacked = stacked.reshape(2, FBLOCKS, FBLOCK, PADDED).transpose(1, 0, 2, 3)
    return np.ascontiguousarray(stacked.reshape(FBLOCKS, 2 * FBLOCK, PADDED))


def inverse_matrix():
    lag = np.arange(LAGS) - (LAGS - 1) // 2
    angle = lag[:, None] * frequencies()[None, :]
    padded = np.zeros((2, LAGPAD, FREQS))
    padded[0, :LAGS] = np.cos(angle)
    padded[1, :LAGS] = -np.sin(angle)
    padded *= 2.0 / LENGTH / math.sqrt(RECORD)
    whole = split_bf16(padded.reshape(2 * LAGPAD, FREQS))[0]
    return [np.ascontiguousarray(piece) for piece in np.split(whole, [EARLY], axis=1)]


def whiten(taps_ref, flags_ref, padded, filtered, whitened, rows, ready):
    edge = jnp.zeros((ROWS, 128), jnp.float32)
    padded[:, 0:128] = edge
    padded[:, 128 + RECORD : 256 + RECORD] = edge
    filtered[:, 0:128] = edge
    filtered[:, 128 + RECORD : 256 + RECORD] = edge
    whitened[:, RECORD : RECORD + 128] = edge

    offset = lax.broadcasted_iota(jnp.int32, (384, 128), 0) - lax.broadcasted_iota(jnp.int32, (384, 128), 1)
    band = jnp.zeros((384, 128), jnp.float32)
    for tap in range(TAPS):
        band = jnp.where(offset == 128 - (TAPS - 1) // 2 + tap, taps_ref[tap], band)
    band_high = band.astype(jnp.bfloat16)
    band_low = (band - band_high.astype(jnp.float32)).astype(jnp.bfloat16)
    box = jnp.where((offset >= 128 - RADIUS) & (offset <= 128 + RADIUS), 1.0, 0.0).astype(jnp.bfloat16)

    def side_by_side(matrix):
        return jnp.concatenate([matrix[:128], matrix[128:256], matrix[256:]], axis=1)

    band_high, band_low, box = side_by_side(band_high), side_by_side(band_low), side_by_side(box)
    band_twice = jnp.concatenate([band_high, band_high], axis=0)
    box_twice = jnp.concatenate([box, box], axis=0)

    def blocks(ref, start):
        window = ref[:, pl.ds(start, (PER + 2) * 128)]
        return jnp.concatenate([window[:, 128 * i : 128 * i + 128] for i in range(PER + 2)], axis=0)

    def halves(values):
        high = values.astype(jnp.bfloat16)
        return jnp.concatenate([high, (values - high.astype(jnp.float32)).astype(jnp.bfloat16)], axis=1)

    def over_neighbours(parts):
        size = ROWS * PER
        shifted = [parts[ROWS * i : ROWS * i + size, 128 * i : 128 * i + 128] for i in range(3)]
        return shifted[0] + shifted[1] + shifted[2]

    def product(left, right):
        return jnp.dot(left, right, preferred_element_type=jnp.float32)

    def place(ref, start, values):
        for i in range(PER):
            ref[:, pl.ds(pl.multiple_of(start + 128 * i, 128), 128)] = values[ROWS * i : ROWS * (i + 1)]

    ready()

    @pl.loop(0, BLOCKS // PER)
    def _(chunk):
        start = pl.multiple_of(chunk * (PER * 128), 128)
        both = halves(blocks(padded, start))
        total = over_neighbours(product(both, band_twice) + product(both[:, :128], band_low))
        place(filtered, start + 128, total)

    @pl.loop(0, BLOCKS // PER)
    def _(chunk):
        start = pl.multiple_of(chunk * (PER * 128), 128)
        values = blocks(filtered, start)
        level = over_neighbours(product(halves(jnp.abs(values)), box_twice)) / (2 * RADIUS + 1)
        place(whitened, start, values[ROWS : ROWS * (PER + 1)] / (level + EPS))

    flags = flags_ref[...].astype(jnp.float32)
    for seg in range(SEGS):
        piece = whitened[:, seg * SAMP : seg * SAMP + PADDED] * flags[:, seg : seg + 1]
        for part in range(PADDED // 128):
            rows[part, pl.ds(seg, ROWS, stride=SEGPITCH), :] = piece[:, part * 128 : part * 128 + 128]


def gathered_samples(rows):
    columns = []
    for part in range(PADDED // 128):
        pieces = [rows[part, SEGPITCH * row : SEGPITCH * row + SEGS, :] for row in range(ROWS)]
        columns.append(jnp.concatenate(pieces, axis=0))
    return jnp.concatenate(columns, axis=1).astype(jnp.bfloat16)


def spectrum(step, forward, samples, block, own):
    low_half = lax.broadcasted_iota(jnp.int32, (FBLOCK, 128), 1) < HALF
    both = lax.dot_general(forward[step], samples, (((1,), (1,)), ((), ())), preferred_element_type=jnp.float32)
    for pair in range(ROWS // 2):
        real = both[:FBLOCK, pair * 128 : pair * 128 + 128]
        imag = both[FBLOCK:, pair * 128 : pair * 128 + 128]
        even = jnp.where(low_half, real, pltpu.roll(imag, HALF, 1))
        odd = jnp.where(low_half, pltpu.roll(real, HALF, 1), imag)
        block[pl.ds(2 * pair, FBLOCK, stride=ROWS), :] = even
        block[pl.ds(2 * pair + 1, FBLOCK, stride=ROWS), :] = odd
    own[pl.ds(step * FBLOCK, FBLOCK)] = block[...].reshape(FBLOCK, ROWS, 128).astype(jnp.bfloat16)


UNROLL = 13

ROWS_ALONG_X = (2,)
COLUMNS_ALONG_X = (1, 4)
SLACK = 2.5
LATER = 2


def transfer_order():
    unit, latency, twin = 15.7 / PARTS, 2.5, 4.0 / PARTS
    product, transform, turns = 12.7 * UNROLL / FREQS, 0.25 + 0.55 * EARLY_PARTS / PARTS, FREQS // PARTS // UNROLL
    rank = ("rel", "stp", "pro", "pco", "prp", "pcp", "cro", "cco", "ccp", "done")
    links_of = {"owx": "l", "owy": "y+", "owz": "z+"}
    acts = {}
    for part in range(PARTS):
        in_rows, in_columns = part in ROWS_ALONG_X, part in COLUMNS_ALONG_X

        def both(axis, stage, share):
            return [(link, stage + link, share * unit) for link in (axis + "+", axis + "-")]

        table = {
            "owx": ("", [("l", "l", unit), ("t", "t0", twin)]),
            "owy": ("", both("y", "o", 1)),
            "owz": ("", both("z", "o", 1)),
            "pro": ("oy+ oy-", both("y", "f", 0.5) + [("l c", "r1", 2 * unit)] * in_rows),
            "pco": ("oz+ oz-", both("z", "f", 0.5) + [("l", "c1", 2 * unit)] * in_columns + [("t", "t1", 2 * twin)]),
            "rel": ("l", [("c", "c", unit), ("t", "t2", twin)] + ([] if in_columns else both("z", "p", 1))),
            "stp": ("c", [] if in_rows else both("y", "p", 1)),
            "cco": ("fz+ fz-", [("l", "c2", unit)] * in_columns + [("t", "t4", twin)]),
        }
        if in_rows:
            table["cro"] = ("fy+ fy-", [("l c", "r2", unit)])
        else:
            table["prp"] = ("py+ py-", both("y", "q", 0.5))
        if in_columns:
            table["ccp"] = ("c1 c2", [("t", "t3", 3 * twin)])
        else:
            table["pcp"] = ("pz+ pz-", both("z", "q", 0.5) + [("t", "t3", 2 * twin)])
            table["ccp"] = ("qz+ qz-", [("t", "t5", twin)])
        ends = "fy+ fy- t0 t1 t2 t3 t4 " + ("r1 r2" if in_rows else "qy+ qy-") + ("" if in_columns else " t5")
        table["done"] = (ends, [])
        for name, (waits, issues) in table.items():
            acts[name, part] = ([(key, part) for key in waits.split()], issues)
    now, free, arrival, order, products, early, count = 0.0, {}, {}, [], [], [], 0

    def issue(act):
        for links, key, length in acts.pop(act)[1]:
            end = 0.0
            for link in links.split():
                free[link] = max(now, free.get(link, 0.0)) + length
                end = max(end, free[link])
            arrival[key, act[1]] = end + latency
        order.append(act)

    def extend(name, part, turn):
        if order[-1][:2] == (name, part):
            order[-1] = (name, part, order[-1][2], turn + 1)
        else:
            order.append((name, part, turn, turn + 1))

    while acts or products or early:
        known = []
        for act, (waits, _) in acts.items():
            name, part = act
            if name in links_of:
                if not any((name, other) in acts for other in range(part)):
                    place = part - 1 if name == "owx" else part + LATER
                    known.append((free.get(links_of[name], 0.0) - SLACK, (place, -1, act)))
            elif all(key in arrival for key in waits):
                known.append((max(arrival[key] for key in waits), (part, rank.index(name), act)))
        ready = [choice for when, choice in known if when <= now]
        if ready:
            act = min(ready)[2]
            issue(act)
            if act[0] == "done":
                products += [(act[1], turn) for turn in range(turns)]
        elif products:
            part, turn = products.pop(0)
            extend("mul", part, turn)
            now += product
            count += part < EARLY_PARTS
            if part < EARLY_PARTS and count == EARLY_PARTS * turns:
                early = list(range(SEG))
        elif early:
            extend("inv", 0, early.pop(0))
            now += transform
        else:
            now = min(when for when, _ in known)
    return order


def pairs_kernel(
    taps_ref, flags_hbm, traces_hbm, forward_hbm, early_hbm, late_hbm, out_ref, flags_ref, forward, early_ref, late_ref,
    padded, filtered, whitened, rows_ref, block, own_ref, left_ref, right_ref, cross, message, stage, early_sum,
    send_sem, recv_sem, local_sem, out_send, out_recv,
):
    loads = ((traces_hbm, padded.at[:, pl.ds(128, RECORD)]), (flags_hbm, flags_ref), (forward_hbm, forward))
    loads += ((early_hbm, early_ref), (late_hbm, late_ref))
    loads = [pltpu.make_async_copy(*pair, local_sem.at[2 + index]) for index, pair in enumerate(loads)]
    for copy in loads:
        copy.start()
    stn, seg = lax.axis_index("stn"), lax.axis_index("seg")
    core, z, x_lo = stn % 2, (stn // 2) % 4, stn // 8
    x_hi, y = seg % 2, seg // 2
    size = FREQS // PARTS
    half = size // 2

    def on_row(yy, hh):
        return (stn, (yy % 4) * 2 + hh)

    def on_column(zz, ll, cc):
        return ((ll * 4 + zz % 4) * 2 + cc, seg)

    def row_slot(yy, hh):
        return (yy % 4) * 2 + hh

    def column_slot(zz, ll, cc):
        return (ll * 4 + zz % 4) * 2 + cc

    across = (on_column(z, 1 - x_lo, core)[0], row_slot(y, 1 - x_hi))
    twin = on_column(z, x_lo, 1 - core)
    neighbours = [on_column(z + 1, x_lo, core), on_column(z + 3, x_lo, core), on_column(z, 1 - x_lo, core), twin, across]
    neighbours += [(stn, (seg + shift) % SEG) for shift in range(1, SEG)]
    barrier = pltpu.get_barrier_semaphore()
    for device in neighbours:
        pl.semaphore_signal(barrier, inc=1, device_id=device, device_id_type=MESH)

    def ready():
        loads[0].wait()
        loads[1].wait()

    whiten(taps_ref, flags_ref, padded, filtered, whitened, rows_ref, ready)
    samples = gathered_samples(rows_ref)
    loads[2].wait()
    spectrum(0, forward, samples, block, own_ref)
    pl.semaphore_wait(barrier, len(neighbours))

    started = []

    def send(kind, part, source, target, device):
        copy = pltpu.make_async_remote_copy(
            src_ref=source,
            dst_ref=target,
            send_sem=send_sem.at[part, kind],
            recv_sem=recv_sem.at[part, kind],
            device_id=device,
            device_id_type=MESH,
        )
        copy.start()
        started.append(copy)

    def arrive(kind, part, target):
        pltpu.make_async_remote_copy(
            src_ref=target,
            dst_ref=target,
            send_sem=send_sem.at[part, kind],
            recv_sem=recv_sem.at[part, kind],
            device_id=(stn, seg),
            device_id_type=MESH,
        ).wait_recv()

    def piece(ref, slot, part, which=None):
        first = part * size if which is None else part * size + which * half
        return ref.at[slot, pl.ds(first, size if which is None else half)]

    class Ring:
        def __init__(self, ref, slot, device, place, first):
            self.ref, self.slot, self.device, self.place, self.first = ref, slot, device, place, first

        def start(self, part, source, group, kind):
            slot = self.slot(self.place, group)
            for side, step in ((0, 1), (1, 3)):
                send(self.first + kind + side, part, source, piece(self.ref, slot, part), self.device(self.place + step))

        def pass_on(self, part, group, kind):
            for side, step in ((0, 3), (1, 1)):
                slot = self.slot(self.place + step, group)
                arrive(self.first + kind + side, part, piece(self.ref, slot, part))
                data = piece(self.ref, slot, part, side)
                send(self.first + kind + 2 + side, part, data, data, self.device(self.place + 4 - step))

        def finish(self, part, group, kind):
            slot = self.slot(self.place + 2, group)
            for side in (0, 1):
                arrive(self.first + kind + 2 + side, part, piece(self.ref, slot, part, side))

    rows = Ring(left_ref, row_slot, lambda yy: on_row(yy, x_hi), y, 0)
    columns = Ring(right_ref, lambda zz, ll: column_slot(zz, ll, core), lambda zz: on_column(zz, x_lo, core), z, 9)

    def share(kind, part, zz, ll):
        data = piece(right_ref, column_slot(zz, ll, core), part)
        send(kind, part, data, data, twin)

    beside = on_column(z, 1 - x_lo, core)

    def own_piece(part):
        return own_ref.at[pl.ds(part * size, size)]

    def start_rows(part):
        rows.start(part, own_piece(part), x_hi, 0)

    def start_columns(part):
        columns.start(part, own_piece(part), x_lo, 0)

    def start_beside(part):
        source = own_piece(part)
        own_column = piece(right_ref, column_slot(z, x_lo, core), part)
        send(17, part, source, own_column, beside)
        send(18, part, source, own_column, twin)

    def pass_along(kind, part, ref, slot, device):
        data = piece(ref, slot, part)
        send(kind, part, data, data, device)

    def pass_rows(part):
        rows.pass_on(part, x_hi, 0)
        if part in ROWS_ALONG_X:
            for kind, step in ((4, 3), (5, 1)):
                pass_along(kind, part, left_ref, row_slot(y + step, x_hi), on_row(y, 1 - x_hi))

    def pass_columns(part):
        columns.pass_on(part, x_lo, 0)
        if part in COLUMNS_ALONG_X:
            for kind, step in ((13, 3), (14, 1)):
                pass_along(kind, part, right_ref, column_slot(z + step, x_lo, core), beside)
        share(19, part, z + 3, x_lo)
        share(20, part, z + 1, x_lo)

    def relay(part):
        data = piece(right_ref, column_slot(z, 1 - x_lo, core), part)
        arrive(17, part, data)
        send(8, part, data, piece(left_ref, row_slot(y, x_hi), part), across)
        if part not in COLUMNS_ALONG_X:
            columns.start(part, data, 1 - x_lo, 4)
        share(22, part, z, 1 - x_lo)

    def start_partner(part):
        data = piece(left_ref, row_slot(y, 1 - x_hi), part)
        arrive(8, part, data)
        if part not in ROWS_ALONG_X:
            rows.start(part, data, 1 - x_hi, 4)

    def pass_partner_rows(part):
        rows.pass_on(part, 1 - x_hi, 4)

    def pass_partner_columns(part):
        columns.pass_on(part, 1 - x_lo, 4)
        share(23, part, z + 3, 1 - x_lo)
        share(24, part, z + 1, 1 - x_lo)

    def end_rows(part):
        rows.finish(part, x_hi, 0)
        pass_along(6, part, left_ref, row_slot(y + 2, x_hi), on_row(y, 1 - x_hi))

    def end_columns(part):
        columns.finish(part, x_lo, 0)
        if part in COLUMNS_ALONG_X:
            pass_along(15, part, right_ref, column_slot(z + 2, x_lo, core), beside)
        share(21, part, z + 2, x_lo)

    def end_partner_columns(part):
        if part in COLUMNS_ALONG_X:
            for kind, share_kind, step in ((13, 23, 3), (14, 24, 1), (15, 25, 2)):
                arrive(kind, part, piece(right_ref, column_slot(z + step, 1 - x_lo, core), part))
                share(share_kind, part, z + step, 1 - x_lo)
        else:
            columns.finish(part, 1 - x_lo, 4)
            share(25, part, z + 2, 1 - x_lo)

    def complete(part):
        if part in ROWS_ALONG_X:
            for kind, step in ((4, 3), (5, 1), (6, 2)):
                arrive(kind, part, piece(left_ref, row_slot(y + step, 1 - x_hi), part))
        else:
            rows.finish(part, x_hi, 0)
            rows.finish(part, 1 - x_hi, 4)
        order = ((18, 0, x_lo), (19, 3, x_lo), (20, 1, x_lo), (21, 2, x_lo))
        order += ((22, 0, 1 - x_lo), (23, 3, 1 - x_lo), (24, 1, 1 - x_lo), (25, 2, 1 - x_lo))
        for kind, step, ll in order:
            arrive(kind, part, piece(right_ref, column_slot(z + step, ll, 1 - core), part))

    def multiply(part, first, last):
        @pl.loop(first, last)
        def _(turn):
            for offset in range(UNROLL):
                index = part * size + turn * UNROLL + offset
                left = left_ref[:, index].reshape(LEFT, 128)
                right = right_ref[:, index].reshape(RIGHT, 128)
                turned = jnp.concatenate([-left[:, HALF:], left[:, :HALF]], axis=1)
                both = jnp.concatenate([left, turned], axis=0)
                product = lax.dot_general(right, both, (((1,), (1,)), ((), ())), preferred_element_type=jnp.float32)
                cross[pl.ds(pl.multiple_of(index * PITCH, 8), RIGHT), :] = product

    low_half = lax.broadcasted_iota(jnp.int32, (LAGPAD, 128), 1) < HALF

    def inverse(group, matrix_ref, first, last, into, after_first=lambda: None):
        def lagged(row):
            values = cross[pl.ds(first * PITCH + row, last - first, stride=PITCH), :].astype(jnp.bfloat16)
            parts = jnp.dot(matrix_ref[...], values, preferred_element_type=jnp.float32)
            return parts[:LAGPAD], parts[LAGPAD:]

        for row in range(ROWS):
            first_re, first_im = lagged(group * (2 * ROWS) + row)
            second_re, second_im = lagged(group * (2 * ROWS) + ROWS + row)
            straight = jnp.where(low_half, first_re, second_im)
            crossed = jnp.where(low_half, second_re, first_im)
            into[pl.ds(row, LAGPAD, stride=ROWS), :] = straight + pltpu.roll(crossed, HALF, 1)
            if row == 1:
                after_first()

    def transform_early(first, last):
        @pl.loop(first, last)
        def _(group):
            inverse(group, early_ref, 0, EARLY, early_sum.at[group])

    actions = {
        "owx": start_beside,
        "owy": start_rows,
        "owz": start_columns,
        "pro": pass_rows,
        "pco": pass_columns,
        "rel": relay,
        "stp": start_partner,
        "prp": pass_partner_rows,
        "pcp": pass_partner_columns,
        "cro": end_rows,
        "cco": end_columns,
        "ccp": end_partner_columns,
        "done": complete,
    }
    per = PARTS // FBLOCKS
    blocks_done = 1
    locals_ = []
    for name, part, *turns in transfer_order():
        needed = part // per + 1 if name in ("owx", "owy", "owz") else FBLOCKS
        while blocks_done < needed:
            spectrum(blocks_done, forward, samples, block, own_ref)
            blocks_done += 1
            if blocks_done == FBLOCKS:
                loads[3].wait()
                loads[4].wait()
                for index, target in enumerate(
                    (left_ref.at[row_slot(y, x_hi)], right_ref.at[column_slot(z, x_lo, core)])
                ):
                    copy = pltpu.make_async_copy(own_ref, target, local_sem.at[index])
                    copy.start()
                    locals_.append(copy)
        if name == "mul":
            if locals_:
                locals_.pop().wait()
                locals_.pop().wait()
            multiply(part, *turns)
        elif name == "inv":
            transform_early(*turns)
        else:
            actions[name](part)

    def peer_of(turn, sign):
        if isinstance(turn, int):
            along_y, along_x = ((2, 1), (2, 0), (1, 1), (3, 1), (0, 1), (1, 0), (3, 0))[turn]
        else:
            odd = jnp.where((turn == 2) | (turn == 5), 1, jnp.where(turn == 4, 0, 3))
            along_y = jnp.where(turn < 2, 2, odd)
            along_x = jnp.where((turn == 0) | ((turn >= 2) & (turn <= 4)), 1, 0)
        return ((y + 4 + sign * along_y) % 4) * 2 + (x_hi + along_x) % 2

    def hand_over(turn):
        peer = peer_of(turn, 1)
        return pltpu.make_async_remote_copy(
            src_ref=message.at[peer],
            dst_ref=out_ref.at[seg],
            send_sem=out_send.at[turn],
            recv_sem=out_recv.at[turn],
            device_id=(stn, peer),
            device_id_type=MESH,
        )

    def transform(group, after_first):
        inverse(group, late_ref, EARLY, FREQS, stage, after_first)
        both = stage[: LAGS * ROWS, :] + early_sum[group, : LAGS * ROWS, :]
        return both.reshape(LAGS, ROWS, 128).astype(jnp.bfloat16)

    @pl.loop(0, SEG - 1)
    def _(turn):
        group = peer_of(turn, 1)

        def send_last():
            @pl.when(turn > 0)
            def _():
                hand_over(turn - 1).start()

        message[group] = transform(group, send_last)

    message[seg] = transform(seg, lambda: hand_over(SEG - 2).start())
    keep = pltpu.make_async_copy(message.at[seg], out_ref.at[seg], local_sem.at[7])
    keep.start()
    for copy in started:
        copy.wait_send()
    for turn in range(SEG - 1):
        slot = out_ref.at[peer_of(turn, -1)]
        pltpu.make_async_remote_copy(
            src_ref=slot,
            dst_ref=slot,
            send_sem=out_send.at[turn],
            recv_sem=out_recv.at[turn],
            device_id=(stn, seg),
            device_id_type=MESH,
        ).wait_recv()
        hand_over(turn).wait_send()
    keep.wait()


def pairs(traces, fir_taps, seg_flags):
    result = (SEG, LAGS, ROWS, 128)
    spectra = (FREQS, ROWS, 128)
    forward = forward_matrix()
    early, late = inverse_matrix()
    return pl.pallas_call(
        pairs_kernel,
        out_shape=jax.ShapeDtypeStruct(result, jnp.bfloat16),
        in_specs=[pl.BlockSpec(memory_space=pltpu.SMEM), HBM, HBM, HBM, HBM, HBM],
        out_specs=HBM,
        scratch_shapes=[
            pltpu.VMEM((ROWS, SEGS), jnp.int32),
            pltpu.VMEM(forward.shape, jnp.bfloat16),
            pltpu.VMEM(early.shape, jnp.bfloat16),
            pltpu.VMEM(late.shape, jnp.bfloat16),
            pltpu.VMEM((ROWS, RECORD + 256), jnp.float32),
            pltpu.VMEM((ROWS, RECORD + 256), jnp.float32),
            pltpu.VMEM((ROWS, RECORD + 128), jnp.float32),
            pltpu.VMEM((PADDED // 128, ROWS * SEGPITCH, 128), jnp.float32),
            pltpu.VMEM((FBLOCK * ROWS, 128), jnp.float32),
            pltpu.VMEM(spectra, jnp.bfloat16),
            pltpu.VMEM((SEG,) + spectra, jnp.bfloat16),
            pltpu.VMEM((STN,) + spectra, jnp.bfloat16),
            pltpu.VMEM((FREQS * PITCH, 128), jnp.float32),
            pltpu.VMEM(result, jnp.bfloat16),
            pltpu.VMEM((LAGPAD * ROWS, 128), jnp.float32),
            pltpu.VMEM((SEG, LAGPAD * ROWS, 128), jnp.float32),
            pltpu.SemaphoreType.DMA((PARTS, 26)),
            pltpu.SemaphoreType.DMA((PARTS, 26)),
            pltpu.SemaphoreType.DMA((8,)),
            pltpu.SemaphoreType.DMA((SEG,)),
            pltpu.SemaphoreType.DMA((SEG,)),
        ],
        compiler_params=pltpu.CompilerParams(collective_id=0, has_side_effects=True, vmem_limit_bytes=60 << 20),
        name="pairs",
    )(fir_taps, seg_flags, traces, jnp.asarray(forward), jnp.asarray(early), jnp.asarray(late))


def finish_kernel(values_ref, mask_ref, out_ref, buffer, sem):
    keep = mask_ref[...].astype(jnp.float32)
    place = lax.broadcasted_iota(jnp.int32, (LEFT, 128), 1) % LEFT
    pick = jnp.where(place == lax.broadcasted_iota(jnp.int32, (LEFT, 128), 0), 1.0, 0.0).astype(jnp.bfloat16)
    first = lax.broadcasted_iota(jnp.int32, (LEFT, 128), 1) < LEFT
    copies = []
    for start in range(0, LAGS, 8):
        stop = min(start + 8, LAGS)
        for lag in range(start, stop):
            values = values_ref[:, lag].astype(jnp.float32).reshape(LEFT, 128)
            spread = jnp.concatenate([jnp.where(first, values, 0.0), jnp.where(first, 0.0, values)], axis=0)
            turned = lax.dot_general(
                pick, spread.astype(jnp.bfloat16), (((1,), (1,)), ((), ())), preferred_element_type=jnp.float32
            )
            buffer[lag] = turned * keep
        copy = pltpu.make_async_copy(
            buffer.at[pl.ds(start, stop - start)], out_ref.at[pl.ds(start, stop - start)], sem.at[start // 8]
        )
        copy.start()
        copies.append(copy)
    for copy in copies:
        copy.wait()


def finish(values, pair_mask):
    shape = (LAGS, LEFT, RIGHT)
    return pl.pallas_call(
        finish_kernel,
        out_shape=jax.ShapeDtypeStruct(shape, jnp.float32),
        in_specs=[VMEM, VMEM],
        out_specs=HBM,
        scratch_shapes=[pltpu.VMEM(shape, jnp.float32), pltpu.SemaphoreType.DMA((6,))],
        name="finish",
    )(values, pair_mask)


def body(traces, fir_taps, seg_flags, pair_mask):
    return finish(pairs(traces, fir_taps, seg_flags), pair_mask)


def solution(mesh):
    return jax.shard_map(
        body,
        mesh=mesh,
        in_specs=(P(("stn", "seg"), None), P(), P(("stn", "seg"), None), P("stn", "seg")),
        out_specs=P(None, "stn", "seg"),
        check_vma=False,
    )
```
